32 devices in a mesh: dev: 16 (over z, y, x), ta: 2 (over core).
Axes of the slice: x: 2, y: 2, z: 4, core: 2. Of those that a mesh axis runs over, the one named last changes fastest.
Arguments:
- token_ids: int32 [16384], P('dev'), may hold values from 0 to 50303
- bucket: int32 [16], P('dev'), may hold values from 256 to 1024, as said below
- seq_lengths: int32 [16, 4], P('dev'), may hold values from 0 to 1024, as said below
- loss_pos: int32 [4096], P('dev'), may hold values from 0 to 1023, as said below
- targets: int32 [4096], P('dev'), may hold values from 0 to 50303
- wte: bfloat16 [50304, 1024], P(('dev', 'ta')), may hold values from -0.359375 to 0.359375
- wpe: bfloat16 [1024, 1024], replicated, may hold values from -0.1796875 to 0.1796875
- w_qkv: bfloat16 [2, 3, 1024, 1024], P(None, None, 'dev', 'ta'), may hold values from -0.1875 to 0.1875
- w_out: bfloat16 [2, 1024, 1024], P(None, 'ta', 'dev'), may hold values from -1 to 1
- w_fc: bfloat16 [2, 1024, 4096], P(None, 'dev', 'ta'), may hold values from -0.1875 to 0.1875
- w_proj: bfloat16 [2, 4096, 1024], P(None, 'ta', 'dev'), may hold values from -0.09375 to 0.09375
- frozen_vec: float32 [2, 9, 1024], replicated
- fc_bias: float32 [2, 4096], P(None, 'ta'), may hold values from -0.6 to 0.6
- final_norm: float32 [2, 1024], replicated
- prefix_table: float32 [10, 512], replicated, may hold values from -0.6 to 0.6
- inner_weight: float32 [512, 512], P(None, 'dev'), may hold values from -0.25 to 0.25
- inner_bias: float32 [512], P('dev'), may hold values from -0.3 to 0.3
- outer_weight: float32 [512, 2, 2, 1024], P('dev', None, None, 'ta'), may hold values from -0.25 to 0.25
- outer_bias: float32 [2, 2, 1024], P(None, None, 'ta'), may hold values from -0.6 to 0.6
- moment_prefix: float32 [10, 512], replicated, may hold values from -4.172325e-07 to 4.172325e-07
- square_prefix: float32 [10, 512], replicated, may hold values from 4.2211477e-16 to 1.6884591e-15
- moment_inner: float32 [512, 512], P(None, 'dev'), may hold values from -4.172325e-07 to 4.172325e-07
- square_inner: float32 [512, 512], P(None, 'dev'), may hold values from 4.2211477e-16 to 1.6884591e-15
- moment_inner_bias: float32 [512], P('dev'), may hold values from -1.1920929e-06 to 1.1920929e-06
- square_inner_bias: float32 [512], P('dev'), may hold values from 3.799033e-15 to 1.5196132e-14
- moment_outer: float32 [512, 2, 2, 1024], P('dev', None, None, 'ta'), may hold values from -4.172325e-07 to 4.172325e-07
- square_outer: float32 [512, 2, 2, 1024], P('dev', None, None, 'ta'), may hold values from 4.2211477e-16 to 1.6884591e-15
- moment_outer_bias: float32 [2, 2, 1024], P(None, None, 'ta'), may hold values from -1.1920929e-06 to 1.1920929e-06
- square_outer_bias: float32 [2, 2, 1024], P(None, None, 'ta'), may hold values from 3.799033e-15 to 1.5196132e-14
Outputs:
- mean_loss: float32 [1], replicated
- grad_norm: float32 [1], replicated
- prefix_new: float32 [10, 512], replicated
- prefix_moment: float32 [10, 512], replicated
- prefix_square: float32 [10, 512], replicated
- inner_new: float32 [512, 512], P(None, 'dev')
- inner_moment: float32 [512, 512], P(None, 'dev')
- inner_square: float32 [512, 512], P(None, 'dev')
- inner_bias_new: float32 [512], P('dev')
- inner_bias_moment: float32 [512], P('dev')
- inner_bias_square: float32 [512], P('dev')
- outer_new: float32 [512, 2, 2, 1024], P('dev', None, None, 'ta')
- outer_moment: float32 [512, 2, 2, 1024], P('dev', None, None, 'ta')
- outer_square: float32 [512, 2, 2, 1024], P('dev', None, None, 'ta')
- outer_bias_new: float32 [2, 2, 1024], P(None, None, 'ta')
- outer_bias_moment: float32 [2, 2, 1024], P(None, None, 'ta')
- outer_bias_square: float32 [2, 2, 1024], P(None, None, 'ta')
- prefix_copy: bfloat16 [10, 512], replicated
- inner_copy: bfloat16 [512, 512], P(None, 'dev')
- inner_bias_copy: bfloat16 [512], P('dev')
- outer_copy: bfloat16 [512, 2, 2, 1024], P('dev', None, None, 'ta')
- outer_bias_copy: bfloat16 [2, 2, 1024], P(None, None, 'ta')
The draws below stay inside these ranges and needn't reach their ends.
Inputs may be any that keep to these rules, and one draw needn't show every extreme that they name: `bucket`: each entry is 256 or 1024; both occur. `seq_lengths`: for a group of bucket 1024, entry 0 is its one sequence's length and the others are 0; for a group of bucket 256, the 4 entries are its sequences' lengths, each 1 or more. Some group of each bucket has a sequence of full length. `loss_pos`: rows within a group, all different within a group.
All inputs are finite; a program needn't handle non-finite values.
Results may differ from the reference program's by a relative error of at most 0.01.
Values may be sent and summed in bfloat16 or wider, within the bound.
No kernel may reach another device: no remote copies, remote signals or barrier semaphores. Data moves between devices by JAX's collectives and lax.ppermute only.
A program may use at most 280 MiB of HBM per device.

```python
import math
from functools import partial
import jax
import jax.numpy as jnp
import numpy as np
from jax import lax

D = 1024
HEADS = 16
HEAD_DIM = 64
FF = 4096
VOCAB = 50304
LAYERS = 2
PREFIX = 10
EMBED = 512
REPARAM = 512
LONG = 1024
SHORT = 256
LOSS_DEV = 256
SLOTS = 4
TOKENS = 16384
COUNTED = 4096
PARAMS = 2369024
N_DEV = 16


def bucket_law(key):
    picks = jax.random.randint(jax.random.fold_in(key, 7), (N_DEV,), 0, 2)
    return picks.at[N_DEV - 1].set(1).at[N_DEV - 2].set(0)


def draw_bucket(key, part):
    return jnp.where(bucket_law(key) == 1, LONG, SHORT).astype(jnp.int32)


def draw_seq_lengths(key, part):
    longs = bucket_law(key)
    index = jnp.arange(N_DEV, dtype=jnp.int32)
    long_base = LONG // 3 + 2 * LONG // 3 * index // (N_DEV - 1)
    long_len = jnp.minimum(long_base + jax.random.randint(jax.random.fold_in(key, 8), (N_DEV,), 0, LONG // 8 + 1), LONG)
    long_len = long_len.at[N_DEV - 1].set(LONG)
    short_base = SHORT // 3 + 2 * SHORT // 3 * index // (N_DEV - 1)
    short_len = short_base[:, None] + jax.random.randint(jax.random.fold_in(key, 9), (N_DEV, SLOTS), 0, SHORT // 8 + 1)
    short_len = jnp.clip(short_len, 1, SHORT).at[N_DEV - 2, 0].set(SHORT)
    slots = jnp.arange(SLOTS)[None]
    long_rows = jnp.where(slots == 0, long_len[:, None], 0)
    return jnp.where(longs[:, None] == 1, long_rows, short_len).astype(jnp.int32)


def draw_loss_pos(key, part):
    scores = jax.random.randint(jax.random.fold_in(key, 23), (N_DEV, LONG), 0, 4096) * LONG + jnp.arange(LONG)[None]
    order = jnp.argsort(scores, axis=1)[:, :LOSS_DEV]
    first_rows = jnp.arange(LOSS_DEV).at[LOSS_DEV - 1].set(LONG - 1)
    order = order.at[0].set(first_rows)
    return order.reshape(-1).astype(jnp.int32)


def draw_frozen_vec(key, part):
    noise = jax.random.normal(jax.random.fold_in(key, 21), (LAYERS, 9, D), jnp.float32)
    rows = jnp.arange(9)[None, :, None]
    gains = (rows == 0) | (rows == 2)
    return jnp.where(gains, 1.0 + 0.1 * noise, 0.05 * noise)


def draw_final_norm(key, part):
    noise = jax.random.normal(jax.random.fold_in(key, 22), (2, D), jnp.float32)
    rows = jnp.arange(2)[:, None]
    return jnp.where(rows == 0, 1.0 + 0.1 * noise, 0.05 * noise)


def touch_ends(array, own_key, low, high):
    shape = array.shape
    index_at = [jax.random.randint(jax.random.fold_in(own_key, axis), (), 0, shape[axis]) for axis in range(len(shape))]
    array = array.at[tuple(index_at)].set(low)
    longest = shape.index(max(shape))
    index_at[longest] = (index_at[longest] + 1) % shape[longest]
    return array.at[tuple(index_at)].set(high)


def block_scale(key, dims, pieces, least, high):
    level, own = 1.0, jax.random.fold_in(key, 6)
    for position, blocks in pieces:
        steps = jnp.exp(jax.random.uniform(jax.random.fold_in(own, position), (blocks,), jnp.float32, least / len(pieces), high / len(pieces)))
        level = level * jnp.repeat(steps, dims[position] // blocks).reshape([-1 if axis == position else 1 for axis in range(len(dims))])
    return level


def rank_bounds(number_of, slope):
    loads = [(1 << 20) // math.isqrt(rank ** slope) + 1 for rank in range(1, number_of + 1)]
    deviation = 1 + sum(loads) // (1 << 30)
    return np.cumsum(np.array([max(1, weight // deviation) for weight in loads]))


def ranked(own_key, extent, count, lean):
    grid = rank_bounds(count, lean)
    pick = jax.random.randint(jax.random.fold_in(own_key, 1), extent, 0, int(grid[count - 1]))
    rank = jnp.searchsorted(jnp.asarray(grid, jnp.int32), pick, side="right")
    return jax.random.permutation(jax.random.fold_in(own_key, 2), count)[rank].astype(jnp.int32)


def gaussian(own_key, shape, deviation, bound, split=(), kind=jnp.bfloat16):
    drawn = jax.random.normal(own_key, shape, jnp.float32) * deviation
    if len(split) > 0:
        drawn = block_scale(own_key, shape, split, -0.22, 0.18) * drawn
    return jnp.clip(drawn, min=-bound, max=bound).astype(kind)


def setup_inputs(seed: int = 0) -> dict:
    seeds = jax.random.split(jax.random.key(seed), 30)
    return {
        "token_ids": touch_ends(ranked(seeds[0], (TOKENS,), VOCAB, 2), jax.random.fold_in(seeds[0], 3), 0, VOCAB - 1).astype(jnp.int32),
        "bucket": draw_bucket(jax.random.fold_in(seeds[29], 71), 0),
        "seq_lengths": draw_seq_lengths(jax.random.fold_in(seeds[29], 71), 0),
        "loss_pos": draw_loss_pos(jax.random.fold_in(seeds[29], 71), 0),
        "targets": touch_ends(ranked(seeds[4], (COUNTED,), VOCAB, 2), jax.random.fold_in(seeds[4], 3), 0, VOCAB - 1).astype(jnp.int32),
        "wte": gaussian(seeds[5], (VOCAB, D), 0.06, 0.359375, ((0, 32),)),
        "wpe": gaussian(seeds[6], (LONG, D), 0.03, 0.1796875),
        "w_qkv": gaussian(seeds[7], (LAYERS, 3, D, D), D ** -0.5, 0.1875, ((2, 16), (3, 2))),
        "w_out": gaussian(seeds[8], (LAYERS, D, D), (D // 32) ** -0.5, 1.0, ((1, 2), (2, 16))),
        "w_fc": gaussian(seeds[9], (LAYERS, D, FF), D ** -0.5, 0.1875, ((1, 16), (2, 2))),
        "w_proj": gaussian(seeds[10], (LAYERS, FF, D), FF ** -0.5, 0.09375, ((1, 2), (2, 16))),
        "frozen_vec": draw_frozen_vec(jax.random.fold_in(seeds[29], 71), 0),
        "fc_bias": gaussian(seeds[12], (LAYERS, FF), 0.1, 0.6, ((1, 2),), jnp.float32),
        "final_norm": draw_final_norm(jax.random.fold_in(seeds[29], 71), 0),
        "prefix_table": gaussian(seeds[14], (PREFIX, EMBED), 0.1, 0.6, (), jnp.float32),
        "inner_weight": gaussian(seeds[15], (EMBED, REPARAM), EMBED ** -0.5, 0.25, ((1, 16),), jnp.float32),
        "inner_bias": gaussian(seeds[16], (REPARAM,), 0.05, 0.3, ((0, 16),), jnp.float32),
        "outer_weight": gaussian(seeds[17], (REPARAM, LAYERS, 2, D), REPARAM ** -0.5, 0.25, ((0, 16), (3, 2)), jnp.float32),
        "outer_bias": gaussian(seeds[18], (LAYERS, 2, D), 0.1, 0.6, ((2, 2),), jnp.float32),
        "moment_prefix": gaussian(seeds[19], (PREFIX, EMBED), (0.000111 * PARAMS ** -0.5), 4.172325134277344e-07, (), jnp.float32),
        "square_prefix": jnp.clip(jnp.exp(jax.random.uniform(seeds[20], (PREFIX, EMBED), jnp.float32, math.log(4.221147664483423e-16), math.log(1.6884590657933692e-15))), 4.221147664483423e-16, 1.6884590657933692e-15),
        "moment_inner": gaussian(seeds[21], (EMBED, REPARAM), (0.000111 * PARAMS ** -0.5), 4.172325134277344e-07, ((1, 16),), jnp.float32),
        "square_inner": jnp.clip(jnp.exp(math.log(1.6884590657933692e-15) - 1.3862944 * jax.random.uniform(seeds[22], (EMBED, REPARAM), jnp.float32) ** block_scale(seeds[22], (EMBED, REPARAM), ((1, 16),), -0.2, 0.2)), 4.221147664483423e-16, 1.6884590657933692e-15),
        "moment_inner_bias": gaussian(seeds[23], (REPARAM,), (0.000333 * PARAMS ** -0.5), 1.1920928955078125e-06, ((0, 16),), jnp.float32),
        "square_inner_bias": jnp.clip(jnp.exp(math.log(1.5196131909777678e-14) - 1.3862944 * jax.random.uniform(seeds[24], (REPARAM,), jnp.float32) ** block_scale(seeds[24], (REPARAM,), ((0, 16),), -0.2, 0.2)), 3.7990329774444196e-15, 1.5196131909777678e-14),
        "moment_outer": gaussian(seeds[25], (REPARAM, LAYERS, 2, D), (0.000111 * PARAMS ** -0.5), 4.172325134277344e-07, ((0, 16), (3, 2)), jnp.float32),
        "square_outer": jnp.clip(jnp.exp(math.log(1.6884590657933692e-15) - 1.3862944 * jax.random.uniform(seeds[26], (REPARAM, LAYERS, 2, D), jnp.float32) ** block_scale(seeds[26], (REPARAM, LAYERS, 2, D), ((0, 16), (3, 2)), -0.2, 0.2)), 4.221147664483423e-16, 1.6884590657933692e-15),
        "moment_outer_bias": gaussian(seeds[27], (LAYERS, 2, D), (0.000333 * PARAMS ** -0.5), 1.1920928955078125e-06, ((2, 2),), jnp.float32),
        "square_outer_bias": jnp.clip(jnp.exp(math.log(1.5196131909777678e-14) - 1.3862944 * jax.random.uniform(seeds[28], (LAYERS, 2, D), jnp.float32) ** block_scale(seeds[28], (LAYERS, 2, D), ((2, 2),), -0.2, 0.2)), 3.7990329774444196e-15, 1.5196131909777678e-14),
    }


@jax.custom_vjp
def low(v):
    return lax.optimization_barrier(v.astype(jnp.bfloat16)).astype(jnp.float32)

@jax.custom_vjp
def low_back(v):
    return v

def low_keep(v):
    return (low(v), None)

def low_pass(kept, grad):
    return (grad,)

def back_keep(v):
    return (v, None)

def back_low(kept, grad):
    return (low(grad),)
low.defvjp(low_keep, low_pass)
low_back.defvjp(back_keep, back_low)
EPS_NORM = 1e-05
CLIP_NORM = 0.001
LEARN_RATE = 0.02
BETA_ONE = 0.9
BETA_TWO = 0.999
ADAM_EPS = 1e-08
DECAY_RATE = 0.01
adam_steps = 10.0
NEG_BIG = -1e+30
HIGHEST = lax.Precision.HIGHEST

def layer_norm(stream, gain, shift):
    center = stream - lax.optimization_barrier(jnp.mean(stream, -1, keepdims=True))
    spread = lax.optimization_barrier(jnp.mean(center * center, -1, keepdims=True))
    return center * lax.rsqrt(spread + EPS_NORM) * gain + shift

def group_layout(bucket_width, lengths):
    positions = jnp.arange(LONG, dtype=jnp.int32)
    segment = positions // bucket_width
    seq_pos = positions % bucket_width
    slots = jnp.arange(SLOTS, dtype=jnp.int32)
    seg_len = lax.optimization_barrier(jnp.sum(jnp.where(segment[:, None] == slots[None], lengths[None], 0), 1))
    return (positions, segment, seq_pos, seq_pos < seg_len)

def block_layer(stream, prefix_kv, visible, weights):
    w_qkv, w_out, w_fc, w_proj, vectors, fc_half = weights
    normed = low(layer_norm(stream, vectors[0], vectors[1]))
    qkv = low(low_back(jnp.einsum('rd,cde->rce', normed, w_qkv, precision=HIGHEST) + vectors[4:7][None]))
    queries = qkv[:, 0].reshape(LONG, HEADS, HEAD_DIM)
    keys = jnp.concatenate([prefix_kv[0], qkv[:, 1]], 0).reshape(PREFIX + LONG, HEADS, HEAD_DIM)
    values = jnp.concatenate([prefix_kv[1], qkv[:, 2]], 0).reshape(PREFIX + LONG, HEADS, HEAD_DIM)
    scores = low_back(jnp.einsum('qhd,khd->hqk', queries, keys, precision=HIGHEST) * HEAD_DIM ** (-0.5))
    scores = jnp.where(visible[None], scores, NEG_BIG)
    highest = lax.optimization_barrier(jnp.max(scores, -1, keepdims=True))
    exponent = jnp.exp(scores - highest)
    shares = low(low_back(exponent / lax.optimization_barrier(jnp.sum(exponent, -1, keepdims=True))))
    mixed_heads = low(low_back(jnp.einsum('hqk,khd->qhd', shares, values, precision=HIGHEST).reshape(LONG, D)))
    middle = stream + low_back(jnp.dot(mixed_heads, w_out, precision=HIGHEST) + vectors[7])
    normed_two = low(layer_norm(middle, vectors[2], vectors[3]))
    upward = low_back(jnp.dot(normed_two, w_fc, precision=HIGHEST) + fc_half)
    active = low(jax.nn.gelu(upward, approximate=True))
    return middle + low_back(jnp.dot(active, w_proj, precision=HIGHEST) + vectors[8])

def adamw_update(weight, moment, square, gradient, corr_one, corr_two):
    moment = BETA_ONE * moment + (1.0 - BETA_ONE) * gradient
    square = BETA_TWO * square + (1.0 - BETA_TWO) * gradient * gradient
    weight = weight - LEARN_RATE * (moment / corr_one / (jnp.sqrt(square / corr_two) + ADAM_EPS) + DECAY_RATE * weight)
    return (weight, moment, square)

def reference(token_ids, bucket, seq_lengths, loss_pos, targets, wte, wpe, w_qkv, w_out, w_fc, w_proj, frozen_vec, fc_bias, final_norm, prefix_table, inner_weight, inner_bias, outer_weight, outer_bias, moment_prefix, square_prefix, moment_inner, square_inner, moment_inner_bias, square_inner_bias, moment_outer, square_outer, moment_outer_bias, square_outer_bias):
    float_type = prefix_table.dtype
    table = wte.astype(float_type)
    places = wpe.astype(float_type)
    qkv_all = w_qkv.astype(float_type)
    out_all = w_out.astype(float_type)
    fc_all = w_fc.astype(float_type)
    proj_all = w_proj.astype(float_type)
    group_ids = token_ids.reshape(N_DEV, LONG)
    group_picks = loss_pos.reshape(N_DEV, LOSS_DEV)
    group_goals = targets.reshape(N_DEV, LOSS_DEV)
    present_all = jax.vmap(lambda width, lengths: group_layout(width, lengths)[3])(bucket, seq_lengths)
    counted = jnp.take_along_axis(present_all, group_picks, 1).astype(float_type)

    def group_loss(prefix_kv, element):
        ids, bucket_width, lengths, picks, goals, weight_rows = element
        positions, segment, seq_pos, present = group_layout(bucket_width, lengths)
        tokens_seen = (segment[:, None] == segment[None]) & (positions[None] <= positions[:, None]) & present[None]
        visible = jnp.concatenate([jnp.ones((LONG, PREFIX), bool), tokens_seen], 1)
        stream = table[ids] + places[seq_pos]
        for layer_id in range(LAYERS):
            weights = (qkv_all[layer_id], out_all[layer_id], fc_all[layer_id], proj_all[layer_id], frozen_vec[layer_id], fc_bias[layer_id])
            stream = block_layer(stream, prefix_kv[layer_id], visible, weights)
        head_in = low(layer_norm(stream[picks], final_norm[0], final_norm[1]))
        logits = jnp.dot(head_in, table.T, precision=HIGHEST)
        highest = lax.optimization_barrier(jnp.max(logits, -1, keepdims=True))
        log_total = highest[:, 0] + jnp.log(lax.optimization_barrier(jnp.sum(jnp.exp(logits - highest), -1)))
        chosen = jnp.take_along_axis(logits, goals[:, None], 1)[:, 0]
        return jnp.sum((log_total - chosen) * weight_rows)

    def total_loss(params):
        table_param, inner, ibias, outer, obias = params
        hidden = jnp.tanh(jnp.dot(table_param, inner, precision=HIGHEST) + ibias)
        prefix_kv = low(jnp.einsum('pr,rlcd->lcpd', hidden, outer, precision=HIGHEST) + obias[:, :, None, :])
        per_group = lax.map(jax.checkpoint(partial(group_loss, prefix_kv)), (group_ids, bucket, seq_lengths, group_picks, group_goals, counted))
        return jnp.sum(per_group) / COUNTED
    params = (prefix_table, inner_weight, inner_bias, outer_weight, outer_bias)
    loss_value, pullback = jax.vjp(total_loss, params)
    grads = pullback(jnp.ones((), float_type))[0]
    square_total = sum((jnp.sum(gradient * gradient) for gradient in grads))
    grad_total = jnp.sqrt(square_total)
    factor = jnp.minimum(1.0, CLIP_NORM / (grad_total + 1e-06))
    corr_one = 1.0 - BETA_ONE ** adam_steps
    corr_two = 1.0 - BETA_TWO ** adam_steps
    states = ((moment_prefix, square_prefix), (moment_inner, square_inner), (moment_inner_bias, square_inner_bias), (moment_outer, square_outer), (moment_outer_bias, square_outer_bias))
    results = []
    for weight, gradient, state in zip(params, grads, states):
        results.extend(adamw_update(weight, state[0], state[1], factor * gradient, corr_one, corr_two))
    return (loss_value.reshape(1), grad_total.reshape(1), results[0], results[1], results[2], results[3], results[4], results[5], results[6], results[7], results[8], results[9], results[10], results[11], results[12], results[13], results[14], results[0].astype(jnp.bfloat16), results[3].astype(jnp.bfloat16), results[6].astype(jnp.bfloat16), results[9].astype(jnp.bfloat16), results[12].astype(jnp.bfloat16))
```

```python
import functools

import jax
import jax.numpy as jnp
from jax import lax
from jax.experimental import pallas as pl
from jax.experimental.pallas import tpu as pltpu
from jax.sharding import PartitionSpec as P

HEAD_DIM = 64


EPS_NORM = 1e-05
CLIP_NORM = 0.001
LEARN_RATE = 0.02
BETA_ONE = 0.9
BETA_TWO = 0.999
ADAM_EPS = 1e-08
DECAY_RATE = 0.01
adam_steps = 10.0
NEG_BIG = -1e30
HIGHEST = lax.Precision.HIGHEST
F32 = jnp.float32
B16 = jnp.bfloat16
GELU_SCALE = 0.7978845608028654
GELU_CUBE = 0.044715
SLOT_ROWS = 48
BLOCK = 256
LANES = 128
SWAP = [(0, 1), (1, 0)]


def shape(dims, dtype):
    return jax.ShapeDtypeStruct(dims, dtype)


def params(**more):
    return pltpu.CompilerParams(dimension_semantics=("arbitrary",), **more)


def flip(array, bit):
    size = lax.axis_size("dev")
    return lax.ppermute(array, "dev", [(i, i ^ bit) for i in range(size)])


def partner(array):
    return lax.ppermute(array, "ta", SWAP)


def bit_orders(size):
    bits = [1 << k for k in range(size.bit_length() - 1)]
    if size == 16:
        x, y, near, far = bits
        return ((far, y, near, x), (near, far, x, y), (far, x, y, near))
    return tuple(tuple(bits[k:] + bits[:k]) for k in range(3))


def offsets_of(order):
    found = [0]
    for bit in order[:-1]:
        found = found + [o ^ bit for o in found]
    return found


def doubling_rounds(schedule, state, orders):
    before = []
    for pairs in schedule:
        keys = [(chunk, part, stage) for chunk, stage in pairs for part in range(len(orders))]
        sends = []
        for chunk, part, stage in keys:
            held = state[chunk, part]
            sends.append(held[0] if len(held) == 1 else jnp.concatenate(held, 0))
        tied = lax.optimization_barrier(tuple(sends) + tuple(before))
        before = []
        for (chunk, part, stage), send in zip(keys, tied):
            got = flip(send, orders[part][stage])
            state[chunk, part] = [send, got]
            before.append(got)
    return state


def sum_over_dev(array):
    bit = 1
    while bit < lax.axis_size("dev"):
        array = array + flip(array, bit)
        bit = bit * 2
    return array


def norm_rows(x):
    center = x - jnp.mean(x, -1, keepdims=True)
    scale = lax.rsqrt(jnp.mean(center * center, -1, keepdims=True) + EPS_NORM)
    return center * scale, scale


def norm_rows_back(gradient, x, gain):
    xhat, scale = norm_rows(x)
    e2 = gradient * gain
    mean_one = jnp.mean(e2, -1, keepdims=True)
    mean_two = jnp.mean(e2 * xhat, -1, keepdims=True)
    return (e2 - mean_one - xhat * mean_two) * scale


def dot_nn(a, b):
    return lax.dot_general(a, b, (((1,), (0,)), ((), ())), preferred_element_type=F32)


def dot_nt(a, b):
    return lax.dot_general(a, b, (((1,), (1,)), ((), ())), preferred_element_type=F32)


def dot_tn(a, b):
    return lax.dot_general(a, b, (((0,), (0,)), ((), ())), preferred_element_type=F32)


class Gathered:
    def __init__(self, pair, order, columns=None):
        self.pair = pair
        self.order = order
        blocks, rows, width = pair[0].shape
        self.blocks, self.rows = blocks, rows
        self.columns = (0, width) if columns is None else columns
        self.scratch = [
            pltpu.VMEM((2 * blocks * rows, self.columns[1] - self.columns[0]), B16),
            pltpu.SemaphoreType.DMA((2 * blocks,)),
        ]

    def copies(self, me, held, taken, full, sems):
        first, last = self.columns
        for index, offset in enumerate(offsets_of(self.order)):
            for side, (ref, extra) in enumerate(((held, 0), (taken, self.order[-1]))):
                start = pl.multiple_of((me ^ (offset ^ extra)) * self.rows, self.rows)
                source = ref.at[index]
                if (first, last) != (0, ref.shape[2]):
                    source = source.at[:, pl.ds(first, last - first)]
                yield pltpu.make_async_copy(
                    source, full.at[pl.ds(start, self.rows)], sems.at[2 * index + side]
                )

    def start(self, *refs):
        for copy in self.copies(*refs):
            copy.start()

    def wait(self, *refs):
        for copy in self.copies(*refs):
            copy.wait()


ANY = pl.BlockSpec(memory_space=pl.ANY)


def rows_spec(width, block=BLOCK):
    return pl.BlockSpec((block, width), lambda i, *refs: (i, 0))


def whole_spec(dims):
    return pl.BlockSpec(dims, lambda i, *refs: (0,) * len(dims))


def key_bias(layout_ref, query_pos, key_count):
    shift = layout_ref[0]
    dims = (query_pos.shape[0], key_count)
    key_pos = lax.broadcasted_iota(jnp.int32, (1, key_count), 1)
    key_seg = lax.shift_right_logical(key_pos, jnp.full((1, key_count), shift, jnp.int32))
    query_seg = lax.shift_right_logical(query_pos, jnp.full(query_pos.shape, shift, jnp.int32))
    length = jnp.zeros((1, key_count), jnp.int32)
    for slot in range(layout_ref.shape[0] - 2):
        length = jnp.where(key_seg == slot, layout_ref[2 + slot], length)
    place = key_pos - key_seg * layout_ref[1]
    key_seg = jnp.where(place < length, key_seg, -1)
    seen = (jnp.broadcast_to(query_seg, dims) == jnp.broadcast_to(key_seg, dims)) & (
        jnp.broadcast_to(key_pos, dims) <= jnp.broadcast_to(query_pos, dims)
    )
    return jnp.where(seen, 0.0, NEG_BIG)


def prefix_bias(rows, prefix_rows, prefix_len):
    lane = lax.broadcasted_iota(jnp.int32, (rows, prefix_rows), 1)
    return jnp.where(lane < prefix_len, 0.0, NEG_BIG)


def attend(query, key, value, key_prefix, value_prefix, bias, bias_prefix):
    scores = dot_nt(query, key) + bias
    scores_prefix = dot_nt(query, key_prefix) + bias_prefix
    highest = jnp.maximum(
        jnp.max(scores, -1, keepdims=True), jnp.max(scores_prefix, -1, keepdims=True)
    )
    shares = jnp.exp(scores - highest)
    shares_prefix = jnp.exp(scores_prefix - highest)
    total = jnp.sum(shares, -1, keepdims=True) + jnp.sum(shares_prefix, -1, keepdims=True)
    mixed = dot_nn(shares.astype(B16), value) + dot_nn(shares_prefix.astype(B16), value_prefix)
    return mixed / total, highest + jnp.log(total)


def attend_pairs(q_ref, k_ref, v_ref, prefix_ref, mixed_ref, lse_ref, rows, key_count, bias, plen):
    prefix_rows = prefix_ref.shape[1]
    bias_prefix = prefix_bias(BLOCK, prefix_rows, plen)
    lse_ref[rows, :] = jnp.zeros((BLOCK, LANES), F32)
    lane = lax.broadcasted_iota(jnp.int32, (BLOCK, LANES), 1)

    def pair(index, carry):
        columns = pl.ds(pl.multiple_of(index * LANES, LANES), LANES)
        query = q_ref[rows, columns]
        key = k_ref[pl.ds(0, key_count), columns]
        value = v_ref[pl.ds(0, key_count), columns]
        key_prefix = prefix_ref[0, :, columns]
        value_prefix = prefix_ref[1, :, columns]
        parts = []
        for side in range(2):
            cut = slice(side * HEAD_DIM, (side + 1) * HEAD_DIM)
            mixed, lse = attend(
                query[:, cut],
                key[:, cut],
                value[:, cut],
                key_prefix[:, cut],
                value_prefix[:, cut],
                bias,
                bias_prefix,
            )
            parts.append(mixed)
            lse_ref[rows, :] = jnp.where(lane == 2 * index + side, lse, lse_ref[rows, :])
        mixed_ref[rows, columns] = jnp.concatenate(parts, 1).astype(B16)
        return carry

    lax.fori_loop(0, q_ref.shape[1] // LANES, pair, 0)


def first_attention(stream, vectors, bias_qkv, prefix, layout, me, weight, plen):
    row_count, width = stream.shape
    half = prefix.shape[2]
    scale = HEAD_DIM ** (-0.5)

    def body(me_ref, layout_ref, stream_ref, vec_ref, bias_ref, prefix_ref, held, taken,
             part_ref, q_out, mixed_out, lse_out, full, sems, q_s, k_s, v_s):
        step = pl.program_id(0)
        refs = (me_ref[0], held, taken, full, sems)

        @pl.when(step == 0)
        def _():
            weight.start(*refs)
            weight.wait(*refs)

        xhat, unused = norm_rows(stream_ref[...])
        normed = (xhat * vec_ref[0:1, :] + vec_ref[1:2, :]).astype(B16)
        qkv = dot_nn(normed, full[:, : 3 * half]) + bias_ref[...]
        rows = pl.ds(pl.multiple_of(step * BLOCK, BLOCK), BLOCK)
        q_s[...] = (qkv[:, :half].astype(B16) * scale).astype(B16)
        k_s[rows, :] = qkv[:, half : 2 * half].astype(B16)
        v_s[rows, :] = qkv[:, 2 * half :].astype(B16)
        q_out[...] = q_s[...]
        local_pos = lax.broadcasted_iota(jnp.int32, (BLOCK, 1), 0)
        for case in range(row_count // BLOCK):

            @pl.when(step == case)
            def _(case=case):
                key_count = (case + 1) * BLOCK
                bias = key_bias(layout_ref, local_pos + case * BLOCK, key_count)
                attend_pairs(
                    q_s, k_s, v_s, prefix_ref, mixed_out, lse_out,
                    pl.ds(0, BLOCK), key_count, bias, plen,
                )

        part_ref[...] = dot_nt(mixed_out[...], full[:, 3 * half :]).astype(B16)

    return pl.pallas_call(
        body,
        grid_spec=pltpu.PrefetchScalarGridSpec(
            num_scalar_prefetch=2,
            grid=(row_count // BLOCK,),
            in_specs=[
                rows_spec(width),
                whole_spec(vectors.shape),
                whole_spec(bias_qkv.shape),
                whole_spec(prefix.shape),
                ANY,
                ANY,
            ],
            out_specs=[rows_spec(width), rows_spec(half), rows_spec(half), rows_spec(LANES)],
            scratch_shapes=weight.scratch
            + [pltpu.VMEM((BLOCK, half), B16)]
            + [pltpu.VMEM((row_count, half), B16)] * 2,
        ),
        out_shape=[
            shape((row_count, width), B16),
            shape((row_count, half), B16),
            shape((row_count, half), B16),
            shape((row_count, LANES), F32),
        ],
        compiler_params=params(),
        name="first_attention",
    )(me, layout, stream, vectors, bias_qkv, prefix, *weight.pair)


def mlp(base, own, other, vectors, bias_up, me, w_up, w_down):
    row_count, width = base.shape
    hidden = bias_up.shape[1]

    def body(me_ref, base_ref, own_ref, other_ref, vec_ref, bias_ref, up_held, up_taken,
             down_held, down_taken, part_ref, middle_ref, slope_ref, up, up_sems, down, down_sems):
        step = pl.program_id(0)
        up_refs = (me_ref[0], up_held, up_taken, up, up_sems)
        down_refs = (me_ref[0], down_held, down_taken, down, down_sems)

        @pl.when(step == 0)
        def _():
            w_up.start(*up_refs)
            w_down.start(*down_refs)

        middle = base_ref[...] + (
            (own_ref[...].astype(F32) + other_ref[...].astype(F32)) + vec_ref[0:1, :]
        )
        middle_ref[...] = middle
        xhat, unused = norm_rows(middle)
        normed = (xhat * vec_ref[1:2, :] + vec_ref[2:3, :]).astype(B16)

        @pl.when(step == 0)
        def _():
            w_up.wait(*up_refs)

        u = dot_nn(normed, up[...]) + bias_ref[...]
        square = u * u
        t = jnp.tanh(GELU_SCALE * u * (1.0 + GELU_CUBE * square))
        half_one = 0.5 + 0.5 * t
        active = (u * half_one).astype(B16)
        slope = half_one + (0.5 * GELU_SCALE) * u * (1.0 - t * t) * (1.0 + 3 * GELU_CUBE * square)
        slope_ref[...] = slope.astype(B16)

        @pl.when(step == 0)
        def _():
            w_down.wait(*down_refs)

        part_ref[...] = dot_nt(active, down[...]).astype(B16)

    return pl.pallas_call(
        body,
        grid_spec=pltpu.PrefetchScalarGridSpec(
            num_scalar_prefetch=1,
            grid=(row_count // BLOCK,),
            in_specs=[
                rows_spec(width),
                rows_spec(width),
                rows_spec(width),
                whole_spec(vectors.shape),
                whole_spec(bias_up.shape),
                ANY,
                ANY,
                ANY,
                ANY,
            ],
            out_specs=[rows_spec(width), rows_spec(width), rows_spec(hidden)],
            scratch_shapes=w_up.scratch + w_down.scratch,
        ),
        out_shape=[
            shape((row_count, width), B16),
            shape((row_count, width), F32),
            shape((row_count, hidden), B16),
        ],
        compiler_params=params(),
        name="mlp",
    )(me, base, own, other, vectors, bias_up, *w_up.pair, *w_down.pair)


def last_attention(base, own, other, vectors, bias_qkv, prefix, layout, picks, picks_column, me,
                   weight, plen):
    row_count, width = base.shape
    half = prefix.shape[2]
    scored = picks.shape[0]
    steps = row_count // BLOCK
    scale = HEAD_DIM ** (-0.5)

    def body(me_ref, layout_ref, picks_ref, base_ref, own_ref, other_ref, vec_ref, bias_ref,
             prefix_ref, column_ref, held, taken, stream_out, part_ref, k_out, v_out, q_out,
             mixed_out, lse_out, chosen_out, full, sems, stream_s, k_s, v_s):
        step = pl.program_id(0)
        refs = (me_ref[0], held, taken, full, sems)

        @pl.when(step == 0)
        def _():
            weight.start(*refs)
            weight.wait(*refs)

        stream = base_ref[...] + (
            (own_ref[...].astype(F32) + other_ref[...].astype(F32)) + vec_ref[0:1, :]
        )
        stream_out[...] = stream
        rows = pl.ds(pl.multiple_of(step * BLOCK, BLOCK), BLOCK)
        stream_s[rows, :] = stream
        xhat, unused = norm_rows(stream)
        normed = (xhat * vec_ref[1:2, :] + vec_ref[2:3, :]).astype(B16)
        keys_values = (
            dot_nn(normed, full[:, half : 3 * half]) + bias_ref[:, half : 3 * half]
        ).astype(B16)
        k_out[...] = keys_values[:, :half]
        v_out[...] = keys_values[:, half:]
        k_s[rows, :] = keys_values[:, :half]
        v_s[rows, :] = keys_values[:, half:]

        @pl.when(step == steps - 1)
        def _():
            def pick(index, carry):
                chosen_out[pl.ds(index, 1), :] = stream_s[pl.ds(picks_ref[index], 1), :]
                return carry

            lax.fori_loop(0, scored, pick, 0)
            for first in range(0, scored, BLOCK):
                block = pl.ds(first, BLOCK)
                chosen_hat, unused = norm_rows(chosen_out[block, :])
                chosen = (chosen_hat * vec_ref[1:2, :] + vec_ref[2:3, :]).astype(B16)
                query = (dot_nn(chosen, full[:, :half]) + bias_ref[:, :half]).astype(B16)
                q_out[block, :] = (query * scale).astype(B16)
                bias = key_bias(layout_ref, column_ref[block, :], row_count)
                attend_pairs(
                    q_out, k_s, v_s, prefix_ref, mixed_out, lse_out, block, row_count, bias, plen
                )
                part_ref[block, :] = dot_nt(mixed_out[block, :], full[:, 3 * half :]).astype(B16)

    return pl.pallas_call(
        body,
        grid_spec=pltpu.PrefetchScalarGridSpec(
            num_scalar_prefetch=3,
            grid=(steps,),
            in_specs=[
                rows_spec(width),
                rows_spec(width),
                rows_spec(width),
                whole_spec(vectors.shape),
                whole_spec(bias_qkv.shape),
                whole_spec(prefix.shape),
                whole_spec(picks_column.shape),
                ANY,
                ANY,
            ],
            out_specs=[
                rows_spec(width),
                whole_spec((scored, width)),
                rows_spec(half),
                rows_spec(half),
                whole_spec((scored, half)),
                whole_spec((scored, half)),
                whole_spec((scored, LANES)),
                whole_spec((scored, width)),
            ],
            scratch_shapes=weight.scratch
            + [pltpu.VMEM((row_count, width), F32)]
            + [pltpu.VMEM((row_count, half), B16)] * 2,
        ),
        out_shape=[
            shape((row_count, width), F32),
            shape((scored, width), B16),
            shape((row_count, half), B16),
            shape((row_count, half), B16),
            shape((scored, half), B16),
            shape((scored, half), B16),
            shape((scored, LANES), F32),
            shape((scored, width), F32),
        ],
        compiler_params=params(),
        name="last_attention",
    )(me, layout, picks, base, own, other, vectors, bias_qkv, prefix, picks_column, *weight.pair)


def split_lse(lse, rows):
    high = lse.astype(B16).astype(F32)
    middle = (lse - high).astype(B16).astype(F32)
    low = (lse - high) - middle
    lane = lax.broadcasted_iota(jnp.int32, (rows, LANES), 1)
    packed = jnp.where(lane == 0, high, jnp.where(lane == 1, middle, jnp.where(lane == 2, low, 0.0)))
    return packed.astype(B16)


def vocabulary(rows, table, entries):
    row_count, width = rows.shape
    padded = table.shape[0]
    tail = padded - LANES

    def body(rows_ref, table_ref, out_ref):
        logits = dot_nt(rows_ref[...], table_ref[...])
        if entries < padded:
            lane = lax.broadcasted_iota(jnp.int32, (BLOCK, LANES), 1) + tail
            masked = jnp.where(lane < entries, logits[:, tail:], NEG_BIG)
            logits = jnp.concatenate([logits[:, :tail], masked], 1)
        highest = jnp.max(logits, -1, keepdims=True)
        shares = jnp.exp(logits - highest)
        total = jnp.sum(shares, -1, keepdims=True)
        mean = dot_nn(shares.astype(B16), table_ref[...]) / total
        out_ref[:, :width] = mean.astype(B16)
        out_ref[:, width:] = split_lse(highest + jnp.log(total), BLOCK)

    return pl.pallas_call(
        body,
        grid=(row_count // BLOCK,),
        in_specs=[rows_spec(width), whole_spec(table.shape)],
        out_specs=rows_spec(width + LANES),
        out_shape=shape((row_count, width + LANES), B16),
        compiler_params=params(),
        name="vocabulary",
    )(rows, table)


def joined_lse(ref, width):
    last = ref[:, width:].astype(F32)
    return jnp.sum(last[:, 0:4], -1, keepdims=True)


def merge(first, second):
    row_count, wide = first.shape
    width = wide - LANES
    block = next(b for b in (256, 128, 64, 48, 32, 16) if row_count % b == 0)

    def body(first_ref, second_ref, out_ref):
        one, two = joined_lse(first_ref, width), joined_lse(second_ref, width)
        highest = jnp.maximum(one, two)
        scale_one, scale_two = jnp.exp(one - highest), jnp.exp(two - highest)
        total = scale_one + scale_two
        mean = first_ref[:, :width].astype(F32) * (scale_one / total)
        mean = mean + second_ref[:, :width].astype(F32) * (scale_two / total)
        out_ref[:, :width] = mean.astype(B16)
        out_ref[:, width:] = split_lse(highest + jnp.log(total), block)

    return pl.pallas_call(
        body,
        grid=(row_count // block,),
        in_specs=[rows_spec(wide, block)] * 2,
        out_specs=rows_spec(wide, block),
        out_shape=shape((row_count, wide), B16),
        compiler_params=params(),
        name="merge",
    )(first, second)


def head_back(means, head_rows, head_in, target_rows, counted, final_norm, count_total):
    scored, width = head_rows.shape

    def body(mean_ref, rows_ref, in_ref, target_ref, counted_ref, norm_ref, grad_ref, loss_ref):
        lse = joined_lse(mean_ref, width)
        target = target_ref[...].astype(F32)
        logit = jnp.sum(in_ref[...].astype(F32) * target, -1, keepdims=True)
        seen = counted_ref[...]
        loss_ref[...] = jnp.broadcast_to((lse - logit) * seen, (BLOCK, LANES))
        d_head = (mean_ref[:, :width].astype(F32) - target) * (seen / count_total)
        grad_ref[...] = norm_rows_back(d_head, rows_ref[...], norm_ref[0:1, :])

    return pl.pallas_call(
        body,
        grid=(scored // BLOCK,),
        in_specs=[
            rows_spec(width + LANES),
            rows_spec(width),
            rows_spec(width),
            rows_spec(width),
            rows_spec(1),
            whole_spec(final_norm.shape),
        ],
        out_specs=[rows_spec(width), rows_spec(LANES)],
        out_shape=[shape((scored, width), F32), shape((scored, LANES), F32)],
        compiler_params=params(),
        name="head_back",
    )(means, head_rows, head_in, target_rows, counted, final_norm)


def mlp_back(gradient, slope, me, w_up, w_down, residual=None):
    row_count, width = gradient.shape
    hidden = slope.shape[1]
    extra = [] if residual is None else list(residual)

    def body(me_ref, *refs):
        grad_ref, slope_ref = refs[0], refs[1]
        extra_refs = refs[2 : 2 + len(extra)]
        up_held, up_taken, down_held, down_taken, part_ref, *rest = refs[2 + len(extra) :]
        up, up_sems, down, down_sems = rest[-4:]
        step = pl.program_id(0)
        up_refs = (me_ref[0], up_held, up_taken, up, up_sems)
        down_refs = (me_ref[0], down_held, down_taken, down, down_sems)

        @pl.when(step == 0)
        def _():
            w_down.start(*down_refs)
            w_up.start(*up_refs)

        grad = grad_ref[...]
        if extra:
            stream_ref, gain_ref, own_ref, other_ref = extra_refs
            incoming = own_ref[...].astype(F32) + other_ref[...].astype(F32)
            grad = grad + norm_rows_back(incoming, stream_ref[...], gain_ref[...])
            rest[0][...] = grad

        @pl.when(step == 0)
        def _():
            w_down.wait(*down_refs)

        d_active = dot_nn(grad.astype(B16), down[...])
        d_upward = (d_active * slope_ref[...].astype(F32)).astype(B16)

        @pl.when(step == 0)
        def _():
            w_up.wait(*up_refs)

        part_ref[...] = dot_nt(d_upward, up[...]).astype(B16)

    extra_specs = (
        [rows_spec(width), whole_spec(extra[1].shape), rows_spec(width), rows_spec(width)]
        if extra
        else []
    )
    return pl.pallas_call(
        body,
        grid_spec=pltpu.PrefetchScalarGridSpec(
            num_scalar_prefetch=1,
            grid=(row_count // BLOCK,),
            in_specs=[rows_spec(width), rows_spec(hidden)] + extra_specs + [ANY] * 4,
            out_specs=[rows_spec(width)] * (2 if extra else 1),
            scratch_shapes=w_up.scratch + w_down.scratch,
        ),
        out_shape=[shape((row_count, width), B16)]
        + ([shape((row_count, width), F32)] if extra else []),
        compiler_params=params(),
        name="mlp_back",
    )(me, gradient, slope, *extra, *w_up.pair, *w_down.pair)


def last_attention_back(gradient, own, other, middle, gain, q, k, v, mixed, lse, prefix, layout,
                        picks, picks_column, me, weight, plen):
    scored, width = gradient.shape
    row_count, half = k.shape
    prefix_rows = prefix.shape[1]
    scale = HEAD_DIM ** (-0.5)

    def body(me_ref, layout_ref, picks_ref, grad_ref, own_ref, other_ref, middle_ref, gain_ref,
             q_ref, k_ref, v_ref, mixed_ref, lse_ref, prefix_ref, column_ref, held, taken,
             part_ref, spread_ref, dprefix_ref, full, sems, dmix_s, dq_s, dk_s, dv_s, sum_s, rows_s):
        refs = (me_ref[0], held, taken, full, sems)
        weight.start(*refs)
        incoming = own_ref[...].astype(F32) + other_ref[...].astype(F32)
        grad_mid = grad_ref[...] + norm_rows_back(incoming, middle_ref[...], gain_ref[...])
        rows_s[...] = grad_mid
        spread_ref[...] = jnp.zeros((row_count, width), F32)

        def put(index, carry):
            spread_ref[pl.ds(picks_ref[index], 1), :] = rows_s[pl.ds(index, 1), :]
            return carry

        lax.fori_loop(0, scored, put, 0)
        weight.wait(*refs)
        dmix_s[...] = dot_nn(grad_mid.astype(B16), full[:, 3 * half :]).astype(B16)
        bias = key_bias(layout_ref, column_ref[...], row_count)
        bias_prefix = prefix_bias(scored, prefix_rows, plen)
        lane = lax.broadcasted_iota(jnp.int32, (scored, LANES), 1)

        def pair(index, carry):
            columns = pl.ds(pl.multiple_of(index * LANES, LANES), LANES)
            query, key, value = q_ref[:, columns], k_ref[:, columns], v_ref[:, columns]
            d_mixed = dmix_s[:, columns]
            key_p, value_p = prefix_ref[0, :, columns], prefix_ref[1, :, columns]
            found = [[], [], [], [], []]
            for side in range(2):
                cut = slice(side * HEAD_DIM, (side + 1) * HEAD_DIM)
                log_total = jnp.sum(
                    jnp.where(lane == 2 * index + side, lse_ref[...], 0.0), -1, keepdims=True
                )
                qh, dh = query[:, cut], d_mixed[:, cut]
                shares = jnp.exp(dot_nt(qh, key[:, cut]) + bias - log_total)
                shares_p = jnp.exp(dot_nt(qh, key_p[:, cut]) + bias_prefix - log_total)
                d_shares = dot_nt(dh, value[:, cut]).astype(B16).astype(F32)
                d_shares_p = dot_nt(dh, value_p[:, cut]).astype(B16).astype(F32)
                inner = jnp.sum(shares * d_shares, -1, keepdims=True) + jnp.sum(
                    shares_p * d_shares_p, -1, keepdims=True
                )
                d_scores = (shares * (d_shares - inner)).astype(B16)
                d_scores_p = (shares_p * (d_shares_p - inner)).astype(B16)
                found[0].append(
                    (dot_nn(d_scores, key[:, cut]) + dot_nn(d_scores_p, key_p[:, cut])) * scale
                )
                found[1].append(dot_tn(d_scores, qh))
                found[2].append(dot_tn(shares.astype(B16), dh))
                found[3].append(dot_tn(d_scores_p, qh))
                found[4].append(dot_tn(shares_p.astype(B16), dh))
            joined = [jnp.concatenate(f, 1) for f in found]
            dq_s[:, columns] = joined[0].astype(B16)
            dk_s[:, columns] = joined[1].astype(B16)
            dv_s[:, columns] = joined[2].astype(B16)
            dprefix_ref[0, :, columns] = joined[3]
            dprefix_ref[1, :, columns] = joined[4]
            return carry

        lax.fori_loop(0, half // LANES, pair, 0)
        sum_s[...] = dot_nt(dk_s[...], full[:, half : 2 * half]) + dot_nt(
            dv_s[...], full[:, 2 * half : 3 * half]
        )
        rows_s[...] = dot_nt(dq_s[...], full[:, :half])

        def add(index, carry):
            place = pl.ds(picks_ref[index], 1)
            sum_s[place, :] = sum_s[place, :] + rows_s[pl.ds(index, 1), :]
            return carry

        lax.fori_loop(0, scored, add, 0)
        part_ref[...] = sum_s[...].astype(B16)

    inputs = [gradient, own, other, middle, gain, q, k, v, mixed, lse, prefix, picks_column]
    return pl.pallas_call(
        body,
        grid_spec=pltpu.PrefetchScalarGridSpec(
            num_scalar_prefetch=3,
            grid=(1,),
            in_specs=[whole_spec(a.shape) for a in inputs] + [ANY, ANY],
            out_specs=[
                whole_spec((row_count, width)),
                whole_spec((row_count, width)),
                whole_spec(prefix.shape),
            ],
            scratch_shapes=weight.scratch
            + [
                pltpu.VMEM((scored, half), B16),
                pltpu.VMEM((scored, half), B16),
                pltpu.VMEM((row_count, half), B16),
                pltpu.VMEM((row_count, half), B16),
                pltpu.VMEM((row_count, width), F32),
                pltpu.VMEM((scored, width), F32),
            ],
        ),
        out_shape=[
            shape((row_count, width), B16),
            shape((row_count, width), F32),
            shape(prefix.shape, F32),
        ],
        compiler_params=params(),
        name="last_attention_back",
    )(me, layout, picks, *inputs, *weight.pair)


def first_prefix_back(gradient, own, other, middle, gain, q, mixed, lse, prefix, me, weight, plen):
    row_count, width = gradient.shape
    half = q.shape[1]
    prefix_rows = prefix.shape[1]

    def body(me_ref, grad_ref, own_ref, other_ref, middle_ref, gain_ref, q_ref, mixed_ref,
             lse_ref, prefix_ref, held, taken, dprefix_ref, full, sems):
        step = pl.program_id(0)
        refs = (me_ref[0], held, taken, full, sems)

        @pl.when(step == 0)
        def _():
            weight.start(*refs)
            dprefix_ref[...] = jnp.zeros(prefix.shape, F32)

        incoming = own_ref[...].astype(F32) + other_ref[...].astype(F32)
        grad_mid = grad_ref[...] + norm_rows_back(incoming, middle_ref[...], gain_ref[...])

        @pl.when(step == 0)
        def _():
            weight.wait(*refs)

        d_mixed = dot_nn(grad_mid.astype(B16), full[...]).astype(B16)
        product = d_mixed.astype(F32) * mixed_ref[...].astype(F32)
        bias_prefix = prefix_bias(BLOCK, prefix_rows, plen)
        d_keys = []
        d_values = []
        for head in range(half // HEAD_DIM):
            cut = slice(head * HEAD_DIM, (head + 1) * HEAD_DIM)
            qh, dh = q_ref[:, cut], d_mixed[:, cut]
            inner = jnp.sum(product[:, cut], -1, keepdims=True)
            shares = jnp.exp(
                dot_nt(qh, prefix_ref[0, :, cut]) + bias_prefix - lse_ref[:, head : head + 1]
            )
            d_shares = dot_nt(dh, prefix_ref[1, :, cut]).astype(B16).astype(F32)
            d_scores = (shares * (d_shares - inner)).astype(B16)
            d_keys.append(dot_tn(d_scores, qh))
            d_values.append(dot_tn(shares.astype(B16), dh))
        dprefix_ref[0] += jnp.concatenate(d_keys, 1)
        dprefix_ref[1] += jnp.concatenate(d_values, 1)

    return pl.pallas_call(
        body,
        grid_spec=pltpu.PrefetchScalarGridSpec(
            num_scalar_prefetch=1,
            grid=(row_count // BLOCK,),
            in_specs=[
                rows_spec(width),
                rows_spec(width),
                rows_spec(width),
                rows_spec(width),
                whole_spec(gain.shape),
                rows_spec(half),
                rows_spec(half),
                rows_spec(LANES),
                whole_spec(prefix.shape),
                ANY,
                ANY,
            ],
            out_specs=whole_spec(prefix.shape),
            scratch_shapes=weight.scratch,
        ),
        out_shape=shape(prefix.shape, F32),
        compiler_params=params(),
        name="first_prefix_back",
    )(me, gradient, own, other, middle, gain, q, mixed, lse, prefix, *weight.pair)


def table_rows(ids, table):
    count = ids.shape[0]
    shard_rows, width = table.shape
    size = lax.axis_size("dev")
    own = lax.axis_index("ta")
    ta_size = lax.axis_size("ta")
    shard = ids // shard_rows
    inside = ids % shard_rows
    order = jnp.arange(count, dtype=jnp.int32)
    same = ids[:, None] == ids[None, :]
    first = jnp.min(jnp.where(same, order[None], count), 1)
    is_first = first == order
    earlier = is_first[None] & (shard[None] == shard[:, None]) & (order[None] < first[:, None])
    rank = jnp.sum(earlier.astype(jnp.int32), 1)
    mine = shard % ta_size == own
    need = jnp.max(jnp.where(mine, rank, 0)) // SLOT_ROWS + 1
    slots = jnp.arange(size * SLOT_ROWS, dtype=jnp.int32)

    def fetch(turn, rows):
        local_rank = rank - turn * SLOT_ROWS
        used = mine & (local_rank >= 0) & (local_rank < SLOT_ROWS)
        slot = jnp.where(used, shard // ta_size * SLOT_ROWS + local_rank, -1)
        asked = jnp.max(jnp.where(slot[None] == slots[:, None], inside[None], 0), 1)
        asked = asked.reshape(size, SLOT_ROWS)
        header = jnp.broadcast_to(need, (size, 1))
        wanted = lax.all_to_all(jnp.concatenate([asked, header], 1), "dev", 0, 0)
        numbers = jnp.arange(shard_rows, dtype=jnp.int32)
        pick = (wanted[:, :SLOT_ROWS].reshape(-1, 1) == numbers[None]).astype(B16)
        sent = jnp.dot(pick, table, preferred_element_type=F32).astype(B16)
        got = lax.all_to_all(sent.reshape(size, SLOT_ROWS, width), "dev", 0, 0)
        spread = (slot[:, None] == slots[None]).astype(B16)
        found = jnp.dot(spread, got.reshape(-1, width), preferred_element_type=F32).astype(B16)
        return rows + found, jnp.max(wanted[:, SLOT_ROWS])

    rows, most = fetch(0, jnp.zeros((count, width), B16))
    most = jnp.maximum(most, partner(most.reshape(1, 1))[0, 0])

    def again(state):
        return state[0] < most

    def turn(state):
        return (state[0] + 1, fetch(state[0], state[1])[0])

    rows = lax.while_loop(again, turn, (jnp.int32(1), rows))[1]
    return rows + partner(rows)


def adamw_update(weight, moment, square, gradient, corr_one, corr_two):
    moment = BETA_ONE * moment + (1.0 - BETA_ONE) * gradient
    square = BETA_TWO * square + (1.0 - BETA_TWO) * gradient * gradient
    weight = weight - LEARN_RATE * (
        moment / corr_one / (jnp.sqrt(square / corr_two) + ADAM_EPS) + DECAY_RATE * weight
    )
    return (weight, moment, square)


def local(
    token_ids,
    bucket,
    seq_lengths,
    loss_pos,
    targets,
    wte,
    wpe,
    w_qkv,
    w_out,
    w_fc,
    w_proj,
    frozen_vec,
    fc_bias,
    final_norm,
    prefix_table,
    inner_weight,
    inner_bias,
    outer_weight,
    outer_bias,
    moment_prefix,
    square_prefix,
    moment_inner,
    square_inner,
    moment_inner_bias,
    square_inner_bias,
    moment_outer,
    square_outer,
    moment_outer_bias,
    square_outer_bias,
):
    row_count = token_ids.shape[0]
    scored = loss_pos.shape[0]
    width = wte.shape[1]
    half = w_qkv.shape[3]
    size = lax.axis_size("dev")
    own_index = lax.axis_index("ta")
    plen = prefix_table.shape[0]
    prefix_rows = 16
    me = lax.axis_index("dev").astype(jnp.int32).reshape(1)
    orders = bit_orders(size)
    stages = len(orders[0])
    bucket_width = bucket[0]
    shift = jnp.where(bucket_width == 256, 8, 10).astype(jnp.int32)
    layout = jnp.concatenate([shift.reshape(1), bucket_width.reshape(1), seq_lengths[0]])

    state = {}
    for layer_id in range(2):
        attention = jnp.concatenate(
            [w_qkv[layer_id, c] for c in range(3)] + [w_out[layer_id].T], 1
        )
        for part, rows in enumerate((attention, w_fc[layer_id], w_proj[layer_id].T)):
            state[layer_id, part] = [rows[None]]
    schedule = [[(layer_id, stage)] for layer_id in range(2) for stage in range(stages)]
    state = doubling_rounds(schedule, state, orders)

    def weight(layer_id, part, columns=None):
        return Gathered(state[layer_id, part], orders[part], columns)

    hidden = jnp.tanh(jnp.dot(prefix_table, inner_weight, precision=HIGHEST) + inner_bias)
    partial_kv = jnp.einsum("pr,rlcd->lcpd", hidden, outer_weight, precision=HIGHEST)
    prefix_kv = (sum_over_dev(partial_kv) + outer_bias[:, :, None, :]).astype(B16)
    prefix_kv = jnp.pad(prefix_kv, ((0, 0), (0, 0), (0, prefix_rows - plen), (0, 0)))

    rows = table_rows(jnp.concatenate([token_ids, targets]), wte)
    target_rows = rows[row_count:]
    repeat = row_count // 256
    places = jnp.where(bucket_width == 256, jnp.tile(wpe[:256], (repeat, 1)), wpe[:row_count])
    stream = rows[:row_count].astype(F32) + places.astype(F32)

    def head_bias(layer_id):
        part = lax.dynamic_slice_in_dim(frozen_vec[layer_id, 4:7], own_index * half, half, 1)
        return part.reshape(1, 3 * half)

    part, q0, mixed0, lse0 = first_attention(
        stream, frozen_vec[0, 0:2], head_bias(0), prefix_kv[0], layout, me, weight(0, 0), plen
    )
    vec = frozen_vec[0]
    part_two, middle0, slope0 = mlp(
        stream,
        part,
        partner(part),
        jnp.stack([vec[7], vec[2], vec[3]]),
        fc_bias[0:1],
        me,
        weight(0, 1),
        weight(0, 2),
    )

    vec_last = frozen_vec[1]
    picks_column = loss_pos.reshape(scored, 1)
    stream1, part, k1, v1, q1, mixed1, lse1, chosen = last_attention(
        middle0,
        part_two,
        partner(part_two),
        jnp.stack([vec[8], vec_last[0], vec_last[1]]),
        head_bias(1),
        prefix_kv[1],
        layout,
        loss_pos,
        picks_column,
        me,
        weight(1, 0),
        plen,
    )
    part_two, middle1, slope1 = mlp(
        chosen,
        part,
        partner(part),
        jnp.stack([vec_last[7], vec_last[2], vec_last[3]]),
        fc_bias[1:2],
        me,
        weight(1, 1),
        weight(1, 2),
    )
    both = part_two.astype(F32) + partner(part_two).astype(F32)
    head_rows = middle1 + (both + vec_last[8])
    center = head_rows - jnp.mean(head_rows, -1, keepdims=True)
    spread = jnp.mean(center * center, -1, keepdims=True)
    head_in = (center * lax.rsqrt(spread + EPS_NORM) * final_norm[0] + final_norm[1]).astype(B16)

    entries = 2 * wte.shape[0]
    padded = -(-entries // LANES) * LANES
    table = jnp.concatenate(
        [wte, partner(wte), jnp.zeros((padded - entries, width), B16)], 0
    )
    core_rows = scored // 2
    mine = lax.dynamic_slice_in_dim(head_in, own_index * core_rows, core_rows, 0)
    cuts = (0, 48, 96, core_rows)
    head = {(0, p): [mine[None, cuts[p] : cuts[p + 1]]] for p in range(3)}
    head = doubling_rounds([[(0, stage)] for stage in range(stages)], head, orders)
    results = []
    for side in range(2):
        stacks = [head[0, p][side].reshape(-1, width) for p in range(3)]
        answer = vocabulary(jnp.concatenate(stacks, 0), table, entries)
        ends = [0]
        for stack in stacks:
            ends.append(ends[-1] + stack.shape[0])
        results.append([answer[ends[p] : ends[p + 1]] for p in range(3)])
    keep, send = results
    for stage in reversed(range(stages)):
        if stage < stages - 1:
            split = [a.shape[0] // 2 for a in keep]
            send = [a[s:] for a, s in zip(keep, split)]
            keep = [a[:s] for a, s in zip(keep, split)]
        send = lax.optimization_barrier(tuple(send))
        keep = [merge(a, flip(b, orders[p][stage])) for p, (a, b) in enumerate(zip(keep, send))]
    own_means = jnp.concatenate(keep, 0)
    other_means = partner(own_means)
    means = jnp.where(
        own_index == 0,
        jnp.concatenate([own_means, other_means], 0),
        jnp.concatenate([other_means, own_means], 0),
    )
    place = loss_pos % bucket_width
    slot = loss_pos // bucket_width
    lengths = jnp.sum(
        jnp.where(
            slot[:, None] == jnp.arange(seq_lengths.shape[1], dtype=jnp.int32)[None],
            seq_lengths[0][None],
            0,
        ),
        1,
    )
    counted = (place < lengths).astype(F32).reshape(scored, 1)
    count_total = float(scored * size)
    grad_rows, loss_terms = head_back(
        means, head_rows, head_in, target_rows, counted, final_norm, count_total
    )
    loss_part = jnp.sum(loss_terms[:, 0])

    (part,) = mlp_back(grad_rows, slope1, me, weight(1, 1), weight(1, 2))
    part, spread_grad, d_prefix1 = last_attention_back(
        grad_rows,
        part,
        partner(part),
        middle1,
        vec_last[2:3],
        q1,
        k1,
        v1,
        mixed1,
        lse1,
        prefix_kv[1],
        layout,
        loss_pos,
        picks_column,
        me,
        weight(1, 0),
        plen,
    )
    d_prefix1 = sum_over_dev(d_prefix1[:, :plen])
    part, grad_stream = mlp_back(
        spread_grad,
        slope0,
        me,
        weight(0, 1),
        weight(0, 2),
        (stream1, vec_last[0:1], part, partner(part)),
    )
    d_prefix0 = first_prefix_back(
        grad_stream,
        part,
        partner(part),
        middle0,
        vec[2:3],
        q0,
        mixed0,
        lse0,
        prefix_kv[0],
        me,
        weight(0, 0, (3 * half, 4 * half)),
        plen,
    )
    d_prefix0 = sum_over_dev(d_prefix0[:, :plen])
    d_prefix = jnp.stack([d_prefix0, d_prefix1])

    d_outer = jnp.einsum("pr,lcpd->rlcd", hidden, d_prefix, precision=HIGHEST)
    d_outer_bias = jnp.sum(d_prefix, 2)
    hidden_part = jnp.einsum("lcpd,rlcd->pr", d_prefix, outer_weight, precision=HIGHEST)
    outer_square = jnp.sum(d_outer * d_outer) + jnp.sum(d_outer_bias * d_outer_bias) / size
    over_ta = jnp.concatenate(
        [hidden_part, jnp.broadcast_to(outer_square, (1, hidden_part.shape[1]))], 0
    )
    over_ta = over_ta + partner(over_ta)
    d_hidden = over_ta[:plen]
    d_pre = d_hidden * (1.0 - hidden * hidden)
    d_inner = jnp.dot(prefix_table.T, d_pre, precision=HIGHEST)
    d_inner_bias = jnp.sum(d_pre, 0)
    table_part = jnp.dot(d_pre, inner_weight.T, precision=HIGHEST)
    squares = over_ta[plen, 0] + jnp.sum(d_inner * d_inner) + jnp.sum(d_inner_bias * d_inner_bias)
    lane = jnp.arange(table_part.shape[1], dtype=jnp.int32)
    last_row = jnp.where(lane == 0, squares, jnp.where(lane == 1, loss_part, 0.0))
    totals = sum_over_dev(jnp.concatenate([table_part, last_row[None]], 0))
    d_table = totals[:plen]
    square_sum = totals[plen, 0]
    loss_value = totals[plen, 1] / count_total
    grad_total = jnp.sqrt(square_sum + jnp.sum(d_table * d_table))
    factor = jnp.minimum(1.0, CLIP_NORM / (grad_total + 1e-06))
    corr_one = 1.0 - BETA_ONE**adam_steps
    corr_two = 1.0 - BETA_TWO**adam_steps
    prefix_out = adamw_update(
        prefix_table, moment_prefix, square_prefix, factor * d_table, corr_one, corr_two
    )
    inner_out = adamw_update(
        inner_weight, moment_inner, square_inner, factor * d_inner, corr_one, corr_two
    )
    ibias_out = adamw_update(
        inner_bias, moment_inner_bias, square_inner_bias, factor * d_inner_bias, corr_one, corr_two
    )
    outer_out = adamw_update(
        outer_weight, moment_outer, square_outer, factor * d_outer, corr_one, corr_two
    )
    obias_out = adamw_update(
        outer_bias, moment_outer_bias, square_outer_bias, factor * d_outer_bias, corr_one, corr_two
    )
    return (
        loss_value.reshape(1),
        grad_total.reshape(1),
        prefix_out[0],
        prefix_out[1],
        prefix_out[2],
        inner_out[0],
        inner_out[1],
        inner_out[2],
        ibias_out[0],
        ibias_out[1],
        ibias_out[2],
        outer_out[0],
        outer_out[1],
        outer_out[2],
        obias_out[0],
        obias_out[1],
        obias_out[2],
        prefix_out[0].astype(B16),
        inner_out[0].astype(B16),
        ibias_out[0].astype(B16),
        outer_out[0].astype(B16),
        obias_out[0].astype(B16),
    )


def solution(mesh):
    in_specs = (
        P("dev"),
        P("dev"),
        P("dev", None),
        P("dev"),
        P("dev"),
        P(("dev", "ta"), None),
        P(),
        P(None, None, "dev", "ta"),
        P(None, "ta", "dev"),
        P(None, "dev", "ta"),
        P(None, "ta", "dev"),
        P(),
        P(None, "ta"),
        P(),
        P(),
        P(None, "dev"),
        P("dev"),
        P("dev", None, None, "ta"),
        P(None, None, "ta"),
        P(),
        P(),
        P(None, "dev"),
        P(None, "dev"),
        P("dev"),
        P("dev"),
        P("dev", None, None, "ta"),
        P("dev", None, None, "ta"),
        P(None, None, "ta"),
        P(None, None, "ta"),
    )
    out_specs = (
        P(),
        P(),
        P(),
        P(),
        P(),
        P(None, "dev"),
        P(None, "dev"),
        P(None, "dev"),
        P("dev"),
        P("dev"),
        P("dev"),
        P("dev", None, None, "ta"),
        P("dev", None, None, "ta"),
        P("dev", None, None, "ta"),
        P(None, None, "ta"),
        P(None, None, "ta"),
        P(None, None, "ta"),
        P(),
        P(None, "dev"),
        P("dev"),
        P("dev", None, None, "ta"),
        P(None, None, "ta"),
    )
    return jax.shard_map(local, mesh=mesh, in_specs=in_specs, out_specs=out_specs, check_vma=False)
```

```python
import functools

import jax
import jax.numpy as jnp
from jax import lax
from jax.experimental import pallas as pl
from jax.experimental.pallas import tpu as pltpu
from jax.sharding import PartitionSpec as P

HEAD_DIM = 64


EPS_NORM = 1e-05
CLIP_NORM = 0.001
LEARN_RATE = 0.02
BETA_ONE = 0.9
BETA_TWO = 0.999
ADAM_EPS = 1e-08
DECAY_RATE = 0.01
adam_steps = 10.0
NEG_BIG = -1e30
HIGHEST = lax.Precision.HIGHEST
F32 = jnp.float32
B16 = jnp.bfloat16
GELU_SCALE = 0.7978845608028654
GELU_CUBE = 0.044715
SLOT_ROWS = 48
BLOCK = 256
LANES = 128
SWAP = [(0, 1), (1, 0)]


def shape(dims, dtype):
    return jax.ShapeDtypeStruct(dims, dtype)


def params(**more):
    return pltpu.CompilerParams(dimension_semantics=("arbitrary",), **more)


def cost(microseconds):
    return pl.CostEstimate(
        flops=int(microseconds * 1.15e9), transcendentals=0, bytes_accessed=1024
    )


def flip(array, bit):
    size = lax.axis_size("dev")
    return lax.ppermute(array, "dev", [(i, i ^ bit) for i in range(size)])


def partner(array):
    return lax.ppermute(array, "ta", SWAP)


def bit_orders(size, parts):
    bits = [1 << k for k in range(size.bit_length() - 1)]
    if size == 16:
        x, y, near, far = bits
        if parts == 3:
            return ((far, y, near, x), (near, far, x, y), (far, x, y, near))
        return (
            (x, y, near, far),
            (x, y, far, near),
            (near, far, x, y),
            (far, near, y, x),
        )
    return tuple(tuple(bits[k:] + bits[:k]) for k in range(parts))


def cuts_of(total, unit, parts):
    sixths = (0, 2, 4) if parts == 3 else (0, 1, 2, 4)
    return [total * k // 6 // unit * unit for k in sixths] + [total]


def pack(groups):
    arrays = [array for group, unused, unused in groups for array in group]
    outs = []
    moves = []
    for number, (group, first, last) in enumerate(groups):
        total = 0
        for array in group:
            moves.append((number, total, array.shape[0], first, last - first))
            total += array.shape[0]
        outs.append(shape((total, group[0].shape[1], last - first), group[0].dtype))

    def body(*refs):
        sems = refs[-1]
        copies = [
            pltpu.make_async_copy(
                refs[index].at[:, :, pl.ds(first, wide)],
                refs[len(arrays) + number].at[pl.ds(begin, count)],
                sems.at[index],
            )
            for index, (number, begin, count, first, wide) in enumerate(moves)
        ]
        for copy in copies:
            copy.start()
        for copy in copies:
            copy.wait()

    return pl.pallas_call(
        body,
        in_specs=[pl.BlockSpec(memory_space=pl.ANY)] * len(arrays),
        out_specs=[pl.BlockSpec(memory_space=pltpu.VMEM)] * len(outs),
        out_shape=outs,
        scratch_shapes=[pltpu.SemaphoreType.DMA((len(arrays),))],
        cost_estimate=cost(2),
        name="pack",
    )(*arrays)


class Rounds:
    def __init__(self):
        self.orders = {}
        self.held = {}
        self.split = {}
        self.before = []

    def add(self, chunk, orders, arrays, splits=None):
        self.orders[chunk] = orders
        for part, array in enumerate(arrays):
            self.held[chunk, part] = [array[None]]
            self.split[chunk, part] = splits[part] if splits else None

    def step(self, chunk, stage, side=None, through=()):
        parts = range(len(self.orders[chunk]))
        held = [self.held[chunk, part] for part in parts]
        if stage == 0:
            sends = [arrays[0] for arrays in held]
        else:
            spans = []
            for part, arrays in zip(parts, held):
                cut, width = self.split[chunk, part], arrays[0].shape[2]
                spans.append((cut if side == 1 else 0, cut if side == 0 else width))
            sends = pack([(arrays, *span) for arrays, span in zip(held, spans)])
        through, sends, unused = lax.optimization_barrier((through, sends, self.before))
        self.before = []
        for part, send in enumerate(sends):
            got = flip(send, self.orders[chunk][part][stage])
            self.held[(chunk, part) if side is None else (chunk, part, side)] = [send, got]
            self.before.append(got)
        return through


def sum_over_dev(array):
    size = lax.axis_size("dev")
    bit = 1
    while bit < size:
        if bit * 2 < size:
            near, far, both = flip(array, bit), flip(array, bit * 2), flip(array, bit * 3)
            array = (array + near) + (far + both)
        else:
            array = array + flip(array, bit)
        bit = bit * 4
    return array


def norm_rows(x):
    center = x - jnp.mean(x, -1, keepdims=True)
    scale = lax.rsqrt(jnp.mean(center * center, -1, keepdims=True) + EPS_NORM)
    return center * scale, scale


def norm_rows_back(gradient, x, gain):
    xhat, scale = norm_rows(x)
    e2 = gradient * gain
    mean_one = jnp.mean(e2, -1, keepdims=True)
    mean_two = jnp.mean(e2 * xhat, -1, keepdims=True)
    return (e2 - mean_one - xhat * mean_two) * scale


def dot_nn(a, b):
    return lax.dot_general(a, b, (((1,), (0,)), ((), ())), preferred_element_type=F32)


def dot_nt(a, b):
    return lax.dot_general(a, b, (((1,), (1,)), ((), ())), preferred_element_type=F32)


def dot_tn(a, b):
    return lax.dot_general(a, b, (((0,), (0,)), ((), ())), preferred_element_type=F32)


class Gathered:
    def __init__(self, segments, first, last):
        self.pieces = []
        for stacks, order, begin, end, skip in segments:
            low, high = max(first, begin), min(last, end)
            if low < high:
                self.pieces.append((stacks, order, low - begin + skip, high - low, low - first))
        stacks, order, *unused = self.pieces[0]
        self.rows = stacks[0].shape[1]
        self.blocks = 1 << len(order)
        self.scratch = [
            pltpu.VMEM((self.blocks * self.rows, last - first), B16),
            pltpu.SemaphoreType.DMA((len(self.pieces) * self.blocks,)),
        ]
        self.operands = [array for piece in self.pieces for array in piece[0]]
        self.specs = [pl.BlockSpec(memory_space=pl.ANY)] * len(self.operands)

    def each(self, act, me, refs, full, sems):
        for number, (stacks, order, source, wide, target) in enumerate(self.pieces):
            blocks = self.blocks // len(stacks)
            for side, ref in enumerate(refs[number * len(stacks) : (number + 1) * len(stacks)]):

                def one(index, carry, side=side, ref=ref):
                    place = me ^ (order[-1] if side else 0)
                    for k, bit in enumerate(order[:-1]):
                        place = place ^ jnp.where((index >> k) % 2 == 1, bit, 0)
                    start = pl.multiple_of(place * self.rows, self.rows)
                    copy = pltpu.make_async_copy(
                        ref.at[index, :, pl.ds(source, wide)],
                        full.at[pl.ds(start, self.rows), pl.ds(target, wide)],
                        sems.at[number * self.blocks + side * blocks + index],
                    )
                    act(copy)
                    return carry

                lax.fori_loop(0, blocks, one, 0)

    def start(self, *refs):
        self.each(lambda copy: copy.start(), *refs)

    def wait(self, *refs):
        self.each(lambda copy: copy.wait(), *refs)


def rows_spec(width, block=BLOCK):
    return pl.BlockSpec((block, width), lambda i, *refs: (i, 0))


def whole_spec(dims):
    return pl.BlockSpec(dims, lambda i, *refs: (0,) * len(dims))


def key_bias(layout_ref, query_pos, key_count):
    shift = layout_ref[0]
    dims = (query_pos.shape[0], key_count)
    key_pos = lax.broadcasted_iota(jnp.int32, (1, key_count), 1)
    key_seg = lax.shift_right_logical(key_pos, jnp.full((1, key_count), shift, jnp.int32))
    query_seg = lax.shift_right_logical(query_pos, jnp.full(query_pos.shape, shift, jnp.int32))
    length = jnp.zeros((1, key_count), jnp.int32)
    for slot in range(layout_ref.shape[0] - 2):
        length = jnp.where(key_seg == slot, layout_ref[2 + slot], length)
    place = key_pos - key_seg * layout_ref[1]
    key_seg = jnp.where(place < length, key_seg, -1)
    seen = (jnp.broadcast_to(query_seg, dims) == jnp.broadcast_to(key_seg, dims)) & (
        jnp.broadcast_to(key_pos, dims) <= jnp.broadcast_to(query_pos, dims)
    )
    return jnp.where(seen, 0.0, NEG_BIG)


def prefix_bias(rows, prefix_rows, prefix_len):
    lane = lax.broadcasted_iota(jnp.int32, (rows, prefix_rows), 1)
    return jnp.where(lane < prefix_len, 0.0, NEG_BIG)


def attend(query, key, value, key_prefix, value_prefix, bias, bias_prefix):
    scores = dot_nt(query, key) + bias
    scores_prefix = dot_nt(query, key_prefix) + bias_prefix
    highest = jnp.maximum(
        jnp.max(scores, -1, keepdims=True), jnp.max(scores_prefix, -1, keepdims=True)
    )
    shares = jnp.exp(scores - highest)
    shares_prefix = jnp.exp(scores_prefix - highest)
    total = jnp.sum(shares, -1, keepdims=True) + jnp.sum(shares_prefix, -1, keepdims=True)
    mixed = dot_nn(shares.astype(B16), value) + dot_nn(shares_prefix.astype(B16), value_prefix)
    return mixed / total, highest + jnp.log(total)


def attend_pairs(q_ref, k_ref, v_ref, prefix_ref, mixed_ref, lse_ref, rows, key_count, bias, plen):
    prefix_rows = prefix_ref.shape[1]
    bias_prefix = prefix_bias(BLOCK, prefix_rows, plen)
    lse_ref[rows, :] = jnp.zeros((BLOCK, LANES), F32)
    lane = lax.broadcasted_iota(jnp.int32, (BLOCK, LANES), 1)

    def pair(index, carry):
        columns = pl.ds(pl.multiple_of(index * LANES, LANES), LANES)
        query = q_ref[rows, columns]
        key = k_ref[pl.ds(0, key_count), columns]
        value = v_ref[pl.ds(0, key_count), columns]
        key_prefix = prefix_ref[0, :, columns]
        value_prefix = prefix_ref[1, :, columns]
        parts = []
        for side in range(2):
            cut = slice(side * HEAD_DIM, (side + 1) * HEAD_DIM)
            mixed, lse = attend(
                query[:, cut],
                key[:, cut],
                value[:, cut],
                key_prefix[:, cut],
                value_prefix[:, cut],
                bias,
                bias_prefix,
            )
            parts.append(mixed)
            lse_ref[rows, :] = jnp.where(
                lane // prefix_rows == 2 * index + side, lse, lse_ref[rows, :]
            )
        mixed_ref[rows, columns] = jnp.concatenate(parts, 1).astype(B16)
        return carry

    lax.fori_loop(0, q_ref.shape[1] // LANES, pair, 0)


def first_attention(stream, vectors, bias_qkv, prefix, layout, me, weight, plen):
    row_count, width = stream.shape
    half = prefix.shape[2]
    scale = HEAD_DIM ** (-0.5)

    stacks = len(weight.operands)

    def body(me_ref, layout_ref, stream_ref, vec_ref, bias_ref, prefix_ref, *refs):
        part_ref, q_out, mixed_out, lse_out, full, sems, q_s, k_s, v_s = refs[stacks:]
        step = pl.program_id(0)
        refs = (me_ref[0], refs[:stacks], full, sems)

        @pl.when(step == 0)
        def _():
            weight.start(*refs)
            weight.wait(*refs)

        xhat, unused = norm_rows(stream_ref[...])
        normed = (xhat * vec_ref[0:1, :] + vec_ref[1:2, :]).astype(B16)
        qkv = dot_nn(normed, full[:, : 3 * half]) + bias_ref[...]
        rows = pl.ds(pl.multiple_of(step * BLOCK, BLOCK), BLOCK)
        q_s[...] = (qkv[:, :half].astype(B16) * scale).astype(B16)
        k_s[rows, :] = qkv[:, half : 2 * half].astype(B16)
        v_s[rows, :] = qkv[:, 2 * half :].astype(B16)
        q_out[...] = q_s[...]
        local_pos = lax.broadcasted_iota(jnp.int32, (BLOCK, 1), 0)
        for case in range(row_count // BLOCK):

            @pl.when(step == case)
            def _(case=case):
                key_count = (case + 1) * BLOCK
                bias = key_bias(layout_ref, local_pos + case * BLOCK, key_count)
                attend_pairs(
                    q_s, k_s, v_s, prefix_ref, mixed_out, lse_out,
                    pl.ds(0, BLOCK), key_count, bias, plen,
                )

        part_ref[...] = dot_nt(mixed_out[...], full[:, 3 * half :]).astype(B16)

    return pl.pallas_call(
        body,
        grid_spec=pltpu.PrefetchScalarGridSpec(
            num_scalar_prefetch=2,
            grid=(row_count // BLOCK,),
            in_specs=[
                rows_spec(width),
                whole_spec(vectors.shape),
                whole_spec(bias_qkv.shape),
                whole_spec(prefix.shape),
                *weight.specs,
            ],
            out_specs=[rows_spec(width), rows_spec(half), rows_spec(half), rows_spec(LANES)],
            scratch_shapes=weight.scratch
            + [pltpu.VMEM((BLOCK, half), B16)]
            + [pltpu.VMEM((row_count, half), B16)] * 2,
        ),
        out_shape=[
            shape((row_count, width), B16),
            shape((row_count, half), B16),
            shape((row_count, half), B16),
            shape((row_count, LANES), F32),
        ],
        compiler_params=params(),
        cost_estimate=cost(30 * row_count // 1024),
        name="first_attention",
    )(me, layout, stream, vectors, bias_qkv, prefix, *weight.operands)


def mlp(base, own, other, vectors, bias_up, me, w_up, w_down):
    row_count, width = base.shape
    hidden = bias_up.shape[1]

    ups, downs = len(w_up.operands), len(w_down.operands)

    def body(me_ref, base_ref, own_ref, other_ref, vec_ref, bias_ref, *refs):
        part_ref, middle_ref, slope_ref, up, up_sems, down, down_sems = refs[ups + downs :]
        step = pl.program_id(0)
        up_refs = (me_ref[0], refs[:ups], up, up_sems)
        down_refs = (me_ref[0], refs[ups : ups + downs], down, down_sems)

        @pl.when(step == 0)
        def _():
            w_up.start(*up_refs)
            w_down.start(*down_refs)

        middle = base_ref[...] + (
            (own_ref[...].astype(F32) + other_ref[...].astype(F32)) + vec_ref[0:1, :]
        )
        middle_ref[...] = middle
        xhat, unused = norm_rows(middle)
        normed = (xhat * vec_ref[1:2, :] + vec_ref[2:3, :]).astype(B16)

        @pl.when(step == 0)
        def _():
            w_up.wait(*up_refs)

        u = dot_nn(normed, up[...]) + bias_ref[...]
        square = u * u
        t = jnp.tanh(GELU_SCALE * u * (1.0 + GELU_CUBE * square))
        half_one = 0.5 + 0.5 * t
        active = (u * half_one).astype(B16)
        slope = half_one + (0.5 * GELU_SCALE) * u * (1.0 - t * t) * (1.0 + 3 * GELU_CUBE * square)
        slope_ref[...] = slope.astype(B16)

        @pl.when(step == 0)
        def _():
            w_down.wait(*down_refs)

        part_ref[...] = dot_nt(active, down[...]).astype(B16)

    return pl.pallas_call(
        body,
        grid_spec=pltpu.PrefetchScalarGridSpec(
            num_scalar_prefetch=1,
            grid=(row_count // BLOCK,),
            in_specs=[
                rows_spec(width),
                rows_spec(width),
                rows_spec(width),
                whole_spec(vectors.shape),
                whole_spec(bias_up.shape),
                *w_up.specs,
                *w_down.specs,
            ],
            out_specs=[rows_spec(width), rows_spec(width), rows_spec(hidden)],
            scratch_shapes=w_up.scratch + w_down.scratch,
        ),
        out_shape=[
            shape((row_count, width), B16),
            shape((row_count, width), F32),
            shape((row_count, hidden), B16),
        ],
        compiler_params=params(),
        cost_estimate=cost(23 * row_count // 1024),
        name="mlp",
    )(me, base, own, other, vectors, bias_up, *w_up.operands, *w_down.operands)


def last_attention(base, own, other, vectors, bias_qkv, prefix, layout, picks, picks_column, me,
                   weight, plen):
    row_count, width = base.shape
    half = prefix.shape[2]
    scored = picks.shape[0]
    steps = row_count // BLOCK
    scale = HEAD_DIM ** (-0.5)

    stacks = len(weight.operands)

    def body(me_ref, layout_ref, picks_ref, base_ref, own_ref, other_ref, vec_ref, bias_ref,
             prefix_ref, column_ref, *refs):
        (stream_out, part_ref, k_out, v_out, q_out, mixed_out, lse_out, chosen_out,
         full, sems, stream_s, k_s, v_s) = refs[stacks:]
        step = pl.program_id(0)
        refs = (me_ref[0], refs[:stacks], full, sems)

        @pl.when(step == 0)
        def _():
            weight.start(*refs)
            weight.wait(*refs)

        stream = base_ref[...] + (
            (own_ref[...].astype(F32) + other_ref[...].astype(F32)) + vec_ref[0:1, :]
        )
        stream_out[...] = stream
        rows = pl.ds(pl.multiple_of(step * BLOCK, BLOCK), BLOCK)
        stream_s[rows, :] = stream
        xhat, unused = norm_rows(stream)
        normed = (xhat * vec_ref[1:2, :] + vec_ref[2:3, :]).astype(B16)
        keys_values = (
            dot_nn(normed, full[:, half : 3 * half]) + bias_ref[:, half : 3 * half]
        ).astype(B16)
        k_out[...] = keys_values[:, :half]
        v_out[...] = keys_values[:, half:]
        k_s[rows, :] = keys_values[:, :half]
        v_s[rows, :] = keys_values[:, half:]

        @pl.when(step == steps - 1)
        def _():
            def pick(index, carry):
                chosen_out[pl.ds(index, 1), :] = stream_s[pl.ds(picks_ref[index], 1), :]
                return carry

            lax.fori_loop(0, scored, pick, 0, unroll=8)
            for first in range(0, scored, BLOCK):
                block = pl.ds(first, BLOCK)
                chosen_hat, unused = norm_rows(chosen_out[block, :])
                chosen = (chosen_hat * vec_ref[1:2, :] + vec_ref[2:3, :]).astype(B16)
                query = (dot_nn(chosen, full[:, :half]) + bias_ref[:, :half]).astype(B16)
                q_out[block, :] = (query * scale).astype(B16)
                bias = key_bias(layout_ref, column_ref[block, :], row_count)
                attend_pairs(
                    q_out, k_s, v_s, prefix_ref, mixed_out, lse_out, block, row_count, bias, plen
                )
                part_ref[block, :] = dot_nt(mixed_out[block, :], full[:, 3 * half :]).astype(B16)

    return pl.pallas_call(
        body,
        grid_spec=pltpu.PrefetchScalarGridSpec(
            num_scalar_prefetch=3,
            grid=(steps,),
            in_specs=[
                rows_spec(width),
                rows_spec(width),
                rows_spec(width),
                whole_spec(vectors.shape),
                whole_spec(bias_qkv.shape),
                whole_spec(prefix.shape),
                whole_spec(picks_column.shape),
                *weight.specs,
            ],
            out_specs=[
                rows_spec(width),
                whole_spec((scored, width)),
                rows_spec(half),
                rows_spec(half),
                whole_spec((scored, half)),
                whole_spec((scored, half)),
                whole_spec((scored, LANES)),
                whole_spec((scored, width)),
            ],
            scratch_shapes=weight.scratch
            + [pltpu.VMEM((row_count, width), F32)]
            + [pltpu.VMEM((row_count, half), B16)] * 2,
        ),
        out_shape=[
            shape((row_count, width), F32),
            shape((scored, width), B16),
            shape((row_count, half), B16),
            shape((row_count, half), B16),
            shape((scored, half), B16),
            shape((scored, half), B16),
            shape((scored, LANES), F32),
            shape((scored, width), F32),
        ],
        compiler_params=params(),
        cost_estimate=cost(22),
        name="last_attention",
    )(me, layout, picks, base, own, other, vectors, bias_qkv, prefix, picks_column, *weight.operands)


def split_lse(lse, rows):
    high = lse.astype(B16).astype(F32)
    middle = (lse - high).astype(B16).astype(F32)
    low = (lse - high) - middle
    lane = lax.broadcasted_iota(jnp.int32, (rows, LANES), 1)
    packed = jnp.where(lane == 0, high, jnp.where(lane == 1, middle, jnp.where(lane == 2, low, 0.0)))
    return packed.astype(B16)


VMEM = pl.BlockSpec(memory_space=pltpu.VMEM)


def vocabulary(stacks, table, entries):
    width = table.shape[1]
    padded = table.shape[0]
    half = padded // 2
    ends = [0]
    for stack in stacks:
        ends.append(ends[-1] + stack.shape[0])
    block = max(b for b in range(16, 400, 16) if ends[-1] % b == 0)

    def body(*refs):
        table_ref = refs[len(stacks)]
        outs = refs[len(stacks) + 1 : -2]
        rows_s, mean_s = refs[-2:]
        for ref, first, last in zip(refs, ends[:-1], ends[1:]):
            rows_s[first:last, :] = ref[...]

        def turn(index, carry):
            rows = pl.ds(pl.multiple_of(index * block, block), block)
            logits = dot_nt(rows_s[rows, :], table_ref[...])
            pieces = []
            for first in range(0, padded, LANES):
                piece = logits[:, first : first + LANES]
                if any(c % half >= entries for c in range(first, first + LANES)):
                    lane = lax.broadcasted_iota(jnp.int32, piece.shape, 1) + first
                    piece = jnp.where(lane % half < entries, piece, NEG_BIG)
                pieces.append(piece)
            logits = jnp.concatenate(pieces, 1)
            highest = jnp.max(logits, -1, keepdims=True)
            shares = jnp.exp(logits - highest)
            total = jnp.sum(shares, -1, keepdims=True)
            mean = dot_nn(shares.astype(B16), table_ref[...]) / total
            mean_s[rows, :width] = mean.astype(B16)
            mean_s[rows, width:] = split_lse(highest + jnp.log(total), block)
            return carry

        lax.fori_loop(0, ends[-1] // block, turn, 0)
        for out, first, last in zip(outs, ends[:-1], ends[1:]):
            out[...] = mean_s[first:last, :]

    return pl.pallas_call(
        body,
        in_specs=[VMEM] * (len(stacks) + 1),
        out_specs=[VMEM] * len(stacks),
        out_shape=[shape((stack.shape[0], width + LANES), B16) for stack in stacks],
        scratch_shapes=[
            pltpu.VMEM((ends[-1], width), B16),
            pltpu.VMEM((ends[-1], width + LANES), B16),
        ],
        cost_estimate=cost(10 * ends[-1] // 384),
        name="vocabulary",
    )(*stacks, table)


def joined_lse(block, width):
    return jnp.sum(block[:, width:].astype(F32)[:, 0:4], -1, keepdims=True)


def merge(firsts, seconds, last):
    wide = firsts[0].shape[1]
    width = wide - LANES
    count = len(firsts)
    pieces = 1 if last else 2

    def body(*refs):
        outs = refs[2 * count :]
        for part in range(count):
            first_ref, second_ref = refs[part], refs[count + part]
            rows = first_ref.shape[0] // pieces
            for piece in range(pieces):
                one = first_ref[piece * rows : (piece + 1) * rows, :]
                two = second_ref[piece * rows : (piece + 1) * rows, :]
                lse_one, lse_two = joined_lse(one, width), joined_lse(two, width)
                highest = jnp.maximum(lse_one, lse_two)
                scale_one, scale_two = jnp.exp(lse_one - highest), jnp.exp(lse_two - highest)
                total = scale_one + scale_two
                mean = one[:, :width].astype(F32) * (scale_one / total)
                mean = mean + two[:, :width].astype(F32) * (scale_two / total)
                out_ref = outs[piece * count + part]
                out_ref[:, :width] = mean.astype(B16)
                out_ref[:, width:] = split_lse(highest + jnp.log(total), rows)

    outs = pl.pallas_call(
        body,
        in_specs=[VMEM] * (2 * count),
        out_specs=[VMEM] * (pieces * count),
        out_shape=[shape((a.shape[0] // pieces, wide), B16) for a in firsts] * pieces,
        cost_estimate=cost(3),
        name="merge",
    )(*firsts, *seconds)
    return outs[:count], outs[count:]


def head_back(means, head_rows, head_in, target_rows, counted, final_norm, count_total):
    scored, width = head_rows.shape

    def body(mean_ref, rows_ref, in_ref, target_ref, counted_ref, norm_ref, grad_ref, loss_ref):
        lse = joined_lse(mean_ref[...], width)
        target = target_ref[...].astype(F32)
        logit = jnp.sum(in_ref[...].astype(F32) * target, -1, keepdims=True)
        seen = counted_ref[...]
        loss_ref[...] = jnp.broadcast_to((lse - logit) * seen, (BLOCK, LANES))
        d_head = (mean_ref[:, :width].astype(F32) - target) * (seen / count_total)
        grad_ref[...] = norm_rows_back(d_head, rows_ref[...], norm_ref[0:1, :])

    return pl.pallas_call(
        body,
        grid=(scored // BLOCK,),
        in_specs=[
            rows_spec(width + LANES),
            rows_spec(width),
            rows_spec(width),
            rows_spec(width),
            rows_spec(1),
            whole_spec(final_norm.shape),
        ],
        out_specs=[rows_spec(width), rows_spec(LANES)],
        out_shape=[shape((scored, width), F32), shape((scored, LANES), F32)],
        compiler_params=params(),
        cost_estimate=cost(4),
        name="head_back",
    )(means, head_rows, head_in, target_rows, counted, final_norm)


def mlp_back(gradient, slope, me, w_up, w_down, residual=None):
    row_count, width = gradient.shape
    hidden = slope.shape[1]
    extra = [] if residual is None else list(residual)
    ups, downs = len(w_up.operands), len(w_down.operands)

    def body(me_ref, *refs):
        grad_ref, slope_ref = refs[0], refs[1]
        extra_refs = refs[2 : 2 + len(extra)]
        refs = refs[2 + len(extra) :]
        part_ref, *rest = refs[ups + downs :]
        up, up_sems, down, down_sems = rest[-4:]
        step = pl.program_id(0)
        up_refs = (me_ref[0], refs[:ups], up, up_sems)
        down_refs = (me_ref[0], refs[ups : ups + downs], down, down_sems)

        @pl.when(step == 0)
        def _():
            w_down.start(*down_refs)
            w_up.start(*up_refs)

        grad = grad_ref[...]
        if extra:
            stream_ref, gain_ref, own_ref, other_ref = extra_refs
            incoming = own_ref[...].astype(F32) + other_ref[...].astype(F32)
            grad = grad + norm_rows_back(incoming, stream_ref[...], gain_ref[...])
            rest[0][...] = grad

        @pl.when(step == 0)
        def _():
            w_down.wait(*down_refs)

        d_active = dot_nn(grad.astype(B16), down[...])
        d_upward = (d_active * slope_ref[...].astype(F32)).astype(B16)

        @pl.when(step == 0)
        def _():
            w_up.wait(*up_refs)

        part_ref[...] = dot_nt(d_upward, up[...]).astype(B16)

    extra_specs = (
        [rows_spec(width), whole_spec(extra[1].shape), rows_spec(width), rows_spec(width)]
        if extra
        else []
    )
    return pl.pallas_call(
        body,
        grid_spec=pltpu.PrefetchScalarGridSpec(
            num_scalar_prefetch=1,
            grid=(row_count // BLOCK,),
            in_specs=[rows_spec(width), rows_spec(hidden)] + extra_specs + w_up.specs + w_down.specs,
            out_specs=[rows_spec(width)] * (2 if extra else 1),
            scratch_shapes=w_up.scratch + w_down.scratch,
        ),
        out_shape=[shape((row_count, width), B16)]
        + ([shape((row_count, width), F32)] if extra else []),
        compiler_params=params(),
        cost_estimate=cost(20 * row_count // 1024),
        name="mlp_back",
    )(me, gradient, slope, *extra, *w_up.operands, *w_down.operands)


def last_attention_back(gradient, own, other, middle, gain, q, k, v, lse, prefix, layout, picks,
                        picks_column, me, weight, plen):
    scored, width = gradient.shape
    row_count, half = k.shape
    prefix_rows = prefix.shape[1]
    scale = HEAD_DIM ** (-0.5)

    stacks = len(weight.operands)

    def body(me_ref, layout_ref, picks_ref, grad_ref, own_ref, other_ref, middle_ref, gain_ref,
             q_ref, k_ref, v_ref, lse_ref, prefix_ref, column_ref, *refs):
        (part_ref, spread_ref, dprefix_ref, full, sems,
         dmix_s, dq_s, dk_s, dv_s, sum_s, rows_s) = refs[stacks:]
        refs = (me_ref[0], refs[:stacks], full, sems)
        weight.start(*refs)
        incoming = own_ref[...].astype(F32) + other_ref[...].astype(F32)
        grad_mid = grad_ref[...] + norm_rows_back(incoming, middle_ref[...], gain_ref[...])
        rows_s[...] = grad_mid
        spread_ref[...] = jnp.zeros((row_count, width), F32)

        def put(index, carry):
            spread_ref[pl.ds(picks_ref[index], 1), :] = rows_s[pl.ds(index, 1), :]
            return carry

        lax.fori_loop(0, scored, put, 0, unroll=8)
        weight.wait(*refs)
        dmix_s[...] = dot_nn(grad_mid.astype(B16), full[:, 3 * half :]).astype(B16)
        bias = key_bias(layout_ref, column_ref[...], row_count)
        bias_prefix = prefix_bias(scored, prefix_rows, plen)
        lane = lax.broadcasted_iota(jnp.int32, (scored, LANES), 1)

        def pair(index, carry):
            columns = pl.ds(pl.multiple_of(index * LANES, LANES), LANES)
            query, key, value = q_ref[:, columns], k_ref[:, columns], v_ref[:, columns]
            d_mixed = dmix_s[:, columns]
            key_p, value_p = prefix_ref[0, :, columns], prefix_ref[1, :, columns]
            found = [[], [], [], [], []]
            for side in range(2):
                cut = slice(side * HEAD_DIM, (side + 1) * HEAD_DIM)
                log_total = jnp.sum(
                    jnp.where(lane == prefix_rows * (2 * index + side), lse_ref[...], 0.0),
                    -1,
                    keepdims=True,
                )
                qh, dh = query[:, cut], d_mixed[:, cut]
                shares = jnp.exp(dot_nt(qh, key[:, cut]) + bias - log_total)
                shares_p = jnp.exp(dot_nt(qh, key_p[:, cut]) + bias_prefix - log_total)
                d_shares = dot_nt(dh, value[:, cut]).astype(B16).astype(F32)
                d_shares_p = dot_nt(dh, value_p[:, cut]).astype(B16).astype(F32)
                inner = jnp.sum(shares * d_shares, -1, keepdims=True) + jnp.sum(
                    shares_p * d_shares_p, -1, keepdims=True
                )
                d_scores = (shares * (d_shares - inner)).astype(B16)
                d_scores_p = (shares_p * (d_shares_p - inner)).astype(B16)
                found[0].append(
                    (dot_nn(d_scores, key[:, cut]) + dot_nn(d_scores_p, key_p[:, cut])) * scale
                )
                found[1].append(dot_tn(d_scores, qh))
                found[2].append(dot_tn(shares.astype(B16), dh))
                found[3].append(dot_tn(d_scores_p, qh))
                found[4].append(dot_tn(shares_p.astype(B16), dh))
            joined = [jnp.concatenate(f, 1) for f in found]
            dq_s[:, columns] = joined[0].astype(B16)
            dk_s[:, columns] = joined[1].astype(B16)
            dv_s[:, columns] = joined[2].astype(B16)
            dprefix_ref[0, :, columns] = joined[3]
            dprefix_ref[1, :, columns] = joined[4]
            return carry

        lax.fori_loop(0, half // LANES, pair, 0)
        sum_s[...] = dot_nt(dk_s[...], full[:, half : 2 * half]) + dot_nt(
            dv_s[...], full[:, 2 * half : 3 * half]
        )
        rows_s[...] = dot_nt(dq_s[...], full[:, :half])

        def add(index, carry):
            place = pl.ds(picks_ref[index], 1)
            sum_s[place, :] = sum_s[place, :] + rows_s[pl.ds(index, 1), :]
            return carry

        lax.fori_loop(0, scored, add, 0, unroll=8)
        part_ref[...] = sum_s[...].astype(B16)

    inputs = [gradient, own, other, middle, gain, q, k, v, lse, prefix, picks_column]
    return pl.pallas_call(
        body,
        grid_spec=pltpu.PrefetchScalarGridSpec(
            num_scalar_prefetch=3,
            grid=(1,),
            in_specs=[whole_spec(a.shape) for a in inputs] + weight.specs,
            out_specs=[
                whole_spec((row_count, width)),
                whole_spec((row_count, width)),
                whole_spec(prefix.shape),
            ],
            scratch_shapes=weight.scratch
            + [
                pltpu.VMEM((scored, half), B16),
                pltpu.VMEM((scored, half), B16),
                pltpu.VMEM((row_count, half), B16),
                pltpu.VMEM((row_count, half), B16),
                pltpu.VMEM((row_count, width), F32),
                pltpu.VMEM((scored, width), F32),
            ],
        ),
        out_shape=[
            shape((row_count, width), B16),
            shape((row_count, width), F32),
            shape(prefix.shape, F32),
        ],
        compiler_params=params(),
        cost_estimate=cost(24),
        name="last_attention_back",
    )(me, layout, picks, *inputs, *weight.operands)


def first_prefix_back(gradient, own, other, middle, gain, q, mixed, lse, prefix, me, weight, plen):
    row_count, width = gradient.shape
    half = q.shape[1]
    prefix_rows = prefix.shape[1]
    lanes = half // HEAD_DIM * prefix_rows
    stacks = len(weight.operands)

    def own_head(dims, lane_axis):
        lane = lax.broadcasted_iota(jnp.int32, dims, lane_axis)
        column = lax.broadcasted_iota(jnp.int32, dims, 1 - lane_axis)
        return lane // prefix_rows == column // HEAD_DIM

    def body(me_ref, grad_ref, own_ref, other_ref, middle_ref, gain_ref, q_ref, mixed_ref,
             lse_ref, prefix_ref, *refs):
        dprefix_ref, full, sems, spread_s, sum_s = refs[stacks:]
        step = pl.program_id(0)
        refs = (me_ref[0], refs[:stacks], full, sems)

        @pl.when(step == 0)
        def _():
            weight.start(*refs)
            sum_s[...] = jnp.zeros(sum_s.shape, F32)
            for c in range(2):
                tiled = jnp.concatenate([prefix_ref[c]] * (lanes // prefix_rows), 0)
                spread_s[c] = jnp.where(
                    own_head((lanes, half), 0), tiled.astype(F32), 0.0
                ).astype(B16)
            spread_s[2] = jnp.where(own_head((lanes, half), 0), 1.0, 0.0).astype(B16)

        incoming = own_ref[...].astype(F32) + other_ref[...].astype(F32)
        grad_mid = grad_ref[...] + norm_rows_back(incoming, middle_ref[...], gain_ref[...])

        @pl.when(step == 0)
        def _():
            weight.wait(*refs)

        d_mixed = dot_nn(grad_mid.astype(B16), full[...]).astype(B16)
        product = d_mixed.astype(F32) * mixed_ref[...].astype(F32)
        high = product.astype(B16)
        low = (product - high.astype(F32)).astype(B16)
        inner = dot_nt(high, spread_s[2]) + dot_nt(low, spread_s[2])
        lane = lax.broadcasted_iota(jnp.int32, (BLOCK, lanes), 1)
        shares = jnp.exp(dot_nt(q_ref[...], spread_s[0]) - lse_ref[:, :lanes])
        shares = jnp.where(lane % prefix_rows < plen, shares, 0.0)
        d_shares = dot_nt(d_mixed, spread_s[1]).astype(B16).astype(F32)
        d_scores = (shares * (d_shares - inner)).astype(B16)
        sum_s[0] += dot_tn(d_scores, q_ref[...])
        sum_s[1] += dot_tn(shares.astype(B16), d_mixed)

        @pl.when(step == row_count // BLOCK - 1)
        def _():
            for c in range(2):
                held = jnp.where(own_head((lanes, half), 0), sum_s[c], 0.0)
                total = held[:prefix_rows]
                for first in range(prefix_rows, lanes, prefix_rows):
                    total = total + held[first : first + prefix_rows]
                dprefix_ref[c] = total

    return pl.pallas_call(
        body,
        grid_spec=pltpu.PrefetchScalarGridSpec(
            num_scalar_prefetch=1,
            grid=(row_count // BLOCK,),
            in_specs=[
                rows_spec(width),
                rows_spec(width),
                rows_spec(width),
                rows_spec(width),
                whole_spec(gain.shape),
                rows_spec(half),
                rows_spec(half),
                rows_spec(LANES),
                whole_spec(prefix.shape),
                *weight.specs,
            ],
            out_specs=whole_spec(prefix.shape),
            scratch_shapes=weight.scratch
            + [pltpu.VMEM((3, lanes, half), B16), pltpu.VMEM((2, lanes, half), F32)],
        ),
        out_shape=shape(prefix.shape, F32),
        compiler_params=params(),
        cost_estimate=cost(11),
        name="first_prefix_back",
    )(me, gradient, own, other, middle, gain, q, mixed, lse, prefix, *weight.operands)


class TableRows:
    def __init__(self, ids, table):
        count = ids.shape[0]
        shard_rows = table.shape[0]
        ta_size = lax.axis_size("ta")
        shard = ids // shard_rows
        self.table = table
        self.inside = ids % shard_rows
        self.owner = shard // ta_size
        order = jnp.arange(count, dtype=jnp.int32)
        same = ids[:, None] == ids[None, :]
        first = jnp.min(jnp.where(same, order[None], count), 1)
        is_first = first == order
        earlier = is_first[None] & (shard[None] == shard[:, None]) & (order[None] < first[:, None])
        self.rank = jnp.sum(earlier.astype(jnp.int32), 1)
        self.mine = shard % ta_size == lax.axis_index("ta")
        self.need = jnp.max(jnp.where(self.mine, self.rank, 0)) // SLOT_ROWS + 1
        self.per_core = lax.axis_size("dev") * SLOT_ROWS

    def slot(self, turn):
        rank = self.rank - turn * SLOT_ROWS
        used = (rank >= 0) & (rank < SLOT_ROWS)
        slot = self.owner * SLOT_ROWS + rank + jnp.where(self.mine, 0, self.per_core)
        return jnp.where(used, slot, -1)

    def ask(self, turn):
        slots = jnp.arange(self.per_core, dtype=jnp.int32)
        found = self.slot(turn)[None] == slots[:, None]
        asked = jnp.max(jnp.where(found, self.inside[None], 0), 1).reshape(-1, SLOT_ROWS)
        header = jnp.broadcast_to(self.need, (asked.shape[0], 1))
        return lax.all_to_all(jnp.concatenate([asked, header], 1), "dev", 0, 0)

    def answer(self, wanted):
        numbers = jnp.arange(self.table.shape[0], dtype=jnp.int32)
        pick = (wanted[:, :SLOT_ROWS].reshape(-1, 1) == numbers[None]).astype(B16)
        sent = jnp.dot(pick, self.table, preferred_element_type=F32).astype(B16)
        return sent.reshape(-1, SLOT_ROWS, self.table.shape[1])

    def fetch(self, sent):
        got = lax.all_to_all(sent, "dev", 0, 0)
        return got.reshape(self.per_core, self.table.shape[1])

    def place(self, turn, got):
        slots = jnp.arange(2 * self.per_core, dtype=jnp.int32)
        spread = (self.slot(turn)[:, None] == slots[None]).astype(B16)
        both = jnp.concatenate([got, partner(got)], 0)
        return jnp.dot(spread, both, preferred_element_type=F32)

    def finish(self, base, wanted, got):
        most = jnp.max(wanted[:, SLOT_ROWS])
        most = jnp.maximum(most, partner(most.reshape(1, 1))[0, 0])

        def again(state):
            return state[0] < most

        def turn(state):
            got = self.fetch(self.answer(self.ask(state[0])))
            return (state[0] + 1, state[1] + self.place(state[0], got))

        return lax.while_loop(again, turn, (jnp.int32(1), base + self.place(0, got)))[1]


def adamw_update(weight, moment, square, gradient, corr_one, corr_two):
    moment = BETA_ONE * moment + (1.0 - BETA_ONE) * gradient
    square = BETA_TWO * square + (1.0 - BETA_TWO) * gradient * gradient
    weight = weight - LEARN_RATE * (
        moment / corr_one / (jnp.sqrt(square / corr_two) + ADAM_EPS) + DECAY_RATE * weight
    )
    return (weight, moment, square)


def local(
    token_ids,
    bucket,
    seq_lengths,
    loss_pos,
    targets,
    wte,
    wpe,
    w_qkv,
    w_out,
    w_fc,
    w_proj,
    frozen_vec,
    fc_bias,
    final_norm,
    prefix_table,
    inner_weight,
    inner_bias,
    outer_weight,
    outer_bias,
    moment_prefix,
    square_prefix,
    moment_inner,
    square_inner,
    moment_inner_bias,
    square_inner_bias,
    moment_outer,
    square_outer,
    moment_outer_bias,
    square_outer_bias,
):
    row_count = token_ids.shape[0]
    scored = loss_pos.shape[0]
    width = wte.shape[1]
    half = w_qkv.shape[3]
    size = lax.axis_size("dev")
    own_index = lax.axis_index("ta")
    plen = prefix_table.shape[0]
    prefix_rows = 16
    me = lax.axis_index("dev").astype(jnp.int32).reshape(1)
    orders = (bit_orders(size, 3), bit_orders(size, 4))
    stages = len(orders[0][0])
    bucket_width = bucket[0]
    shift = jnp.where(bucket_width == 256, 8, 10).astype(jnp.int32)
    layout = jnp.concatenate([shift.reshape(1), bucket_width.reshape(1), seq_lengths[0]])

    rounds = Rounds()
    ff = w_fc.shape[2]
    totals = (4 * half, 2 * ff)
    cuts = [[cuts_of(total, LANES, len(order)) for total in totals] for order in orders]

    def add_layer(layer_id, qkv, out, fc, proj):
        sides = (
            jnp.concatenate([qkv[c] for c in range(3)] + [out.T], 1),
            jnp.concatenate([fc, proj.T], 1),
        )
        parts = [
            [
                rows[:, c[p] : c[p + 1]]
                for rows, c in zip(sides, cuts[layer_id])
            ]
            for p in range(len(orders[layer_id]))
        ]
        rounds.add(
            layer_id,
            orders[layer_id],
            [jnp.concatenate(part, 1) for part in parts],
            [part[0].shape[1] for part in parts],
        )

    def weight(layer_id, side, first, last):
        segments = []
        for p, order in enumerate(orders[layer_id]):
            if layer_id == 0:
                stacks, skip = rounds.held[0, p], cuts[0][0][p + 1] - cuts[0][0][p]
                begin = cuts[0][side][p]
                end = cuts[0][side][p + 1]
                segments.append((stacks, order, begin, end, skip if side else 0))
            else:
                stacks = rounds.held[1, p, side]
                segments.append((stacks, order, cuts[1][side][p], cuts[1][side][p + 1], 0))
        return Gathered(segments, first, last)

    def attention_weight(layer_id, first=0):
        return weight(layer_id, 0, first * half, 4 * half)

    def mlp_weights(layer_id):
        return weight(layer_id, 1, 0, ff), weight(layer_id, 1, ff, 2 * ff)

    def head_bias(layer_id):
        part = lax.dynamic_slice_in_dim(frozen_vec[layer_id, 4:7], own_index * half, half, 1)
        return part.reshape(1, 3 * half)

    add_layer(0, w_qkv[0], w_out[0], w_fc[0], w_proj[0])
    ids, prefix_in = rounds.step(
        0,
        0,
        through=(
            (token_ids, targets),
            (prefix_table, inner_weight, inner_bias, outer_weight),
        ),
    )
    lookup = TableRows(jnp.concatenate(ids), wte)
    wanted = lookup.ask(0)
    hidden = jnp.tanh(jnp.dot(prefix_in[0], prefix_in[1], precision=HIGHEST) + prefix_in[2])
    sums = jnp.einsum("pr,rlcd->lcpd", hidden, prefix_in[3], precision=HIGHEST)

    wanted, sums, last_layer = rounds.step(
        0, 1, through=(wanted, sums, (w_qkv[1], w_out[1], w_fc[1], w_proj[1]))
    )
    sent = lookup.answer(wanted)
    for stage in range(stages):
        sums = sums + flip(sums, 1 << stage)
    prefix_kv = (sums + outer_bias[:, :, None, :]).astype(B16)
    prefix_kv = jnp.pad(prefix_kv, ((0, 0), (0, 0), (0, prefix_rows - plen), (0, 0)))
    add_layer(1, *last_layer)
    for stage in range(2, stages - 2):
        rounds.step(0, stage)

    sent, wanted, prefix_kv, next_rows = rounds.step(
        0,
        stages - 2,
        through=(sent, wanted, prefix_kv, [rounds.held[1, p][0] for p in range(len(orders[1]))]),
    )
    for part, array in enumerate(next_rows):
        rounds.held[1, part] = [array]
    got = lookup.fetch(sent)

    got, wanted, places = rounds.step(0, stages - 1, through=(got, wanted, wpe))
    repeat = row_count // 256
    places = jnp.where(bucket_width == 256, jnp.tile(places[:256], (repeat, 1)), places[:row_count])
    places = jnp.concatenate([places, jnp.zeros((scored, width), places.dtype)], 0)
    rows = lookup.finish(places.astype(F32), wanted, got)
    stream = rows[:row_count]
    target_rows = rows[row_count:].astype(B16)

    stream, target_rows = rounds.step(1, 0, through=(stream, target_rows))
    part, q0, mixed0, lse0 = first_attention(
        stream, frozen_vec[0, 0:2], head_bias(0), prefix_kv[0], layout, me, attention_weight(0), plen
    )

    part, table = rounds.step(1, 1, through=(part, wte))
    other = partner(part)
    entries = wte.shape[0]
    table_half = -(-entries // 64) * 64
    table = jnp.pad(table, ((0, table_half - entries), (0, 0)))

    part, other, table = rounds.step(1, 2, through=(part, other, table))
    vec = frozen_vec[0]
    part_two, middle0, slope0 = mlp(
        stream,
        part,
        other,
        jnp.stack([vec[7], vec[2], vec[3]]),
        fc_bias[0:1],
        me,
        *mlp_weights(0),
    )

    for stage in range(3, stages - 1):
        rounds.step(1, stage)

    table, part_two = rounds.step(1, stages - 1, 0, through=(table, part_two))
    other = partner(part_two)
    table = jnp.concatenate([table, partner(table)], 0)

    part_two, other, table = rounds.step(1, stages - 1, 1, through=(part_two, other, table))

    vec_last = frozen_vec[1]
    picks_column = loss_pos.reshape(scored, 1)
    stream1, part, k1, v1, q1, mixed1, lse1, chosen = last_attention(
        middle0,
        part_two,
        other,
        jnp.stack([vec[8], vec_last[0], vec_last[1]]),
        head_bias(1),
        prefix_kv[1],
        layout,
        loss_pos,
        picks_column,
        me,
        attention_weight(1),
        plen,
    )
    part_two, middle1, slope1 = mlp(
        chosen,
        part,
        partner(part),
        jnp.stack([vec_last[7], vec_last[2], vec_last[3]]),
        fc_bias[1:2],
        me,
        *mlp_weights(1),
    )
    both = part_two.astype(F32) + partner(part_two).astype(F32)
    head_rows = middle1 + (both + vec_last[8])
    center = head_rows - jnp.mean(head_rows, -1, keepdims=True)
    spread = jnp.mean(center * center, -1, keepdims=True)
    head_in = (center * lax.rsqrt(spread + EPS_NORM) * final_norm[0] + final_norm[1]).astype(B16)

    core_rows = scored // 2
    mine = lax.dynamic_slice_in_dim(head_in, own_index * core_rows, core_rows, 0)
    cuts_head = (0, 48, 96, core_rows)
    head_order = bit_orders(size, 3)
    head = Rounds()
    head.add(0, head_order, [mine[a:b] for a, b in zip(cuts_head[:-1], cuts_head[1:])])
    for stage in range(stages):
        head.step(0, stage)
    near, far = [
        [head.held[0, p][side].reshape(-1, width) for p in range(len(head_order))]
        for side in range(2)
    ]
    keep = vocabulary(near[:1], table, entries)
    far, keep, near = lax.optimization_barrier((far, keep, near))
    send = vocabulary(far, table, entries)
    keep = list(keep) + list(vocabulary(near[1:], table, entries))
    for stage in reversed(range(stages)):
        got = [flip(array, head_order[p][stage]) for p, array in enumerate(send)]
        keep, send = merge(keep, got, stage == 0)
    own_means = jnp.concatenate(keep, 0)
    other_means = partner(own_means)
    means = jnp.where(
        own_index == 0,
        jnp.concatenate([own_means, other_means], 0),
        jnp.concatenate([other_means, own_means], 0),
    )
    place = loss_pos % bucket_width
    slot = loss_pos // bucket_width
    lengths = jnp.sum(
        jnp.where(
            slot[:, None] == jnp.arange(seq_lengths.shape[1], dtype=jnp.int32)[None],
            seq_lengths[0][None],
            0,
        ),
        1,
    )
    counted = (place < lengths).astype(F32).reshape(scored, 1)
    count_total = float(scored * size)
    grad_rows, loss_terms = head_back(
        means, head_rows, head_in, target_rows, counted, final_norm, count_total
    )
    loss_part = jnp.sum(loss_terms[:, 0])

    (part,) = mlp_back(grad_rows, slope1, me, *mlp_weights(1))
    part, spread_grad, d_prefix1 = last_attention_back(
        grad_rows,
        part,
        partner(part),
        middle1,
        vec_last[2:3],
        q1,
        k1,
        v1,
        lse1,
        prefix_kv[1],
        layout,
        loss_pos,
        picks_column,
        me,
        attention_weight(1),
        plen,
    )
    part, grad_stream = mlp_back(
        spread_grad,
        slope0,
        me,
        *mlp_weights(0),
        (stream1, vec_last[0:1], part, partner(part)),
    )
    d_prefix0 = first_prefix_back(
        grad_stream,
        part,
        partner(part),
        middle0,
        vec[2:3],
        q0,
        mixed0,
        lse0,
        prefix_kv[0],
        me,
        attention_weight(0, 3),
        plen,
    )
    d_prefix = sum_over_dev(jnp.stack([d_prefix0, d_prefix1])[:, :, :plen])

    d_outer = jnp.einsum("pr,lcpd->rlcd", hidden, d_prefix, precision=HIGHEST)
    d_outer_bias = jnp.sum(d_prefix, 2)
    hidden_part = jnp.einsum("lcpd,rlcd->pr", d_prefix, outer_weight, precision=HIGHEST)
    outer_square = jnp.sum(d_outer * d_outer) + jnp.sum(d_outer_bias * d_outer_bias) / size
    over_ta = jnp.concatenate(
        [hidden_part, jnp.broadcast_to(outer_square, (1, hidden_part.shape[1]))], 0
    )
    over_ta = over_ta + partner(over_ta)
    d_hidden = over_ta[:plen]
    d_pre = d_hidden * (1.0 - hidden * hidden)
    d_inner = jnp.dot(prefix_table.T, d_pre, precision=HIGHEST)
    d_inner_bias = jnp.sum(d_pre, 0)
    table_part = jnp.dot(d_pre, inner_weight.T, precision=HIGHEST)
    squares = over_ta[plen, 0] + jnp.sum(d_inner * d_inner) + jnp.sum(d_inner_bias * d_inner_bias)
    lane = jnp.arange(table_part.shape[1], dtype=jnp.int32)
    last_row = jnp.where(lane == 0, squares, jnp.where(lane == 1, loss_part, 0.0))
    totals = sum_over_dev(jnp.concatenate([table_part, last_row[None]], 0))
    d_table = totals[:plen]
    square_sum = totals[plen, 0]
    loss_value = totals[plen, 1] / count_total
    grad_total = jnp.sqrt(square_sum + jnp.sum(d_table * d_table))
    factor = jnp.minimum(1.0, CLIP_NORM / (grad_total + 1e-06))
    corr_one = 1.0 - BETA_ONE**adam_steps
    corr_two = 1.0 - BETA_TWO**adam_steps
    prefix_out = adamw_update(
        prefix_table, moment_prefix, square_prefix, factor * d_table, corr_one, corr_two
    )
    inner_out = adamw_update(
        inner_weight, moment_inner, square_inner, factor * d_inner, corr_one, corr_two
    )
    ibias_out = adamw_update(
        inner_bias, moment_inner_bias, square_inner_bias, factor * d_inner_bias, corr_one, corr_two
    )
    outer_out = adamw_update(
        outer_weight, moment_outer, square_outer, factor * d_outer, corr_one, corr_two
    )
    obias_out = adamw_update(
        outer_bias, moment_outer_bias, square_outer_bias, factor * d_outer_bias, corr_one, corr_two
    )
    return (
        loss_value.reshape(1),
        grad_total.reshape(1),
        prefix_out[0],
        prefix_out[1],
        prefix_out[2],
        inner_out[0],
        inner_out[1],
        inner_out[2],
        ibias_out[0],
        ibias_out[1],
        ibias_out[2],
        outer_out[0],
        outer_out[1],
        outer_out[2],
        obias_out[0],
        obias_out[1],
        obias_out[2],
        prefix_out[0].astype(B16),
        inner_out[0].astype(B16),
        ibias_out[0].astype(B16),
        outer_out[0].astype(B16),
        obias_out[0].astype(B16),
    )


def solution(mesh):
    in_specs = (
        P("dev"),
        P("dev"),
        P("dev", None),
        P("dev"),
        P("dev"),
        P(("dev", "ta"), None),
        P(),
        P(None, None, "dev", "ta"),
        P(None, "ta", "dev"),
        P(None, "dev", "ta"),
        P(None, "ta", "dev"),
        P(),
        P(None, "ta"),
        P(),
        P(),
        P(None, "dev"),
        P("dev"),
        P("dev", None, None, "ta"),
        P(None, None, "ta"),
        P(),
        P(),
        P(None, "dev"),
        P(None, "dev"),
        P("dev"),
        P("dev"),
        P("dev", None, None, "ta"),
        P("dev", None, None, "ta"),
        P(None, None, "ta"),
        P(None, None, "ta"),
    )
    out_specs = (
        P(),
        P(),
        P(),
        P(),
        P(),
        P(None, "dev"),
        P(None, "dev"),
        P(None, "dev"),
        P("dev"),
        P("dev"),
        P("dev"),
        P("dev", None, None, "ta"),
        P("dev", None, None, "ta"),
        P("dev", None, None, "ta"),
        P(None, None, "ta"),
        P(None, None, "ta"),
        P(None, None, "ta"),
        P(),
        P(None, "dev"),
        P("dev"),
        P("dev", None, None, "ta"),
        P(None, None, "ta"),
    )
    return jax.shard_map(local, mesh=mesh, in_specs=in_specs, out_specs=out_specs, check_vma=False)
```

```python
import functools

import jax
import jax.numpy as jnp
from jax import lax
from jax.experimental import pallas as pl
from jax.experimental.pallas import tpu as pltpu
from jax.sharding import PartitionSpec as P

HEAD_DIM = 64


EPS_NORM = 1e-05
CLIP_NORM = 0.001
LEARN_RATE = 0.02
BETA_ONE = 0.9
BETA_TWO = 0.999
ADAM_EPS = 1e-08
DECAY_RATE = 0.01
adam_steps = 10.0
NEG_BIG = -1e30
HIGHEST = lax.Precision.HIGHEST
F32 = jnp.float32
B16 = jnp.bfloat16
GELU_SCALE = 0.7978845608028654
GELU_CUBE = 0.044715
SLOT_ROWS = 48
BLOCK = 256
LANES = 128
PIECE = 2048
SWAP = [(0, 1), (1, 0)]


def shape(dims, dtype):
    return jax.ShapeDtypeStruct(dims, dtype)


def params(**more):
    return pltpu.CompilerParams(dimension_semantics=("arbitrary",), **more)


def cost(microseconds):
    return pl.CostEstimate(
        flops=int(microseconds * 1.15e9), transcendentals=0, bytes_accessed=1024
    )


def flip(array, bit):
    size = lax.axis_size("dev")
    return lax.ppermute(array, "dev", [(i, i ^ bit) for i in range(size)])


def partner(array):
    return lax.ppermute(array, "ta", SWAP)


def bit_orders(size, parts):
    bits = [1 << k for k in range(size.bit_length() - 1)]
    if size == 16:
        x, y, near, far = bits
        if parts == 3:
            return ((far, y, near, x), (near, far, x, y), (far, x, y, near))
        return (
            (x, y, near, far),
            (x, y, far, near),
            (near, far, x, y),
            (far, near, y, x),
        )
    return tuple(tuple(bits[k:] + bits[:k]) for k in range(parts))


def cuts_of(total, unit, parts):
    sixths = (0, 2, 4) if parts == 3 else (0, 1, 2, 4)
    return [total * k // 6 // unit * unit for k in sixths] + [total]


def pack(groups):
    arrays = [array for group, unused, unused in groups for array in group]
    outs = []
    moves = []
    for number, (group, first, last) in enumerate(groups):
        total = 0
        for array in group:
            moves.append((number, total, array.shape[0], first, last - first))
            total += array.shape[0]
        outs.append(shape((total, group[0].shape[1], last - first), group[0].dtype))

    def body(*refs):
        sems = refs[-1]
        copies = [
            pltpu.make_async_copy(
                refs[index].at[:, :, pl.ds(first, wide)],
                refs[len(arrays) + number].at[pl.ds(begin, count)],
                sems.at[index],
            )
            for index, (number, begin, count, first, wide) in enumerate(moves)
        ]
        for copy in copies:
            copy.start()
        for copy in copies:
            copy.wait()

    return pl.pallas_call(
        body,
        in_specs=[pl.BlockSpec(memory_space=pl.ANY)] * len(arrays),
        out_specs=[pl.BlockSpec(memory_space=pltpu.VMEM)] * len(outs),
        out_shape=outs,
        scratch_shapes=[pltpu.SemaphoreType.DMA((len(arrays),))],
        cost_estimate=cost(2),
        name="pack",
    )(*arrays)


class Rounds:
    def __init__(self):
        self.orders = {}
        self.held = {}
        self.split = {}
        self.before = []

    def add(self, chunk, orders, arrays, splits=None):
        self.orders[chunk] = orders
        for part, array in enumerate(arrays):
            self.held[chunk, part] = [array[None]]
            self.split[chunk, part] = splits[part] if splits else None

    def step(self, chunk, stage, side=None, through=()):
        parts = range(len(self.orders[chunk]))
        held = [self.held[chunk, part] for part in parts]
        if stage == 0:
            sends = [arrays[0] for arrays in held]
        else:
            spans = []
            for part, arrays in zip(parts, held):
                cut, width = self.split[chunk, part], arrays[0].shape[2]
                spans.append((cut if side == 1 else 0, cut if side == 0 else width))
            sends = pack([(arrays, *span) for arrays, span in zip(held, spans)])
        through, sends, unused = lax.optimization_barrier((through, sends, self.before))
        self.before = []
        for part, send in enumerate(sends):
            got = flip(send, self.orders[chunk][part][stage])
            self.held[(chunk, part) if side is None else (chunk, part, side)] = [send, got]
            self.before.append(got)
        return through


def sum_over_dev(array):
    size = lax.axis_size("dev")
    bit = 1
    while bit < size:
        if bit * 2 < size:
            near, far, both = flip(array, bit), flip(array, bit * 2), flip(array, bit * 3)
            array = (array + near) + (far + both)
        else:
            array = array + flip(array, bit)
        bit = bit * 4
    return array


def norm_rows(x):
    center = x - jnp.mean(x, -1, keepdims=True)
    scale = lax.rsqrt(jnp.mean(center * center, -1, keepdims=True) + EPS_NORM)
    return center * scale, scale


def norm_rows_back(gradient, x, gain):
    xhat, scale = norm_rows(x)
    e2 = gradient * gain
    mean_one = jnp.mean(e2, -1, keepdims=True)
    mean_two = jnp.mean(e2 * xhat, -1, keepdims=True)
    return (e2 - mean_one - xhat * mean_two) * scale


def dot_nn(a, b):
    return lax.dot_general(a, b, (((1,), (0,)), ((), ())), preferred_element_type=F32)


def dot_nt(a, b):
    return lax.dot_general(a, b, (((1,), (1,)), ((), ())), preferred_element_type=F32)


def dot_tn(a, b):
    return lax.dot_general(a, b, (((0,), (0,)), ((), ())), preferred_element_type=F32)


class Gathered:
    def __init__(self, segments, first, last):
        self.pieces = []
        for stacks, order, begin in segments:
            low, high = max(first, begin), min(last, begin + stacks[0].shape[2])
            if low < high:
                self.pieces.append((stacks, order, low - begin, high - low, low - first))
        stacks, order, *unused = self.pieces[0]
        self.rows = stacks[0].shape[1]
        self.blocks = 1 << len(order)
        self.scratch = [
            pltpu.VMEM((self.blocks * self.rows, last - first), B16),
            pltpu.SemaphoreType.DMA((len(self.pieces) * self.blocks,)),
        ]
        self.operands = [array for piece in self.pieces for array in piece[0]]
        self.specs = [pl.BlockSpec(memory_space=pl.ANY)] * len(self.operands)

    def each(self, act, me, refs, full, sems):
        for number, (stacks, order, source, wide, target) in enumerate(self.pieces):
            blocks = self.blocks // len(stacks)
            for side, ref in enumerate(refs[number * len(stacks) : (number + 1) * len(stacks)]):

                def one(index, carry, side=side, ref=ref):
                    place = me ^ (order[-1] if side else 0)
                    for k, bit in enumerate(order[:-1]):
                        place = place ^ jnp.where((index >> k) % 2 == 1, bit, 0)
                    start = pl.multiple_of(place * self.rows, self.rows)
                    copy = pltpu.make_async_copy(
                        ref.at[index, :, pl.ds(source, wide)],
                        full.at[pl.ds(start, self.rows), pl.ds(target, wide)],
                        sems.at[number * self.blocks + side * blocks + index],
                    )
                    act(copy)
                    return carry

                lax.fori_loop(0, blocks, one, 0)

    def start(self, *refs):
        self.each(lambda copy: copy.start(), *refs)

    def wait(self, *refs):
        self.each(lambda copy: copy.wait(), *refs)


def rows_spec(width, block=BLOCK):
    return pl.BlockSpec((block, width), lambda i, *refs: (i, 0))


def whole_spec(dims):
    return pl.BlockSpec(dims, lambda i, *refs: (0,) * len(dims))


def key_bias(layout_ref, query_pos, key_count):
    shift = layout_ref[0]
    dims = (query_pos.shape[0], key_count)
    key_pos = lax.broadcasted_iota(jnp.int32, (1, key_count), 1)
    key_seg = lax.shift_right_logical(key_pos, jnp.full((1, key_count), shift, jnp.int32))
    query_seg = lax.shift_right_logical(query_pos, jnp.full(query_pos.shape, shift, jnp.int32))
    length = jnp.zeros((1, key_count), jnp.int32)
    for slot in range(layout_ref.shape[0] - 2):
        length = jnp.where(key_seg == slot, layout_ref[2 + slot], length)
    place = key_pos - key_seg * layout_ref[1]
    key_seg = jnp.where(place < length, key_seg, -1)
    seen = (jnp.broadcast_to(query_seg, dims) == jnp.broadcast_to(key_seg, dims)) & (
        jnp.broadcast_to(key_pos, dims) <= jnp.broadcast_to(query_pos, dims)
    )
    return jnp.where(seen, 0.0, NEG_BIG)


def prefix_bias(rows, prefix_rows, prefix_len):
    lane = lax.broadcasted_iota(jnp.int32, (rows, prefix_rows), 1)
    return jnp.where(lane < prefix_len, 0.0, NEG_BIG)


def attend(query, key, value, key_prefix, value_prefix, bias, bias_prefix):
    scores = dot_nt(query, key) + bias
    scores_prefix = dot_nt(query, key_prefix) + bias_prefix
    highest = jnp.maximum(
        jnp.max(scores, -1, keepdims=True), jnp.max(scores_prefix, -1, keepdims=True)
    )
    shares = jnp.exp(scores - highest)
    shares_prefix = jnp.exp(scores_prefix - highest)
    total = jnp.sum(shares, -1, keepdims=True) + jnp.sum(shares_prefix, -1, keepdims=True)
    mixed = dot_nn(shares.astype(B16), value) + dot_nn(shares_prefix.astype(B16), value_prefix)
    return mixed / total, highest + jnp.log(total)


def attend_pairs(q_ref, k_ref, v_ref, prefix_ref, mixed_ref, lse_ref, rows, key_count, bias, plen):
    prefix_rows = prefix_ref.shape[1]
    bias_prefix = prefix_bias(BLOCK, prefix_rows, plen)
    lse_ref[rows, :] = jnp.zeros((BLOCK, LANES), F32)
    lane = lax.broadcasted_iota(jnp.int32, (BLOCK, LANES), 1)

    def pair(index, carry):
        columns = pl.ds(pl.multiple_of(index * LANES, LANES), LANES)
        query = q_ref[rows, columns]
        key = k_ref[pl.ds(0, key_count), columns]
        value = v_ref[pl.ds(0, key_count), columns]
        key_prefix = prefix_ref[0, :, columns]
        value_prefix = prefix_ref[1, :, columns]
        parts = []
        for side in range(2):
            cut = slice(side * HEAD_DIM, (side + 1) * HEAD_DIM)
            mixed, lse = attend(
                query[:, cut],
                key[:, cut],
                value[:, cut],
                key_prefix[:, cut],
                value_prefix[:, cut],
                bias,
                bias_prefix,
            )
            parts.append(mixed)
            lse_ref[rows, :] = jnp.where(
                lane // prefix_rows == 2 * index + side, lse, lse_ref[rows, :]
            )
        mixed_ref[rows, columns] = jnp.concatenate(parts, 1).astype(B16)
        return carry

    lax.fori_loop(0, q_ref.shape[1] // LANES, pair, 0)


def first_attention(stream, row_count, vectors, bias_qkv, prefix, layout, me, weight, plen):
    width = stream.shape[1]
    half = prefix.shape[2]
    scale = HEAD_DIM ** (-0.5)

    stacks = len(weight.operands)

    def body(me_ref, layout_ref, stream_ref, vec_ref, bias_ref, prefix_ref, *refs):
        part_ref, q_out, mixed_out, lse_out, full, sems, q_s, k_s, v_s = refs[stacks:]
        step = pl.program_id(0)
        refs = (me_ref[0], refs[:stacks], full, sems)

        @pl.when(step == 0)
        def _():
            weight.start(*refs)
            weight.wait(*refs)

        xhat, unused = norm_rows(stream_ref[...])
        normed = (xhat * vec_ref[0:1, :] + vec_ref[1:2, :]).astype(B16)
        qkv = dot_nn(normed, full[:, : 3 * half]) + bias_ref[...]
        rows = pl.ds(pl.multiple_of(step * BLOCK, BLOCK), BLOCK)
        q_s[...] = (qkv[:, :half].astype(B16) * scale).astype(B16)
        k_s[rows, :] = qkv[:, half : 2 * half].astype(B16)
        v_s[rows, :] = qkv[:, 2 * half :].astype(B16)
        q_out[...] = q_s[...]
        local_pos = lax.broadcasted_iota(jnp.int32, (BLOCK, 1), 0)
        for case in range(row_count // BLOCK):

            @pl.when(step == case)
            def _(case=case):
                key_count = (case + 1) * BLOCK
                bias = key_bias(layout_ref, local_pos + case * BLOCK, key_count)
                attend_pairs(
                    q_s, k_s, v_s, prefix_ref, mixed_out, lse_out,
                    pl.ds(0, BLOCK), key_count, bias, plen,
                )

        part_ref[...] = dot_nt(mixed_out[...], full[:, 3 * half :]).astype(B16)

    return pl.pallas_call(
        body,
        grid_spec=pltpu.PrefetchScalarGridSpec(
            num_scalar_prefetch=2,
            grid=(row_count // BLOCK,),
            in_specs=[
                rows_spec(width),
                whole_spec(vectors.shape),
                whole_spec(bias_qkv.shape),
                whole_spec(prefix.shape),
                *weight.specs,
            ],
            out_specs=[rows_spec(width), rows_spec(half), rows_spec(half), rows_spec(LANES)],
            scratch_shapes=weight.scratch
            + [pltpu.VMEM((BLOCK, half), B16)]
            + [pltpu.VMEM((row_count, half), B16)] * 2,
        ),
        out_shape=[
            shape((row_count, width), B16),
            shape((row_count, half), B16),
            shape((row_count, half), B16),
            shape((row_count, LANES), F32),
        ],
        compiler_params=params(),
        cost_estimate=cost(30 * row_count // 1024),
        name="first_attention",
    )(me, layout, stream, vectors, bias_qkv, prefix, *weight.operands)


def mlp(base, own, other, vectors, bias_up, me, w_up, w_down):
    row_count, width = own.shape
    hidden = bias_up.shape[1]

    ups, downs = len(w_up.operands), len(w_down.operands)

    def body(me_ref, base_ref, own_ref, other_ref, vec_ref, bias_ref, *refs):
        part_ref, middle_ref, slope_ref, up, up_sems, down, down_sems = refs[ups + downs :]
        step = pl.program_id(0)
        up_refs = (me_ref[0], refs[:ups], up, up_sems)
        down_refs = (me_ref[0], refs[ups : ups + downs], down, down_sems)

        @pl.when(step == 0)
        def _():
            w_up.start(*up_refs)
            w_down.start(*down_refs)

        middle = base_ref[...] + (
            (own_ref[...].astype(F32) + other_ref[...].astype(F32)) + vec_ref[0:1, :]
        )
        middle_ref[...] = middle
        xhat, unused = norm_rows(middle)
        normed = (xhat * vec_ref[1:2, :] + vec_ref[2:3, :]).astype(B16)

        @pl.when(step == 0)
        def _():
            w_up.wait(*up_refs)

        total = None
        for first in range(0, hidden, PIECE):
            piece = slice(first, first + PIECE)
            u = dot_nn(normed, up[:, piece]) + bias_ref[:, piece]
            square = u * u
            t = jnp.tanh(GELU_SCALE * u * (1.0 + GELU_CUBE * square))
            half_one = 0.5 + 0.5 * t
            active = (u * half_one).astype(B16)
            bend = (0.5 * GELU_SCALE) * u * (1.0 - t * t) * (1.0 + 3 * GELU_CUBE * square)
            slope_ref[:, piece] = (half_one + bend).astype(B16)
            if first == 0:

                @pl.when(step == 0)
                def _():
                    w_down.wait(*down_refs)

            product = dot_nt(active, down[:, piece])
            total = product if total is None else total + product
        part_ref[...] = total.astype(B16)

    return pl.pallas_call(
        body,
        grid_spec=pltpu.PrefetchScalarGridSpec(
            num_scalar_prefetch=1,
            grid=(row_count // BLOCK,),
            in_specs=[
                rows_spec(width),
                rows_spec(width),
                rows_spec(width),
                whole_spec(vectors.shape),
                whole_spec(bias_up.shape),
                *w_up.specs,
                *w_down.specs,
            ],
            out_specs=[rows_spec(width), rows_spec(width), rows_spec(hidden)],
            scratch_shapes=w_up.scratch + w_down.scratch,
        ),
        out_shape=[
            shape((row_count, width), B16),
            shape((row_count, width), F32),
            shape((row_count, hidden), B16),
        ],
        compiler_params=params(),
        cost_estimate=cost(23 * row_count // 1024),
        name="mlp",
    )(me, base, own, other, vectors, bias_up, *w_up.operands, *w_down.operands)


def last_attention(base, own, other, vectors, bias_qkv, prefix, layout, picks, picks_column, me,
                   weight, plen):
    row_count, width = base.shape
    half = prefix.shape[2]
    scored = picks.shape[0]
    steps = row_count // BLOCK
    scale = HEAD_DIM ** (-0.5)

    stacks = len(weight.operands)

    def body(me_ref, layout_ref, picks_ref, base_ref, own_ref, other_ref, vec_ref, bias_ref,
             prefix_ref, column_ref, *refs):
        (stream_out, part_ref, k_out, v_out, q_out, mixed_out, lse_out, chosen_out,
         full, sems, stream_s, k_s, v_s) = refs[stacks:]
        step = pl.program_id(0)
        refs = (me_ref[0], refs[:stacks], full, sems)

        @pl.when(step == 0)
        def _():
            weight.start(*refs)
            weight.wait(*refs)

        stream = base_ref[...] + (
            (own_ref[...].astype(F32) + other_ref[...].astype(F32)) + vec_ref[0:1, :]
        )
        stream_out[...] = stream
        rows = pl.ds(pl.multiple_of(step * BLOCK, BLOCK), BLOCK)
        stream_s[rows, :] = stream
        xhat, unused = norm_rows(stream)
        normed = (xhat * vec_ref[1:2, :] + vec_ref[2:3, :]).astype(B16)
        keys_values = (
            dot_nn(normed, full[:, half : 3 * half]) + bias_ref[:, half : 3 * half]
        ).astype(B16)
        k_out[...] = keys_values[:, :half]
        v_out[...] = keys_values[:, half:]
        k_s[rows, :] = keys_values[:, :half]
        v_s[rows, :] = keys_values[:, half:]

        @pl.when(step == steps - 1)
        def _():
            def pick(index, carry):
                chosen_out[pl.ds(index, 1), :] = stream_s[pl.ds(picks_ref[index], 1), :]
                return carry

            lax.fori_loop(0, scored, pick, 0, unroll=8)
            for first in range(0, scored, BLOCK):
                block = pl.ds(first, BLOCK)
                chosen_hat, unused = norm_rows(chosen_out[block, :])
                chosen = (chosen_hat * vec_ref[1:2, :] + vec_ref[2:3, :]).astype(B16)
                query = (dot_nn(chosen, full[:, :half]) + bias_ref[:, :half]).astype(B16)
                q_out[block, :] = (query * scale).astype(B16)
                bias = key_bias(layout_ref, column_ref[block, :], row_count)
                attend_pairs(
                    q_out, k_s, v_s, prefix_ref, mixed_out, lse_out, block, row_count, bias, plen
                )
                part_ref[block, :] = dot_nt(mixed_out[block, :], full[:, 3 * half :]).astype(B16)

    return pl.pallas_call(
        body,
        grid_spec=pltpu.PrefetchScalarGridSpec(
            num_scalar_prefetch=3,
            grid=(steps,),
            in_specs=[
                rows_spec(width),
                rows_spec(width),
                rows_spec(width),
                whole_spec(vectors.shape),
                whole_spec(bias_qkv.shape),
                whole_spec(prefix.shape),
                whole_spec(picks_column.shape),
                *weight.specs,
            ],
            out_specs=[
                rows_spec(width),
                whole_spec((scored, width)),
                rows_spec(half),
                rows_spec(half),
                whole_spec((scored, half)),
                whole_spec((scored, half)),
                whole_spec((scored, LANES)),
                whole_spec((scored, width)),
            ],
            scratch_shapes=weight.scratch
            + [pltpu.VMEM((row_count, width), F32)]
            + [pltpu.VMEM((row_count, half), B16)] * 2,
        ),
        out_shape=[
            shape((row_count, width), F32),
            shape((scored, width), B16),
            shape((row_count, half), B16),
            shape((row_count, half), B16),
            shape((scored, half), B16),
            shape((scored, half), B16),
            shape((scored, LANES), F32),
            shape((scored, width), F32),
        ],
        compiler_params=params(),
        cost_estimate=cost(22),
        name="last_attention",
    )(me, layout, picks, base, own, other, vectors, bias_qkv, prefix, picks_column, *weight.operands)


def split_lse(lse, rows):
    high = lse.astype(B16).astype(F32)
    middle = (lse - high).astype(B16).astype(F32)
    low = (lse - high) - middle
    lane = lax.broadcasted_iota(jnp.int32, (rows, LANES), 1)
    packed = jnp.where(lane == 0, high, jnp.where(lane == 1, middle, jnp.where(lane == 2, low, 0.0)))
    return packed.astype(B16)


VMEM = pl.BlockSpec(memory_space=pltpu.VMEM)


def vocabulary(stacks, table, entries):
    width = table.shape[1]
    padded = table.shape[0]
    half = padded // 2
    ends = [0]
    for stack in stacks:
        ends.append(ends[-1] + stack.shape[0])
    block = max(b for b in range(16, 400, 16) if ends[-1] % b == 0)

    def body(*refs):
        table_ref = refs[len(stacks)]
        outs = refs[len(stacks) + 1 : -2]
        rows_s, mean_s = refs[-2:]
        for ref, first, last in zip(refs, ends[:-1], ends[1:]):
            rows_s[first:last, :] = ref[...]

        def turn(index, carry):
            rows = pl.ds(pl.multiple_of(index * block, block), block)
            logits = dot_nt(rows_s[rows, :], table_ref[...])
            pieces = []
            for first in range(0, padded, LANES):
                piece = logits[:, first : first + LANES]
                if any(c % half >= entries for c in range(first, first + LANES)):
                    lane = lax.broadcasted_iota(jnp.int32, piece.shape, 1) + first
                    piece = jnp.where(lane % half < entries, piece, NEG_BIG)
                pieces.append(piece)
            logits = jnp.concatenate(pieces, 1)
            highest = jnp.max(logits, -1, keepdims=True)
            shares = jnp.exp(logits - highest)
            total = jnp.sum(shares, -1, keepdims=True)
            mean = dot_nn(shares.astype(B16), table_ref[...]) / total
            mean_s[rows, :width] = mean.astype(B16)
            mean_s[rows, width:] = split_lse(highest + jnp.log(total), block)
            return carry

        lax.fori_loop(0, ends[-1] // block, turn, 0)
        for out, first, last in zip(outs, ends[:-1], ends[1:]):
            out[...] = mean_s[first:last, :]

    return pl.pallas_call(
        body,
        in_specs=[VMEM] * (len(stacks) + 1),
        out_specs=[VMEM] * len(stacks),
        out_shape=[shape((stack.shape[0], width + LANES), B16) for stack in stacks],
        scratch_shapes=[
            pltpu.VMEM((ends[-1], width), B16),
            pltpu.VMEM((ends[-1], width + LANES), B16),
        ],
        cost_estimate=cost(10 * ends[-1] // 384),
        name="vocabulary",
    )(*stacks, table)


def joined_lse(block, width):
    return jnp.sum(block[:, width:].astype(F32)[:, 0:4], -1, keepdims=True)


def merge(firsts, seconds, last):
    wide = firsts[0].shape[1]
    width = wide - LANES
    count = len(firsts)
    pieces = 1 if last else 2

    def body(*refs):
        outs = refs[2 * count :]
        for part in range(count):
            first_ref, second_ref = refs[part], refs[count + part]
            rows = first_ref.shape[0] // pieces
            for piece in range(pieces):
                one = first_ref[piece * rows : (piece + 1) * rows, :]
                two = second_ref[piece * rows : (piece + 1) * rows, :]
                lse_one, lse_two = joined_lse(one, width), joined_lse(two, width)
                highest = jnp.maximum(lse_one, lse_two)
                scale_one, scale_two = jnp.exp(lse_one - highest), jnp.exp(lse_two - highest)
                total = scale_one + scale_two
                mean = one[:, :width].astype(F32) * (scale_one / total)
                mean = mean + two[:, :width].astype(F32) * (scale_two / total)
                out_ref = outs[piece * count + part]
                out_ref[:, :width] = mean.astype(B16)
                out_ref[:, width:] = split_lse(highest + jnp.log(total), rows)

    outs = pl.pallas_call(
        body,
        in_specs=[VMEM] * (2 * count),
        out_specs=[VMEM] * (pieces * count),
        out_shape=[shape((a.shape[0] // pieces, wide), B16) for a in firsts] * pieces,
        cost_estimate=cost(3),
        name="merge",
    )(*firsts, *seconds)
    return outs[:count], outs[count:]


def head_back(means, head_rows, head_in, rows, skip, counted, final_norm, count_total):
    scored, width = head_rows.shape

    def body(mean_ref, rows_ref, in_ref, target_ref, counted_ref, norm_ref, grad_ref, loss_ref):
        lse = joined_lse(mean_ref[...], width)
        target = target_ref[...]
        logit = jnp.sum(in_ref[...].astype(F32) * target, -1, keepdims=True)
        seen = counted_ref[...]
        loss_ref[...] = jnp.broadcast_to((lse - logit) * seen, (BLOCK, LANES))
        d_head = (mean_ref[:, :width].astype(F32) - target) * (seen / count_total)
        grad_ref[...] = norm_rows_back(d_head, rows_ref[...], norm_ref[0:1, :])

    return pl.pallas_call(
        body,
        grid=(scored // BLOCK,),
        in_specs=[
            rows_spec(width + LANES),
            rows_spec(width),
            rows_spec(width),
            pl.BlockSpec((BLOCK, width), lambda i: (i + skip // BLOCK, 0)),
            rows_spec(1),
            whole_spec(final_norm.shape),
        ],
        out_specs=[rows_spec(width), rows_spec(LANES)],
        out_shape=[shape((scored, width), F32), shape((scored, LANES), F32)],
        compiler_params=params(),
        cost_estimate=cost(4),
        name="head_back",
    )(means, head_rows, head_in, rows, counted, final_norm)


def mlp_back(gradient, slope, me, w_up, w_down, residual=None):
    row_count, width = gradient.shape
    hidden = slope.shape[1]
    extra = [] if residual is None else list(residual)
    ups, downs = len(w_up.operands), len(w_down.operands)

    def body(me_ref, *refs):
        grad_ref, slope_ref = refs[0], refs[1]
        extra_refs = refs[2 : 2 + len(extra)]
        refs = refs[2 + len(extra) :]
        part_ref, *rest = refs[ups + downs :]
        up, up_sems, down, down_sems = rest[-4:]
        step = pl.program_id(0)
        up_refs = (me_ref[0], refs[:ups], up, up_sems)
        down_refs = (me_ref[0], refs[ups : ups + downs], down, down_sems)

        @pl.when(step == 0)
        def _():
            w_down.start(*down_refs)
            w_up.start(*up_refs)

        grad = grad_ref[...]
        if extra:
            stream_ref, gain_ref, own_ref, other_ref = extra_refs
            incoming = own_ref[...].astype(F32) + other_ref[...].astype(F32)
            grad = grad + norm_rows_back(incoming, stream_ref[...], gain_ref[...])
            rest[0][...] = grad

        @pl.when(step == 0)
        def _():
            w_down.wait(*down_refs)

        low = grad.astype(B16)
        total = None
        for first in range(0, hidden, PIECE):
            piece = slice(first, first + PIECE)
            d_active = dot_nn(low, down[:, piece])
            d_upward = (d_active * slope_ref[:, piece].astype(F32)).astype(B16)
            if first == 0:

                @pl.when(step == 0)
                def _():
                    w_up.wait(*up_refs)

            product = dot_nt(d_upward, up[:, piece])
            total = product if total is None else total + product
        part_ref[...] = total.astype(B16)

    extra_specs = (
        [rows_spec(width), whole_spec(extra[1].shape), rows_spec(width), rows_spec(width)]
        if extra
        else []
    )
    return pl.pallas_call(
        body,
        grid_spec=pltpu.PrefetchScalarGridSpec(
            num_scalar_prefetch=1,
            grid=(row_count // BLOCK,),
            in_specs=[rows_spec(width), rows_spec(hidden)] + extra_specs + w_up.specs + w_down.specs,
            out_specs=[rows_spec(width)] * (2 if extra else 1),
            scratch_shapes=w_up.scratch + w_down.scratch,
        ),
        out_shape=[shape((row_count, width), B16)]
        + ([shape((row_count, width), F32)] if extra else []),
        compiler_params=params(),
        cost_estimate=cost(20 * row_count // 1024),
        name="mlp_back",
    )(me, gradient, slope, *extra, *w_up.operands, *w_down.operands)


def last_attention_back(gradient, own, other, middle, gain, q, k, v, lse, prefix, layout, picks,
                        picks_column, me, weight, plen):
    scored, width = gradient.shape
    row_count, half = k.shape
    prefix_rows = prefix.shape[1]
    scale = HEAD_DIM ** (-0.5)

    stacks = len(weight.operands)

    def body(me_ref, layout_ref, picks_ref, grad_ref, own_ref, other_ref, middle_ref, gain_ref,
             q_ref, k_ref, v_ref, lse_ref, prefix_ref, column_ref, *refs):
        (part_ref, spread_ref, dprefix_ref, full, sems,
         dmix_s, dq_s, dk_s, dv_s, sum_s, rows_s) = refs[stacks:]
        refs = (me_ref[0], refs[:stacks], full, sems)
        weight.start(*refs)
        incoming = own_ref[...].astype(F32) + other_ref[...].astype(F32)
        grad_mid = grad_ref[...] + norm_rows_back(incoming, middle_ref[...], gain_ref[...])
        rows_s[...] = grad_mid
        spread_ref[...] = jnp.zeros((row_count, width), F32)

        def put(index, carry):
            spread_ref[pl.ds(picks_ref[index], 1), :] = rows_s[pl.ds(index, 1), :]
            return carry

        lax.fori_loop(0, scored, put, 0, unroll=8)
        weight.wait(*refs)
        dmix_s[...] = dot_nn(grad_mid.astype(B16), full[:, 3 * half :]).astype(B16)
        bias = key_bias(layout_ref, column_ref[...], row_count)
        bias_prefix = prefix_bias(scored, prefix_rows, plen)
        lane = lax.broadcasted_iota(jnp.int32, (scored, LANES), 1)

        def pair(index, carry):
            columns = pl.ds(pl.multiple_of(index * LANES, LANES), LANES)
            query, key, value = q_ref[:, columns], k_ref[:, columns], v_ref[:, columns]
            d_mixed = dmix_s[:, columns]
            key_p, value_p = prefix_ref[0, :, columns], prefix_ref[1, :, columns]
            found = [[], [], [], [], []]
            for side in range(2):
                cut = slice(side * HEAD_DIM, (side + 1) * HEAD_DIM)
                log_total = jnp.sum(
                    jnp.where(lane == prefix_rows * (2 * index + side), lse_ref[...], 0.0),
                    -1,
                    keepdims=True,
                )
                qh, dh = query[:, cut], d_mixed[:, cut]
                shares = jnp.exp(dot_nt(qh, key[:, cut]) + bias - log_total)
                shares_p = jnp.exp(dot_nt(qh, key_p[:, cut]) + bias_prefix - log_total)
                d_shares = dot_nt(dh, value[:, cut]).astype(B16).astype(F32)
                d_shares_p = dot_nt(dh, value_p[:, cut]).astype(B16).astype(F32)
                inner = jnp.sum(shares * d_shares, -1, keepdims=True) + jnp.sum(
                    shares_p * d_shares_p, -1, keepdims=True
                )
                d_scores = (shares * (d_shares - inner)).astype(B16)
                d_scores_p = (shares_p * (d_shares_p - inner)).astype(B16)
                found[0].append(
                    (dot_nn(d_scores, key[:, cut]) + dot_nn(d_scores_p, key_p[:, cut])) * scale
                )
                found[1].append(dot_tn(d_scores, qh))
                found[2].append(dot_tn(shares.astype(B16), dh))
                found[3].append(dot_tn(d_scores_p, qh))
                found[4].append(dot_tn(shares_p.astype(B16), dh))
            joined = [jnp.concatenate(f, 1) for f in found]
            dq_s[:, columns] = joined[0].astype(B16)
            dk_s[:, columns] = joined[1].astype(B16)
            dv_s[:, columns] = joined[2].astype(B16)
            dprefix_ref[0, :, columns] = joined[3]
            dprefix_ref[1, :, columns] = joined[4]
            return carry

        lax.fori_loop(0, half // LANES, pair, 0)
        sum_s[...] = dot_nt(dk_s[...], full[:, half : 2 * half]) + dot_nt(
            dv_s[...], full[:, 2 * half : 3 * half]
        )
        rows_s[...] = dot_nt(dq_s[...], full[:, :half])

        def add(index, carry):
            place = pl.ds(picks_ref[index], 1)
            sum_s[place, :] = sum_s[place, :] + rows_s[pl.ds(index, 1), :]
            return carry

        lax.fori_loop(0, scored, add, 0, unroll=8)
        part_ref[...] = sum_s[...].astype(B16)

    inputs = [gradient, own, other, middle, gain, q, k, v, lse, prefix, picks_column]
    return pl.pallas_call(
        body,
        grid_spec=pltpu.PrefetchScalarGridSpec(
            num_scalar_prefetch=3,
            grid=(1,),
            in_specs=[whole_spec(a.shape) for a in inputs] + weight.specs,
            out_specs=[
                whole_spec((row_count, width)),
                whole_spec((row_count, width)),
                whole_spec(prefix.shape),
            ],
            scratch_shapes=weight.scratch
            + [
                pltpu.VMEM((scored, half), B16),
                pltpu.VMEM((scored, half), B16),
                pltpu.VMEM((row_count, half), B16),
                pltpu.VMEM((row_count, half), B16),
                pltpu.VMEM((row_count, width), F32),
                pltpu.VMEM((scored, width), F32),
            ],
        ),
        out_shape=[
            shape((row_count, width), B16),
            shape((row_count, width), F32),
            shape(prefix.shape, F32),
        ],
        compiler_params=params(),
        cost_estimate=cost(24),
        name="last_attention_back",
    )(me, layout, picks, *inputs, *weight.operands)


def first_prefix_back(gradient, own, other, middle, gain, q, mixed, lse, prefix, me, weight, plen):
    row_count, width = gradient.shape
    half = q.shape[1]
    prefix_rows = prefix.shape[1]
    lanes = half // HEAD_DIM * prefix_rows
    stacks = len(weight.operands)

    def own_head(dims, lane_axis):
        lane = lax.broadcasted_iota(jnp.int32, dims, lane_axis)
        column = lax.broadcasted_iota(jnp.int32, dims, 1 - lane_axis)
        return lane // prefix_rows == column // HEAD_DIM

    def body(me_ref, grad_ref, own_ref, other_ref, middle_ref, gain_ref, q_ref, mixed_ref,
             lse_ref, prefix_ref, *refs):
        dprefix_ref, full, sems, spread_s, sum_s = refs[stacks:]
        step = pl.program_id(0)
        refs = (me_ref[0], refs[:stacks], full, sems)

        @pl.when(step == 0)
        def _():
            weight.start(*refs)
            sum_s[...] = jnp.zeros(sum_s.shape, F32)
            for c in range(2):
                tiled = jnp.concatenate([prefix_ref[c]] * (lanes // prefix_rows), 0)
                spread_s[c] = jnp.where(
                    own_head((lanes, half), 0), tiled.astype(F32), 0.0
                ).astype(B16)
            spread_s[2] = jnp.where(own_head((lanes, half), 0), 1.0, 0.0).astype(B16)

        incoming = own_ref[...].astype(F32) + other_ref[...].astype(F32)
        grad_mid = grad_ref[...] + norm_rows_back(incoming, middle_ref[...], gain_ref[...])

        @pl.when(step == 0)
        def _():
            weight.wait(*refs)

        d_mixed = dot_nn(grad_mid.astype(B16), full[...]).astype(B16)
        product = d_mixed.astype(F32) * mixed_ref[...].astype(F32)
        high = product.astype(B16)
        low = (product - high.astype(F32)).astype(B16)
        inner = dot_nt(high, spread_s[2]) + dot_nt(low, spread_s[2])
        lane = lax.broadcasted_iota(jnp.int32, (BLOCK, lanes), 1)
        shares = jnp.exp(dot_nt(q_ref[...], spread_s[0]) - lse_ref[:, :lanes])
        shares = jnp.where(lane % prefix_rows < plen, shares, 0.0)
        d_shares = dot_nt(d_mixed, spread_s[1]).astype(B16).astype(F32)
        d_scores = (shares * (d_shares - inner)).astype(B16)
        sum_s[0] += dot_tn(d_scores, q_ref[...])
        sum_s[1] += dot_tn(shares.astype(B16), d_mixed)

        @pl.when(step == row_count // BLOCK - 1)
        def _():
            for c in range(2):
                held = jnp.where(own_head((lanes, half), 0), sum_s[c], 0.0)
                total = held[:prefix_rows]
                for first in range(prefix_rows, lanes, prefix_rows):
                    total = total + held[first : first + prefix_rows]
                dprefix_ref[c] = total

    return pl.pallas_call(
        body,
        grid_spec=pltpu.PrefetchScalarGridSpec(
            num_scalar_prefetch=1,
            grid=(row_count // BLOCK,),
            in_specs=[
                rows_spec(width),
                rows_spec(width),
                rows_spec(width),
                rows_spec(width),
                whole_spec(gain.shape),
                rows_spec(half),
                rows_spec(half),
                rows_spec(LANES),
                whole_spec(prefix.shape),
                *weight.specs,
            ],
            out_specs=whole_spec(prefix.shape),
            scratch_shapes=weight.scratch
            + [pltpu.VMEM((3, lanes, half), B16), pltpu.VMEM((2, lanes, half), F32)],
        ),
        out_shape=shape(prefix.shape, F32),
        compiler_params=params(),
        cost_estimate=cost(11),
        name="first_prefix_back",
    )(me, gradient, own, other, middle, gain, q, mixed, lse, prefix, *weight.operands)


class TableRows:
    def __init__(self, ids, table):
        count = ids.shape[0]
        shard_rows = table.shape[0]
        ta_size = lax.axis_size("ta")
        shard = ids // shard_rows
        self.table = table
        self.inside = ids % shard_rows
        self.owner = shard // ta_size
        order = jnp.arange(count, dtype=jnp.int32)
        same = ids[:, None] == ids[None, :]
        first = jnp.min(jnp.where(same, order[None], count), 1)
        is_first = first == order
        earlier = is_first[None] & (shard[None] == shard[:, None]) & (order[None] < first[:, None])
        self.rank = jnp.sum(earlier.astype(jnp.int32), 1)
        self.mine = shard % ta_size == lax.axis_index("ta")
        self.need = jnp.max(jnp.where(self.mine, self.rank, 0)) // SLOT_ROWS + 1
        self.per_core = lax.axis_size("dev") * SLOT_ROWS

    def slot(self, turn):
        rank = self.rank - turn * SLOT_ROWS
        used = (rank >= 0) & (rank < SLOT_ROWS)
        slot = self.owner * SLOT_ROWS + rank + jnp.where(self.mine, 0, self.per_core)
        return jnp.where(used, slot, -1)

    def ask(self, turn):
        slots = jnp.arange(self.per_core, dtype=jnp.int32)
        found = self.slot(turn)[None] == slots[:, None]
        asked = jnp.max(jnp.where(found, self.inside[None], 0), 1).reshape(-1, SLOT_ROWS)
        header = jnp.broadcast_to(self.need, (asked.shape[0], 1))
        return lax.all_to_all(jnp.concatenate([asked, header], 1), "dev", 0, 0)

    def answer(self, wanted):
        numbers = jnp.arange(self.table.shape[0], dtype=jnp.int32)
        pick = (wanted[:, :SLOT_ROWS].reshape(-1, 1) == numbers[None]).astype(B16)
        sent = jnp.dot(pick, self.table, preferred_element_type=F32).astype(B16)
        return sent.reshape(-1, SLOT_ROWS, self.table.shape[1])

    def fetch(self, sent):
        got = lax.all_to_all(sent, "dev", 0, 0)
        return got.reshape(self.per_core, self.table.shape[1])

    def place(self, turn, got):
        slots = jnp.arange(2 * self.per_core, dtype=jnp.int32)
        spread = (self.slot(turn)[:, None] == slots[None]).astype(B16)
        both = jnp.concatenate([got, partner(got)], 0)
        return jnp.dot(spread, both, preferred_element_type=F32)

    def finish(self, base, wanted, got):
        most = jnp.max(wanted[:, SLOT_ROWS])
        most = jnp.maximum(most, partner(most.reshape(1, 1))[0, 0])

        def again(state):
            return state[0] < most

        def turn(state):
            got = self.fetch(self.answer(self.ask(state[0])))
            return (state[0] + 1, state[1] + self.place(state[0], got))

        return lax.while_loop(again, turn, (jnp.int32(1), base + self.place(0, got)))[1]


def adamw_update(weight, moment, square, gradient, corr_one, corr_two):
    moment = BETA_ONE * moment + (1.0 - BETA_ONE) * gradient
    square = BETA_TWO * square + (1.0 - BETA_TWO) * gradient * gradient
    weight = weight - LEARN_RATE * (
        moment / corr_one / (jnp.sqrt(square / corr_two) + ADAM_EPS) + DECAY_RATE * weight
    )
    return (weight, moment, square)


def local(
    token_ids,
    bucket,
    seq_lengths,
    loss_pos,
    targets,
    wte,
    wpe,
    w_qkv,
    w_out,
    w_fc,
    w_proj,
    frozen_vec,
    fc_bias,
    final_norm,
    prefix_table,
    inner_weight,
    inner_bias,
    outer_weight,
    outer_bias,
    moment_prefix,
    square_prefix,
    moment_inner,
    square_inner,
    moment_inner_bias,
    square_inner_bias,
    moment_outer,
    square_outer,
    moment_outer_bias,
    square_outer_bias,
):
    row_count = token_ids.shape[0]
    scored = loss_pos.shape[0]
    width = wte.shape[1]
    half = w_qkv.shape[3]
    size = lax.axis_size("dev")
    own_index = lax.axis_index("ta")
    plen = prefix_table.shape[0]
    prefix_rows = 16
    me = lax.axis_index("dev").astype(jnp.int32).reshape(1)
    orders = (bit_orders(size, 3), bit_orders(size, 4))
    stages = len(orders[0][0])
    bucket_width = bucket[0]
    shift = jnp.where(bucket_width == 256, 8, 10).astype(jnp.int32)
    layout = jnp.concatenate([shift.reshape(1), bucket_width.reshape(1), seq_lengths[0]])

    rounds = Rounds()
    ff = w_fc.shape[2]
    totals = (4 * half, 2 * ff)
    cuts = [[cuts_of(total, LANES, len(order)) for total in totals] for order in orders]

    def add_layer(layer_id, qkv, out, fc, proj):
        sides = (
            jnp.concatenate([qkv[c] for c in range(3)] + [out.T], 1),
            jnp.concatenate([fc, proj.T], 1),
        )
        parts = [
            [
                rows[:, c[p] : c[p + 1]]
                for rows, c in zip(sides, cuts[layer_id])
            ]
            for p in range(len(orders[layer_id]))
        ]
        rounds.add(
            layer_id,
            orders[layer_id],
            [jnp.concatenate(part, 1) for part in parts],
            [part[0].shape[1] for part in parts],
        )

    def weight(layer_id, side, first, last):
        segments = [
            (rounds.held[layer_id, p, side], order, cuts[layer_id][side][p])
            for p, order in enumerate(orders[layer_id])
        ]
        return Gathered(segments, first, last)

    def attention_weight(layer_id, first=0):
        return weight(layer_id, 0, first * half, 4 * half)

    def mlp_weights(layer_id):
        return weight(layer_id, 1, 0, ff), weight(layer_id, 1, ff, 2 * ff)

    def head_bias(layer_id):
        part = lax.dynamic_slice_in_dim(frozen_vec[layer_id, 4:7], own_index * half, half, 1)
        return part.reshape(1, 3 * half)

    add_layer(0, w_qkv[0], w_out[0], w_fc[0], w_proj[0])
    ids, prefix_in = rounds.step(
        0,
        0,
        through=(
            (token_ids, targets),
            (prefix_table, inner_weight, inner_bias, outer_weight),
        ),
    )
    lookup = TableRows(jnp.concatenate(ids), wte)
    wanted = lookup.ask(0)
    hidden = jnp.tanh(jnp.dot(prefix_in[0], prefix_in[1], precision=HIGHEST) + prefix_in[2])
    sums = jnp.einsum("pr,rlcd->lcpd", hidden, prefix_in[3], precision=HIGHEST)
    for stage in range(stages - 2):
        sums = sums + flip(sums, 1 << stage)

    wanted, sums = rounds.step(0, 1, through=(wanted, sums))
    sent = lookup.answer(wanted)
    sums = sums + flip(sums, 1 << (stages - 2))
    for stage in range(2, stages - 2):
        rounds.step(0, stage)

    sent, wanted, sums, last_layer = rounds.step(
        0,
        stages - 2,
        through=(sent, wanted, sums, (w_qkv[1], w_out[1], w_fc[1], w_proj[1])),
    )
    got = lookup.fetch(sent)
    add_layer(1, *last_layer)
    sums = sums + flip(sums, 1 << (stages - 1))
    prefix_kv = (sums + outer_bias[:, :, None, :]).astype(B16)
    prefix_kv = jnp.pad(prefix_kv, ((0, 0), (0, 0), (0, prefix_rows - plen), (0, 0)))

    got, wanted, places, prefix_kv, next_rows = rounds.step(
        0,
        stages - 1,
        0,
        through=(got, wanted, wpe, prefix_kv, [rounds.held[1, p][0] for p in range(len(orders[1]))]),
    )
    for part, array in enumerate(next_rows):
        rounds.held[1, part] = [array]
    repeat = row_count // 256
    places = jnp.where(bucket_width == 256, jnp.tile(places[:256], (repeat, 1)), places[:row_count])
    places = jnp.concatenate([places, jnp.zeros((scored, width), places.dtype)], 0)
    stream = lookup.finish(places.astype(F32), wanted, got)

    stream = rounds.step(0, stages - 1, 1, through=stream)
    part, q0, mixed0, lse0 = first_attention(
        stream,
        row_count,
        frozen_vec[0, 0:2],
        head_bias(0),
        prefix_kv[0],
        layout,
        me,
        attention_weight(0),
        plen,
    )

    part = rounds.step(1, 0, through=part)
    other = partner(part)

    part, other = rounds.step(1, 1, through=(part, other))
    vec = frozen_vec[0]
    part_two, middle0, slope0 = mlp(
        stream,
        part,
        other,
        jnp.stack([vec[7], vec[2], vec[3]]),
        fc_bias[0:1],
        me,
        *mlp_weights(0),
    )

    part_two, table = rounds.step(1, 2, through=(part_two, wte))
    other = partner(part_two)
    entries = wte.shape[0]
    table_half = -(-entries // 64) * 64
    table = jnp.pad(table, ((0, table_half - entries), (0, 0)))
    for stage in range(3, stages - 1):
        rounds.step(1, stage)

    table, part_two, other = rounds.step(1, stages - 1, 0, through=(table, part_two, other))
    table = jnp.concatenate([table, partner(table)], 0)

    part_two, other, table = rounds.step(1, stages - 1, 1, through=(part_two, other, table))

    vec_last = frozen_vec[1]
    picks_column = loss_pos.reshape(scored, 1)
    stream1, part, k1, v1, q1, mixed1, lse1, chosen = last_attention(
        middle0,
        part_two,
        other,
        jnp.stack([vec[8], vec_last[0], vec_last[1]]),
        head_bias(1),
        prefix_kv[1],
        layout,
        loss_pos,
        picks_column,
        me,
        attention_weight(1),
        plen,
    )
    part_two, middle1, slope1 = mlp(
        chosen,
        part,
        partner(part),
        jnp.stack([vec_last[7], vec_last[2], vec_last[3]]),
        fc_bias[1:2],
        me,
        *mlp_weights(1),
    )
    both = part_two.astype(F32) + partner(part_two).astype(F32)
    head_rows = middle1 + (both + vec_last[8])
    center = head_rows - jnp.mean(head_rows, -1, keepdims=True)
    spread = jnp.mean(center * center, -1, keepdims=True)
    head_in = (center * lax.rsqrt(spread + EPS_NORM) * final_norm[0] + final_norm[1]).astype(B16)

    core_rows = scored // 2
    mine = lax.dynamic_slice_in_dim(head_in, own_index * core_rows, core_rows, 0)
    cuts_head = (0, 48, 96, core_rows)
    head_order = bit_orders(size, 3)
    head = Rounds()
    head.add(0, head_order, [mine[a:b] for a, b in zip(cuts_head[:-1], cuts_head[1:])])
    for stage in range(stages):
        head.step(0, stage)
    near, far = [
        [head.held[0, p][side].reshape(-1, width) for p in range(len(head_order))]
        for side in range(2)
    ]
    keep = vocabulary(near[:1], table, entries)
    far, keep, near = lax.optimization_barrier((far, keep, near))
    send = vocabulary(far, table, entries)
    keep = list(keep) + list(vocabulary(near[1:], table, entries))
    for stage in reversed(range(stages)):
        got = [flip(array, head_order[p][stage]) for p, array in enumerate(send)]
        keep, send = merge(keep, got, stage == 0)
    own_means = jnp.concatenate(keep, 0)
    other_means = partner(own_means)
    means = jnp.where(
        own_index == 0,
        jnp.concatenate([own_means, other_means], 0),
        jnp.concatenate([other_means, own_means], 0),
    )
    place = loss_pos % bucket_width
    slot = loss_pos // bucket_width
    lengths = jnp.sum(
        jnp.where(
            slot[:, None] == jnp.arange(seq_lengths.shape[1], dtype=jnp.int32)[None],
            seq_lengths[0][None],
            0,
        ),
        1,
    )
    counted = (place < lengths).astype(F32).reshape(scored, 1)
    count_total = float(scored * size)
    grad_rows, loss_terms = head_back(
        means, head_rows, head_in, stream, row_count, counted, final_norm, count_total
    )
    loss_part = jnp.sum(loss_terms[:, 0])

    (part,) = mlp_back(grad_rows, slope1, me, *mlp_weights(1))
    part, spread_grad, d_prefix1 = last_attention_back(
        grad_rows,
        part,
        partner(part),
        middle1,
        vec_last[2:3],
        q1,
        k1,
        v1,
        lse1,
        prefix_kv[1],
        layout,
        loss_pos,
        picks_column,
        me,
        attention_weight(1),
        plen,
    )
    part, grad_stream = mlp_back(
        spread_grad,
        slope0,
        me,
        *mlp_weights(0),
        (stream1, vec_last[0:1], part, partner(part)),
    )
    d_prefix0 = first_prefix_back(
        grad_stream,
        part,
        partner(part),
        middle0,
        vec[2:3],
        q0,
        mixed0,
        lse0,
        prefix_kv[0],
        me,
        attention_weight(0, 3),
        plen,
    )
    d_prefix = sum_over_dev(jnp.stack([d_prefix0, d_prefix1])[:, :, :plen])

    d_outer = jnp.einsum("pr,lcpd->rlcd", hidden, d_prefix, precision=HIGHEST)
    d_outer_bias = jnp.sum(d_prefix, 2)
    hidden_part = jnp.einsum("lcpd,rlcd->pr", d_prefix, outer_weight, precision=HIGHEST)
    outer_square = jnp.sum(d_outer * d_outer) + jnp.sum(d_outer_bias * d_outer_bias) / size
    over_ta = jnp.concatenate(
        [hidden_part, jnp.broadcast_to(outer_square, (1, hidden_part.shape[1]))], 0
    )
    over_ta = over_ta + partner(over_ta)
    d_hidden = over_ta[:plen]
    d_pre = d_hidden * (1.0 - hidden * hidden)
    d_inner = jnp.dot(prefix_table.T, d_pre, precision=HIGHEST)
    d_inner_bias = jnp.sum(d_pre, 0)
    table_part = jnp.dot(d_pre, inner_weight.T, precision=HIGHEST)
    squares = over_ta[plen, 0] + jnp.sum(d_inner * d_inner) + jnp.sum(d_inner_bias * d_inner_bias)
    lane = jnp.arange(table_part.shape[1], dtype=jnp.int32)
    last_row = jnp.where(lane == 0, squares, jnp.where(lane == 1, loss_part, 0.0))
    totals = sum_over_dev(jnp.concatenate([table_part, last_row[None]], 0))
    d_table = totals[:plen]
    square_sum = totals[plen, 0]
    loss_value = totals[plen, 1] / count_total
    grad_total = jnp.sqrt(square_sum + jnp.sum(d_table * d_table))
    factor = jnp.minimum(1.0, CLIP_NORM / (grad_total + 1e-06))
    corr_one = 1.0 - BETA_ONE**adam_steps
    corr_two = 1.0 - BETA_TWO**adam_steps
    prefix_out = adamw_update(
        prefix_table, moment_prefix, square_prefix, factor * d_table, corr_one, corr_two
    )
    inner_out = adamw_update(
        inner_weight, moment_inner, square_inner, factor * d_inner, corr_one, corr_two
    )
    ibias_out = adamw_update(
        inner_bias, moment_inner_bias, square_inner_bias, factor * d_inner_bias, corr_one, corr_two
    )
    outer_out = adamw_update(
        outer_weight, moment_outer, square_outer, factor * d_outer, corr_one, corr_two
    )
    obias_out = adamw_update(
        outer_bias, moment_outer_bias, square_outer_bias, factor * d_outer_bias, corr_one, corr_two
    )
    return (
        loss_value.reshape(1),
        grad_total.reshape(1),
        prefix_out[0],
        prefix_out[1],
        prefix_out[2],
        inner_out[0],
        inner_out[1],
        inner_out[2],
        ibias_out[0],
        ibias_out[1],
        ibias_out[2],
        outer_out[0],
        outer_out[1],
        outer_out[2],
        obias_out[0],
        obias_out[1],
        obias_out[2],
        prefix_out[0].astype(B16),
        inner_out[0].astype(B16),
        ibias_out[0].astype(B16),
        outer_out[0].astype(B16),
        obias_out[0].astype(B16),
    )


def solution(mesh):
    in_specs = (
        P("dev"),
        P("dev"),
        P("dev", None),
        P("dev"),
        P("dev"),
        P(("dev", "ta"), None),
        P(),
        P(None, None, "dev", "ta"),
        P(None, "ta", "dev"),
        P(None, "dev", "ta"),
        P(None, "ta", "dev"),
        P(),
        P(None, "ta"),
        P(),
        P(),
        P(None, "dev"),
        P("dev"),
        P("dev", None, None, "ta"),
        P(None, None, "ta"),
        P(),
        P(),
        P(None, "dev"),
        P(None, "dev"),
        P("dev"),
        P("dev"),
        P("dev", None, None, "ta"),
        P("dev", None, None, "ta"),
        P(None, None, "ta"),
        P(None, None, "ta"),
    )
    out_specs = (
        P(),
        P(),
        P(),
        P(),
        P(),
        P(None, "dev"),
        P(None, "dev"),
        P(None, "dev"),
        P("dev"),
        P("dev"),
        P("dev"),
        P("dev", None, None, "ta"),
        P("dev", None, None, "ta"),
        P("dev", None, None, "ta"),
        P(None, None, "ta"),
        P(None, None, "ta"),
        P(None, None, "ta"),
        P(),
        P(None, "dev"),
        P("dev"),
        P("dev", None, None, "ta"),
        P(None, None, "ta"),
    )
    return jax.shard_map(local, mesh=mesh, in_specs=in_specs, out_specs=out_specs, check_vma=False)
```

```python
import functools

import jax
import jax.numpy as jnp
from jax import lax
from jax.experimental import pallas as pl
from jax.experimental.layout import Layout, with_layout_constraint
from jax.experimental.pallas import tpu as pltpu
from jax.sharding import PartitionSpec as P

HEAD_DIM = 64


EPS_NORM = 1e-05
CLIP_NORM = 0.001
LEARN_RATE = 0.02
BETA_ONE = 0.9
BETA_TWO = 0.999
ADAM_EPS = 1e-08
DECAY_RATE = 0.01
adam_steps = 10.0
NEG_BIG = -1e30
HIGHEST = lax.Precision.HIGHEST
F32 = jnp.float32
B16 = jnp.bfloat16
GELU_SCALE = 0.7978845608028654
GELU_CUBE = 0.044715
SLOT_ROWS = 48
BLOCK = 256
LANES = 128
PIECE = 2048
SWAP = [(0, 1), (1, 0)]


def shape(dims, dtype):
    return jax.ShapeDtypeStruct(dims, dtype)


def params(**more):
    return pltpu.CompilerParams(dimension_semantics=("arbitrary",), **more)


def cost(microseconds):
    return pl.CostEstimate(
        flops=int(microseconds * 1.15e9), transcendentals=0, bytes_accessed=1024
    )


def flip(array, bit):
    size = lax.axis_size("dev")
    return lax.ppermute(array, "dev", [(i, i ^ bit) for i in range(size)])


def partner(array):
    return lax.ppermute(array, "ta", SWAP)


def bit_orders(size, parts):
    bits = [1 << k for k in range(size.bit_length() - 1)]
    if size == 16:
        x, y, near, far = bits
        if parts == 3:
            return ((far, y, near, x), (near, far, x, y), (far, x, y, near))
        return (
            (x, y, near, far),
            (x, y, far, near),
            (near, far, x, y),
            (far, near, y, x),
        )
    return tuple(tuple(bits[k:] + bits[:k]) for k in range(parts))


def cuts_of(total, unit, parts):
    sixths = (0, 2, 4) if parts == 3 else (0, 1, 2, 4)
    return [total * k // 6 // unit * unit for k in sixths] + [total]


def pack(groups):
    arrays = [array for group, unused, unused in groups for array in group]
    outs = []
    moves = []
    for number, (group, first, last) in enumerate(groups):
        total = 0
        for array in group:
            moves.append((number, total, array.shape[0], first, last - first))
            total += array.shape[0]
        outs.append(shape((total, group[0].shape[1], last - first), group[0].dtype))

    def body(*refs):
        sems = refs[-1]
        copies = [
            pltpu.make_async_copy(
                refs[index].at[:, :, pl.ds(first, wide)],
                refs[len(arrays) + number].at[pl.ds(begin, count)],
                sems.at[index],
            )
            for index, (number, begin, count, first, wide) in enumerate(moves)
        ]
        for copy in copies:
            copy.start()
        for copy in copies:
            copy.wait()

    return pl.pallas_call(
        body,
        in_specs=[pl.BlockSpec(memory_space=pl.ANY)] * len(arrays),
        out_specs=[pl.BlockSpec(memory_space=pltpu.VMEM)] * len(outs),
        out_shape=outs,
        scratch_shapes=[pltpu.SemaphoreType.DMA((len(arrays),))],
        cost_estimate=cost(2),
        name="pack",
    )(*arrays)


class Rounds:
    def __init__(self):
        self.orders = {}
        self.held = {}
        self.split = {}
        self.before = []

    def add(self, chunk, orders, arrays, splits=None):
        self.orders[chunk] = orders
        for part, array in enumerate(arrays):
            self.held[chunk, part] = [array[None]]
            self.split[chunk, part] = splits[part] if splits else None

    def step(self, chunk, stage, side=None, through=()):
        parts = range(len(self.orders[chunk]))
        held = [self.held[chunk, part] for part in parts]
        if stage == 0:
            sends = [arrays[0] for arrays in held]
        else:
            spans = []
            for part, arrays in zip(parts, held):
                cut, width = self.split[chunk, part], arrays[0].shape[2]
                spans.append((cut if side == 1 else 0, cut if side == 0 else width))
            sends = pack([(arrays, *span) for arrays, span in zip(held, spans)])
        through, sends, unused = lax.optimization_barrier((through, sends, self.before))
        self.before = []
        for part, send in enumerate(sends):
            got = flip(send, self.orders[chunk][part][stage])
            self.held[(chunk, part) if side is None else (chunk, part, side)] = [send, got]
            self.before.append(got)
        return through


def sum_over_dev(array):
    size = lax.axis_size("dev")
    bit = 1
    while bit < size:
        if bit * 2 < size:
            near, far, both = flip(array, bit), flip(array, bit * 2), flip(array, bit * 3)
            array = (array + near) + (far + both)
        else:
            array = array + flip(array, bit)
        bit = bit * 4
    return array


def norm_rows(x):
    center = x - jnp.mean(x, -1, keepdims=True)
    scale = lax.rsqrt(jnp.mean(center * center, -1, keepdims=True) + EPS_NORM)
    return center * scale, scale


def norm_rows_back(gradient, x, gain):
    xhat, scale = norm_rows(x)
    e2 = gradient * gain
    mean_one = jnp.mean(e2, -1, keepdims=True)
    mean_two = jnp.mean(e2 * xhat, -1, keepdims=True)
    return (e2 - mean_one - xhat * mean_two) * scale


def dot_nn(a, b):
    return lax.dot_general(a, b, (((1,), (0,)), ((), ())), preferred_element_type=F32)


def dot_nt(a, b):
    return lax.dot_general(a, b, (((1,), (1,)), ((), ())), preferred_element_type=F32)


def dot_tn(a, b):
    return lax.dot_general(a, b, (((0,), (0,)), ((), ())), preferred_element_type=F32)


class Gathered:
    def __init__(self, segments, first, last):
        self.pieces = []
        for stacks, order, begin in segments:
            low, high = max(first, begin), min(last, begin + stacks[0].shape[2])
            if low < high:
                self.pieces.append((stacks, order, low - begin, high - low, low - first))
        stacks, order, *unused = self.pieces[0]
        self.rows = stacks[0].shape[1]
        self.blocks = 1 << len(order)
        self.scratch = [
            pltpu.VMEM((self.blocks * self.rows, last - first), B16),
            pltpu.SemaphoreType.DMA((len(self.pieces) * self.blocks,)),
        ]
        self.operands = [array for piece in self.pieces for array in piece[0]]
        self.specs = [pl.BlockSpec(memory_space=pl.ANY)] * len(self.operands)

    def each(self, act, me, refs, full, sems):
        for number, (stacks, order, source, wide, target) in enumerate(self.pieces):
            blocks = self.blocks // len(stacks)
            for side, ref in enumerate(refs[number * len(stacks) : (number + 1) * len(stacks)]):

                def one(index, carry, side=side, ref=ref):
                    place = me ^ (order[-1] if side else 0)
                    for k, bit in enumerate(order[:-1]):
                        place = place ^ jnp.where((index >> k) % 2 == 1, bit, 0)
                    start = pl.multiple_of(place * self.rows, self.rows)
                    copy = pltpu.make_async_copy(
                        ref.at[index, :, pl.ds(source, wide)],
                        full.at[pl.ds(start, self.rows), pl.ds(target, wide)],
                        sems.at[number * self.blocks + side * blocks + index],
                    )
                    act(copy)
                    return carry

                lax.fori_loop(0, blocks, one, 0)

    def start(self, *refs):
        self.each(lambda copy: copy.start(), *refs)

    def wait(self, *refs):
        self.each(lambda copy: copy.wait(), *refs)


def rows_spec(width, block=BLOCK):
    return pl.BlockSpec((block, width), lambda i, *refs: (i, 0))


def whole_spec(dims):
    return pl.BlockSpec(dims, lambda i, *refs: (0,) * len(dims))


def key_bias(layout_ref, query_pos, key_count):
    shift = layout_ref[0]
    dims = (query_pos.shape[0], key_count)
    key_pos = lax.broadcasted_iota(jnp.int32, (1, key_count), 1)
    key_seg = lax.shift_right_logical(key_pos, jnp.full((1, key_count), shift, jnp.int32))
    query_seg = lax.shift_right_logical(query_pos, jnp.full(query_pos.shape, shift, jnp.int32))
    length = jnp.zeros((1, key_count), jnp.int32)
    for slot in range(layout_ref.shape[0] - 2):
        length = jnp.where(key_seg == slot, layout_ref[2 + slot], length)
    place = key_pos - key_seg * layout_ref[1]
    key_seg = jnp.where(place < length, key_seg, -1)
    seen = (jnp.broadcast_to(query_seg, dims) == jnp.broadcast_to(key_seg, dims)) & (
        jnp.broadcast_to(key_pos, dims) <= jnp.broadcast_to(query_pos, dims)
    )
    return jnp.where(seen, 0.0, NEG_BIG)


def prefix_bias(rows, prefix_rows, prefix_len):
    lane = lax.broadcasted_iota(jnp.int32, (rows, prefix_rows), 1)
    return jnp.where(lane < prefix_len, 0.0, NEG_BIG)


def attend(query, key, value, key_prefix, value_prefix, bias, bias_prefix):
    scores = dot_nt(query, key) + bias
    scores_prefix = dot_nt(query, key_prefix) + bias_prefix
    highest = jnp.maximum(
        jnp.max(scores, -1, keepdims=True), jnp.max(scores_prefix, -1, keepdims=True)
    )
    shares = jnp.exp(scores - highest)
    shares_prefix = jnp.exp(scores_prefix - highest)
    total = jnp.sum(shares, -1, keepdims=True) + jnp.sum(shares_prefix, -1, keepdims=True)
    mixed = dot_nn(shares.astype(B16), value) + dot_nn(shares_prefix.astype(B16), value_prefix)
    return mixed / total, highest + jnp.log(total)


def attend_pairs(q_ref, k_ref, v_ref, prefix_ref, mixed_ref, lse_ref, rows, key_count, bias, plen):
    prefix_rows = prefix_ref.shape[1]
    bias_prefix = prefix_bias(BLOCK, prefix_rows, plen)
    lse_ref[rows, :] = jnp.zeros((BLOCK, LANES), F32)
    lane = lax.broadcasted_iota(jnp.int32, (BLOCK, LANES), 1)

    def pair(index, carry):
        columns = pl.ds(pl.multiple_of(index * LANES, LANES), LANES)
        query = q_ref[rows, columns]
        key = k_ref[pl.ds(0, key_count), columns]
        value = v_ref[pl.ds(0, key_count), columns]
        key_prefix = prefix_ref[0, :, columns]
        value_prefix = prefix_ref[1, :, columns]
        parts = []
        for side in range(2):
            cut = slice(side * HEAD_DIM, (side + 1) * HEAD_DIM)
            mixed, lse = attend(
                query[:, cut],
                key[:, cut],
                value[:, cut],
                key_prefix[:, cut],
                value_prefix[:, cut],
                bias,
                bias_prefix,
            )
            parts.append(mixed)
            lse_ref[rows, :] = jnp.where(
                lane // prefix_rows == 2 * index + side, lse, lse_ref[rows, :]
            )
        mixed_ref[rows, columns] = jnp.concatenate(parts, 1).astype(B16)
        return carry

    lax.fori_loop(0, q_ref.shape[1] // LANES, pair, 0)


def first_attention(stream, row_count, vectors, bias_qkv, prefix, layout, me, weight, plen):
    width = stream.shape[1]
    half = prefix.shape[2]
    scale = HEAD_DIM ** (-0.5)

    stacks = len(weight.operands)

    def body(me_ref, layout_ref, stream_ref, vec_ref, bias_ref, prefix_ref, *refs):
        part_ref, q_out, mixed_out, lse_out, full, sems, q_s, k_s, v_s = refs[stacks:]
        step = pl.program_id(0)
        refs = (me_ref[0], refs[:stacks], full, sems)

        @pl.when(step == 0)
        def _():
            weight.start(*refs)
            weight.wait(*refs)

        xhat, unused = norm_rows(stream_ref[...])
        normed = (xhat * vec_ref[0:1, :] + vec_ref[1:2, :]).astype(B16)
        qkv = dot_nn(normed, full[:, : 3 * half]) + bias_ref[...]
        rows = pl.ds(pl.multiple_of(step * BLOCK, BLOCK), BLOCK)
        q_s[...] = (qkv[:, :half].astype(B16) * scale).astype(B16)
        k_s[rows, :] = qkv[:, half : 2 * half].astype(B16)
        v_s[rows, :] = qkv[:, 2 * half :].astype(B16)
        q_out[...] = q_s[...]
        local_pos = lax.broadcasted_iota(jnp.int32, (BLOCK, 1), 0)
        for case in range(row_count // BLOCK):

            @pl.when(step == case)
            def _(case=case):
                key_count = (case + 1) * BLOCK
                bias = key_bias(layout_ref, local_pos + case * BLOCK, key_count)
                attend_pairs(
                    q_s, k_s, v_s, prefix_ref, mixed_out, lse_out,
                    pl.ds(0, BLOCK), key_count, bias, plen,
                )

        part_ref[...] = dot_nt(mixed_out[...], full[:, 3 * half :]).astype(B16)

    return pl.pallas_call(
        body,
        grid_spec=pltpu.PrefetchScalarGridSpec(
            num_scalar_prefetch=2,
            grid=(row_count // BLOCK,),
            in_specs=[
                rows_spec(width),
                whole_spec(vectors.shape),
                whole_spec(bias_qkv.shape),
                whole_spec(prefix.shape),
                *weight.specs,
            ],
            out_specs=[rows_spec(width), rows_spec(half), rows_spec(half), rows_spec(LANES)],
            scratch_shapes=weight.scratch
            + [pltpu.VMEM((BLOCK, half), B16)]
            + [pltpu.VMEM((row_count, half), B16)] * 2,
        ),
        out_shape=[
            shape((row_count, width), B16),
            shape((row_count, half), B16),
            shape((row_count, half), B16),
            shape((row_count, LANES), F32),
        ],
        compiler_params=params(),
        cost_estimate=cost(30 * row_count // 1024),
        name="first_attention",
    )(me, layout, stream, vectors, bias_qkv, prefix, *weight.operands)


def mlp(base, own, other, vectors, bias_up, me, w_up, w_down):
    row_count, width = own.shape
    hidden = bias_up.shape[1]

    ups, downs = len(w_up.operands), len(w_down.operands)

    def body(me_ref, base_ref, own_ref, other_ref, vec_ref, bias_ref, *refs):
        part_ref, middle_ref, slope_ref, up, up_sems, down, down_sems = refs[ups + downs :]
        step = pl.program_id(0)
        up_refs = (me_ref[0], refs[:ups], up, up_sems)
        down_refs = (me_ref[0], refs[ups : ups + downs], down, down_sems)

        @pl.when(step == 0)
        def _():
            w_up.start(*up_refs)
            w_down.start(*down_refs)

        middle = base_ref[...] + (
            (own_ref[...].astype(F32) + other_ref[...].astype(F32)) + vec_ref[0:1, :]
        )
        middle_ref[...] = middle
        xhat, unused = norm_rows(middle)
        normed = (xhat * vec_ref[1:2, :] + vec_ref[2:3, :]).astype(B16)

        @pl.when(step == 0)
        def _():
            w_up.wait(*up_refs)

        total = None
        for first in range(0, hidden, PIECE):
            piece = slice(first, first + PIECE)
            u = dot_nn(normed, up[:, piece]) + bias_ref[:, piece]
            square = u * u
            t = jnp.tanh(GELU_SCALE * u * (1.0 + GELU_CUBE * square))
            half_one = 0.5 + 0.5 * t
            active = (u * half_one).astype(B16)
            bend = (0.5 * GELU_SCALE) * u * (1.0 - t * t) * (1.0 + 3 * GELU_CUBE * square)
            slope_ref[:, piece] = (half_one + bend).astype(B16)
            if first == 0:

                @pl.when(step == 0)
                def _():
                    w_down.wait(*down_refs)

            product = dot_nt(active, down[:, piece])
            total = product if total is None else total + product
        part_ref[...] = total.astype(B16)

    return pl.pallas_call(
        body,
        grid_spec=pltpu.PrefetchScalarGridSpec(
            num_scalar_prefetch=1,
            grid=(row_count // BLOCK,),
            in_specs=[
                rows_spec(width),
                rows_spec(width),
                rows_spec(width),
                whole_spec(vectors.shape),
                whole_spec(bias_up.shape),
                *w_up.specs,
                *w_down.specs,
            ],
            out_specs=[rows_spec(width), rows_spec(width), rows_spec(hidden)],
            scratch_shapes=w_up.scratch + w_down.scratch,
        ),
        out_shape=[
            shape((row_count, width), B16),
            shape((row_count, width), F32),
            shape((row_count, hidden), B16),
        ],
        compiler_params=params(),
        cost_estimate=cost(23 * row_count // 1024),
        name="mlp",
    )(me, base, own, other, vectors, bias_up, *w_up.operands, *w_down.operands)


def last_attention(base, own, other, vectors, bias_qkv, prefix, layout, picks, picks_column, me,
                   weight, plen):
    row_count, width = base.shape
    half = prefix.shape[2]
    scored = picks.shape[0]
    steps = row_count // BLOCK
    scale = HEAD_DIM ** (-0.5)

    stacks = len(weight.operands)

    def body(me_ref, layout_ref, picks_ref, base_ref, own_ref, other_ref, vec_ref, bias_ref,
             prefix_ref, column_ref, *refs):
        (stream_out, part_ref, k_out, v_out, q_out, mixed_out, lse_out, chosen_out,
         full, sems, stream_s, k_s, v_s) = refs[stacks:]
        step = pl.program_id(0)
        refs = (me_ref[0], refs[:stacks], full, sems)

        @pl.when(step == 0)
        def _():
            weight.start(*refs)
            weight.wait(*refs)

        stream = base_ref[...] + (
            (own_ref[...].astype(F32) + other_ref[...].astype(F32)) + vec_ref[0:1, :]
        )
        stream_out[...] = stream
        rows = pl.ds(pl.multiple_of(step * BLOCK, BLOCK), BLOCK)
        stream_s[rows, :] = stream
        xhat, unused = norm_rows(stream)
        normed = (xhat * vec_ref[1:2, :] + vec_ref[2:3, :]).astype(B16)
        keys_values = (
            dot_nn(normed, full[:, half : 3 * half]) + bias_ref[:, half : 3 * half]
        ).astype(B16)
        k_out[...] = keys_values[:, :half]
        v_out[...] = keys_values[:, half:]
        k_s[rows, :] = keys_values[:, :half]
        v_s[rows, :] = keys_values[:, half:]

        @pl.when(step == steps - 1)
        def _():
            def pick(index, carry):
                chosen_out[pl.ds(index, 1), :] = stream_s[pl.ds(picks_ref[index], 1), :]
                return carry

            lax.fori_loop(0, scored, pick, 0, unroll=8)
            for first in range(0, scored, BLOCK):
                block = pl.ds(first, BLOCK)
                chosen_hat, unused = norm_rows(chosen_out[block, :])
                chosen = (chosen_hat * vec_ref[1:2, :] + vec_ref[2:3, :]).astype(B16)
                query = (dot_nn(chosen, full[:, :half]) + bias_ref[:, :half]).astype(B16)
                q_out[block, :] = (query * scale).astype(B16)
                bias = key_bias(layout_ref, column_ref[block, :], row_count)
                attend_pairs(
                    q_out, k_s, v_s, prefix_ref, mixed_out, lse_out, block, row_count, bias, plen
                )
                part_ref[block, :] = dot_nt(mixed_out[block, :], full[:, 3 * half :]).astype(B16)

    return pl.pallas_call(
        body,
        grid_spec=pltpu.PrefetchScalarGridSpec(
            num_scalar_prefetch=3,
            grid=(steps,),
            in_specs=[
                rows_spec(width),
                rows_spec(width),
                rows_spec(width),
                whole_spec(vectors.shape),
                whole_spec(bias_qkv.shape),
                whole_spec(prefix.shape),
                whole_spec(picks_column.shape),
                *weight.specs,
            ],
            out_specs=[
                rows_spec(width),
                whole_spec((scored, width)),
                rows_spec(half),
                rows_spec(half),
                whole_spec((scored, half)),
                whole_spec((scored, half)),
                whole_spec((scored, LANES)),
                whole_spec((scored, width)),
            ],
            scratch_shapes=weight.scratch
            + [pltpu.VMEM((row_count, width), F32)]
            + [pltpu.VMEM((row_count, half), B16)] * 2,
        ),
        out_shape=[
            shape((row_count, width), F32),
            shape((scored, width), B16),
            shape((row_count, half), B16),
            shape((row_count, half), B16),
            shape((scored, half), B16),
            shape((scored, half), B16),
            shape((scored, LANES), F32),
            shape((scored, width), F32),
        ],
        compiler_params=params(),
        cost_estimate=cost(22),
        name="last_attention",
    )(me, layout, picks, base, own, other, vectors, bias_qkv, prefix, picks_column, *weight.operands)


def split_lse(lse, rows):
    high = lse.astype(B16).astype(F32)
    middle = (lse - high).astype(B16).astype(F32)
    low = (lse - high) - middle
    lane = lax.broadcasted_iota(jnp.int32, (rows, LANES), 1)
    packed = jnp.where(lane == 0, high, jnp.where(lane == 1, middle, jnp.where(lane == 2, low, 0.0)))
    return packed.astype(B16)


VMEM = pl.BlockSpec(memory_space=pltpu.VMEM)


def vocabulary(stacks, table, entries):
    width = table.shape[1]
    padded = table.shape[0]
    half = padded // 2
    ends = [0]
    for stack in stacks:
        ends.append(ends[-1] + stack.shape[0])
    block = max(b for b in range(16, 400, 16) if ends[-1] % b == 0)

    def body(*refs):
        table_ref = refs[len(stacks)]
        outs = refs[len(stacks) + 1 : -2]
        rows_s, mean_s = refs[-2:]
        for ref, first, last in zip(refs, ends[:-1], ends[1:]):
            rows_s[first:last, :] = ref[...]

        def turn(index, carry):
            rows = pl.ds(pl.multiple_of(index * block, block), block)
            logits = dot_nt(rows_s[rows, :], table_ref[...])
            pieces = []
            for first in range(0, padded, LANES):
                piece = logits[:, first : first + LANES]
                if any(c % half >= entries for c in range(first, first + LANES)):
                    lane = lax.broadcasted_iota(jnp.int32, piece.shape, 1) + first
                    piece = jnp.where(lane % half < entries, piece, NEG_BIG)
                pieces.append(piece)
            logits = jnp.concatenate(pieces, 1)
            highest = jnp.max(logits, -1, keepdims=True)
            shares = jnp.exp(logits - highest)
            total = jnp.sum(shares, -1, keepdims=True)
            mean = dot_nn(shares.astype(B16), table_ref[...]) / total
            mean_s[rows, :width] = mean.astype(B16)
            mean_s[rows, width:] = split_lse(highest + jnp.log(total), block)
            return carry

        lax.fori_loop(0, ends[-1] // block, turn, 0)
        for out, first, last in zip(outs, ends[:-1], ends[1:]):
            out[...] = mean_s[first:last, :]

    return pl.pallas_call(
        body,
        in_specs=[VMEM] * (len(stacks) + 1),
        out_specs=[VMEM] * len(stacks),
        out_shape=[shape((stack.shape[0], width + LANES), B16) for stack in stacks],
        scratch_shapes=[
            pltpu.VMEM((ends[-1], width), B16),
            pltpu.VMEM((ends[-1], width + LANES), B16),
        ],
        cost_estimate=cost(10 * ends[-1] // 384),
        name="vocabulary",
    )(*stacks, table)


def joined_lse(block, width):
    return jnp.sum(block[:, width:].astype(F32)[:, 0:4], -1, keepdims=True)


def merge(firsts, seconds, last):
    wide = firsts[0].shape[1]
    width = wide - LANES
    count = len(firsts)
    pieces = 1 if last else 2
    begins = [0]
    for array in firsts:
        begins.append(begins[-1] + array.shape[0])

    def body(*refs):
        outs = refs[2 * count :]
        for part in range(count):
            first_ref, second_ref = refs[part], refs[count + part]
            rows = first_ref.shape[0] // pieces
            for piece in range(pieces):
                one = first_ref[piece * rows : (piece + 1) * rows, :]
                two = second_ref[piece * rows : (piece + 1) * rows, :]
                lse_one, lse_two = joined_lse(one, width), joined_lse(two, width)
                highest = jnp.maximum(lse_one, lse_two)
                scale_one, scale_two = jnp.exp(lse_one - highest), jnp.exp(lse_two - highest)
                total = scale_one + scale_two
                mean = one[:, :width].astype(F32) * (scale_one / total)
                mean = mean + two[:, :width].astype(F32) * (scale_two / total)
                if last:
                    out_ref = outs[0].at[begins[part] : begins[part + 1]]
                else:
                    out_ref = outs[piece * count + part]
                out_ref[:, :width] = mean.astype(B16)
                out_ref[:, width:] = split_lse(highest + jnp.log(total), rows)

    outs = pl.pallas_call(
        body,
        in_specs=[VMEM] * (2 * count),
        out_specs=[VMEM] * (1 if last else 2 * count),
        out_shape=[shape((begins[-1], wide), B16)]
        if last
        else [shape((a.shape[0] // 2, wide), B16) for a in firsts] * 2,
        cost_estimate=cost(3),
        name="merge",
    )(*firsts, *seconds)
    return (outs, None) if last else (outs[:count], outs[count:])


def head_rows_of(middle, own, other, vectors, core, cuts):
    scored, width = middle.shape
    core_rows = scored // 2
    sizes = [b - a for a, b in zip(cuts[:-1], cuts[1:])]

    def body(core_ref, middle_ref, own_ref, other_ref, vec_ref, rows_ref, in_ref, *parts):
        both = own_ref[...].astype(F32) + other_ref[...].astype(F32)
        rows = middle_ref[...] + (both + vec_ref[0:1, :])
        rows_ref[...] = rows
        xhat, unused = norm_rows(rows)
        normed = xhat * vec_ref[1:2, :] + vec_ref[2:3, :]
        in_ref[...] = normed.astype(B16)
        mine = jnp.where(core_ref[0] == 0, normed[:core_rows], normed[core_rows:]).astype(B16)
        for ref, first, last in zip(parts, cuts[:-1], cuts[1:]):
            ref[...] = mine[first:last]

    outs = pl.pallas_call(
        body,
        in_specs=[pl.BlockSpec(memory_space=pltpu.SMEM)] + [VMEM] * 4,
        out_specs=[VMEM] * (2 + len(sizes)),
        out_shape=[shape((scored, width), F32), shape((scored, width), B16)]
        + [shape((size, width), B16) for size in sizes],
        cost_estimate=cost(3),
        name="head_rows",
    )(core, middle, own, other, vectors)
    return outs[0], outs[1], outs[2:]


def head_back(own, other, head_rows, head_in, rows, skip, counted, final_norm, core, count_total):
    scored, width = head_rows.shape

    def body(core_ref, own_ref, other_ref, rows_ref, in_ref, target_ref, counted_ref, norm_ref,
             grad_ref, loss_ref):
        own_mean, other_mean = own_ref[...].astype(F32), other_ref[...].astype(F32)
        first = core_ref[0] == 0
        mean = jnp.concatenate(
            [jnp.where(first, own_mean, other_mean), jnp.where(first, other_mean, own_mean)], 0
        )
        lse = joined_lse(mean, width)
        target = target_ref[...]
        logit = jnp.sum(in_ref[...].astype(F32) * target, -1, keepdims=True)
        seen = counted_ref[...]
        loss_ref[...] = jnp.broadcast_to((lse - logit) * seen, (scored, LANES))
        d_head = (mean[:, :width] - target) * (seen / count_total)
        grad_ref[...] = norm_rows_back(d_head, rows_ref[...], norm_ref[0:1, :])

    return pl.pallas_call(
        body,
        grid_spec=pltpu.PrefetchScalarGridSpec(
            num_scalar_prefetch=1,
            grid=(1,),
            in_specs=[
                whole_spec(own.shape),
                whole_spec(other.shape),
                whole_spec(head_rows.shape),
                whole_spec(head_in.shape),
                pl.BlockSpec((scored, width), lambda i, *refs: (skip // scored, 0)),
                whole_spec(counted.shape),
                whole_spec(final_norm.shape),
            ],
            out_specs=[whole_spec((scored, width)), whole_spec((scored, LANES))],
        ),
        out_shape=[shape((scored, width), F32), shape((scored, LANES), F32)],
        compiler_params=params(),
        cost_estimate=cost(4),
        name="head_back",
    )(core, own, other, head_rows, head_in, rows, counted, final_norm)


def mlp_back(gradient, slope, me, w_up, w_down, residual=None):
    row_count, width = gradient.shape
    hidden = slope.shape[1]
    extra = [] if residual is None else list(residual)
    ups, downs = len(w_up.operands), len(w_down.operands)

    def body(me_ref, *refs):
        grad_ref, slope_ref = refs[0], refs[1]
        extra_refs = refs[2 : 2 + len(extra)]
        refs = refs[2 + len(extra) :]
        part_ref, *rest = refs[ups + downs :]
        up, up_sems, down, down_sems = rest[-4:]
        step = pl.program_id(0)
        up_refs = (me_ref[0], refs[:ups], up, up_sems)
        down_refs = (me_ref[0], refs[ups : ups + downs], down, down_sems)

        @pl.when(step == 0)
        def _():
            w_down.start(*down_refs)
            w_up.start(*up_refs)

        grad = grad_ref[...]
        if extra:
            stream_ref, gain_ref, own_ref, other_ref = extra_refs
            incoming = own_ref[...].astype(F32) + other_ref[...].astype(F32)
            grad = grad + norm_rows_back(incoming, stream_ref[...], gain_ref[...])
            rest[0][...] = grad

        @pl.when(step == 0)
        def _():
            w_down.wait(*down_refs)

        low = grad.astype(B16)
        total = None
        for first in range(0, hidden, PIECE):
            piece = slice(first, first + PIECE)
            d_active = dot_nn(low, down[:, piece])
            d_upward = (d_active * slope_ref[:, piece].astype(F32)).astype(B16)
            if first == 0:

                @pl.when(step == 0)
                def _():
                    w_up.wait(*up_refs)

            product = dot_nt(d_upward, up[:, piece])
            total = product if total is None else total + product
        part_ref[...] = total.astype(B16)

    extra_specs = (
        [rows_spec(width), whole_spec(extra[1].shape), rows_spec(width), rows_spec(width)]
        if extra
        else []
    )
    return pl.pallas_call(
        body,
        grid_spec=pltpu.PrefetchScalarGridSpec(
            num_scalar_prefetch=1,
            grid=(row_count // BLOCK,),
            in_specs=[rows_spec(width), rows_spec(hidden)] + extra_specs + w_up.specs + w_down.specs,
            out_specs=[rows_spec(width)] * (2 if extra else 1),
            scratch_shapes=w_up.scratch + w_down.scratch,
        ),
        out_shape=[shape((row_count, width), B16)]
        + ([shape((row_count, width), F32)] if extra else []),
        compiler_params=params(),
        cost_estimate=cost(20 * row_count // 1024),
        name="mlp_back",
    )(me, gradient, slope, *extra, *w_up.operands, *w_down.operands)


def last_attention_back(gradient, own, other, middle, gain, q, k, v, lse, prefix, layout, picks,
                        me, weight, plen):
    scored, width = gradient.shape
    row_count, half = k.shape
    prefix_rows = prefix.shape[1]
    scale = HEAD_DIM ** (-0.5)

    stacks = len(weight.operands)

    def body(me_ref, layout_ref, picks_ref, grad_ref, own_ref, other_ref, middle_ref, gain_ref,
             q_ref, k_ref, v_ref, lse_ref, prefix_ref, picks_row_ref, *refs):
        (part_ref, spread_ref, dprefix_ref, full, sems,
         dmix_s, lse_s, dq_s, dkv_s, sum_s, rows_s) = refs[stacks:]
        refs = (me_ref[0], refs[:stacks], full, sems)
        weight.start(*refs)
        incoming = own_ref[...].astype(F32) + other_ref[...].astype(F32)
        grad_mid = grad_ref[...] + norm_rows_back(incoming, middle_ref[...], gain_ref[...])
        rows_s[...] = grad_mid
        spread_ref[...] = jnp.zeros((row_count, width), F32)

        def put(index, carry):
            spread_ref[pl.ds(picks_ref[index], 1), :] = rows_s[pl.ds(index, 1), :]
            return carry

        lax.fori_loop(0, scored, put, 0, unroll=8)
        weight.wait(*refs)
        dmix_s[...] = dot_nn(grad_mid.astype(B16), full[:, 3 * half :]).astype(B16)
        bias = jnp.transpose(key_bias(layout_ref, jnp.transpose(picks_row_ref[...]), row_count))
        bias_prefix = jnp.where(
            lax.broadcasted_iota(jnp.int32, (prefix_rows, scored), 0) < plen, 0.0, NEG_BIG
        )
        lse_s[...] = jnp.transpose(lse_ref[...])

        def pair(index, carry):
            columns = pl.ds(pl.multiple_of(index * LANES, LANES), LANES)
            query, key, value = q_ref[:, columns], k_ref[:, columns], v_ref[:, columns]
            d_mixed = dmix_s[:, columns]
            key_p, value_p = prefix_ref[0, :, columns], prefix_ref[1, :, columns]
            found = [[], [], [], [], []]
            for side in range(2):
                cut = slice(side * HEAD_DIM, (side + 1) * HEAD_DIM)
                place = pl.multiple_of(prefix_rows * (2 * index + side), prefix_rows)
                log_total = lse_s[pl.ds(place, 1), :]
                qh, dh, kh, kp = query[:, cut], d_mixed[:, cut], key[:, cut], key_p[:, cut]
                shares = jnp.exp(dot_nt(kh, qh) + bias - log_total)
                shares_p = jnp.exp(dot_nt(kp, qh) + bias_prefix - log_total)
                d_shares = dot_nt(value[:, cut], dh).astype(B16).astype(F32)
                d_shares_p = dot_nt(value_p[:, cut], dh).astype(B16).astype(F32)
                inner = jnp.sum(shares * d_shares, 0, keepdims=True) + jnp.sum(
                    shares_p * d_shares_p, 0, keepdims=True
                )
                d_scores = (shares * (d_shares - inner)).astype(B16)
                d_scores_p = (shares_p * (d_shares_p - inner)).astype(B16)
                found[0].append((dot_tn(kh, d_scores) + dot_tn(kp, d_scores_p)) * scale)
                found[1].append(dot_nn(d_scores, qh))
                found[2].append(dot_nn(shares.astype(B16), dh))
                found[3].append(dot_nn(d_scores_p, qh))
                found[4].append(dot_nn(shares_p.astype(B16), dh))
            dq_s[columns, :] = jnp.concatenate(found[0], 0)
            joined = [jnp.concatenate(f, 1) for f in found[1:]]
            dkv_s[:, columns] = joined[0].astype(B16)
            dkv_s[:, pl.ds(pl.multiple_of(half + index * LANES, LANES), LANES)] = joined[1].astype(B16)
            dprefix_ref[0, :, columns] = joined[2]
            dprefix_ref[1, :, columns] = joined[3]
            return carry

        lax.fori_loop(0, half // LANES, pair, 0)
        sum_s[...] = dot_nt(dkv_s[...], full[:, half : 3 * half])
        rows_s[...] = dot_nt(jnp.transpose(dq_s[...]).astype(B16), full[:, :half])

        def add(index, carry):
            place = pl.ds(picks_ref[index], 1)
            sum_s[place, :] = sum_s[place, :] + rows_s[pl.ds(index, 1), :]
            return carry

        lax.fori_loop(0, scored, add, 0, unroll=8)
        part_ref[...] = sum_s[...].astype(B16)

    inputs = [gradient, own, other, middle, gain, q, k, v, lse, prefix, picks.reshape(1, scored)]
    return pl.pallas_call(
        body,
        grid_spec=pltpu.PrefetchScalarGridSpec(
            num_scalar_prefetch=3,
            grid=(1,),
            in_specs=[whole_spec(a.shape) for a in inputs] + weight.specs,
            out_specs=[
                whole_spec((row_count, width)),
                whole_spec((row_count, width)),
                whole_spec(prefix.shape),
            ],
            scratch_shapes=weight.scratch
            + [
                pltpu.VMEM((scored, half), B16),
                pltpu.VMEM((LANES, scored), F32),
                pltpu.VMEM((half, scored), F32),
                pltpu.VMEM((row_count, 2 * half), B16),
                pltpu.VMEM((row_count, width), F32),
                pltpu.VMEM((scored, width), F32),
            ],
        ),
        out_shape=[
            shape((row_count, width), B16),
            shape((row_count, width), F32),
            shape(prefix.shape, F32),
        ],
        compiler_params=params(),
        cost_estimate=cost(24),
        name="last_attention_back",
    )(me, layout, picks, *inputs, *weight.operands)


def first_prefix_back(gradient, own, other, middle, gain, q, mixed, lse, prefix, me, weight, plen):
    row_count, width = gradient.shape
    half = q.shape[1]
    prefix_rows = prefix.shape[1]
    lanes = half // HEAD_DIM * prefix_rows
    stacks = len(weight.operands)

    def own_head(dims, lane_axis):
        lane = lax.broadcasted_iota(jnp.int32, dims, lane_axis)
        column = lax.broadcasted_iota(jnp.int32, dims, 1 - lane_axis)
        return lane // prefix_rows == column // HEAD_DIM

    def body(me_ref, grad_ref, own_ref, other_ref, middle_ref, gain_ref, q_ref, mixed_ref,
             lse_ref, prefix_ref, *refs):
        dprefix_ref, full, sems, spread_s, sum_s = refs[stacks:]
        step = pl.program_id(0)
        refs = (me_ref[0], refs[:stacks], full, sems)

        @pl.when(step == 0)
        def _():
            weight.start(*refs)
            sum_s[...] = jnp.zeros(sum_s.shape, F32)
            for c in range(2):
                tiled = jnp.concatenate([prefix_ref[c]] * (lanes // prefix_rows), 0)
                spread_s[c] = jnp.where(
                    own_head((lanes, half), 0), tiled.astype(F32), 0.0
                ).astype(B16)
            spread_s[2] = jnp.where(own_head((lanes, half), 0), 1.0, 0.0).astype(B16)

        incoming = own_ref[...].astype(F32) + other_ref[...].astype(F32)
        grad_mid = grad_ref[...] + norm_rows_back(incoming, middle_ref[...], gain_ref[...])

        @pl.when(step == 0)
        def _():
            weight.wait(*refs)

        d_mixed = dot_nn(grad_mid.astype(B16), full[...]).astype(B16)
        product = d_mixed.astype(F32) * mixed_ref[...].astype(F32)
        high = product.astype(B16)
        low = (product - high.astype(F32)).astype(B16)
        inner = dot_nt(high, spread_s[2]) + dot_nt(low, spread_s[2])
        lane = lax.broadcasted_iota(jnp.int32, (BLOCK, lanes), 1)
        shares = jnp.exp(dot_nt(q_ref[...], spread_s[0]) - lse_ref[:, :lanes])
        shares = jnp.where(lane % prefix_rows < plen, shares, 0.0)
        d_shares = dot_nt(d_mixed, spread_s[1]).astype(B16).astype(F32)
        d_scores = (shares * (d_shares - inner)).astype(B16)
        sum_s[0] += dot_tn(d_scores, q_ref[...])
        sum_s[1] += dot_tn(shares.astype(B16), d_mixed)

        @pl.when(step == row_count // BLOCK - 1)
        def _():
            for c in range(2):
                held = jnp.where(own_head((lanes, half), 0), sum_s[c], 0.0)
                total = held[:prefix_rows]
                for first in range(prefix_rows, lanes, prefix_rows):
                    total = total + held[first : first + prefix_rows]
                dprefix_ref[c] = total

    return pl.pallas_call(
        body,
        grid_spec=pltpu.PrefetchScalarGridSpec(
            num_scalar_prefetch=1,
            grid=(row_count // BLOCK,),
            in_specs=[
                rows_spec(width),
                rows_spec(width),
                rows_spec(width),
                rows_spec(width),
                whole_spec(gain.shape),
                rows_spec(half),
                rows_spec(half),
                rows_spec(LANES),
                whole_spec(prefix.shape),
                *weight.specs,
            ],
            out_specs=whole_spec(prefix.shape),
            scratch_shapes=weight.scratch
            + [pltpu.VMEM((3, lanes, half), B16), pltpu.VMEM((2, lanes, half), F32)],
        ),
        out_shape=shape(prefix.shape, F32),
        compiler_params=params(),
        cost_estimate=cost(11),
        name="first_prefix_back",
    )(me, gradient, own, other, middle, gain, q, mixed, lse, prefix, *weight.operands)


class TableRows:
    def __init__(self, ids, table):
        count = ids.shape[0]
        shard_rows = table.shape[0]
        ta_size = lax.axis_size("ta")
        shard = ids // shard_rows
        self.table = table
        self.inside = ids % shard_rows
        self.owner = shard // ta_size
        order = jnp.arange(count, dtype=jnp.int32)
        same = ids[:, None] == ids[None, :]
        first = jnp.min(jnp.where(same, order[None], count), 1)
        is_first = first == order
        earlier = is_first[None] & (shard[None] == shard[:, None]) & (order[None] < first[:, None])
        self.rank = jnp.sum(earlier.astype(jnp.int32), 1)
        self.mine = shard % ta_size == lax.axis_index("ta")
        self.need = jnp.max(jnp.where(self.mine, self.rank, 0)) // SLOT_ROWS + 1
        self.per_core = lax.axis_size("dev") * SLOT_ROWS

    def slot(self, turn):
        rank = self.rank - turn * SLOT_ROWS
        used = (rank >= 0) & (rank < SLOT_ROWS)
        slot = self.owner * SLOT_ROWS + rank + jnp.where(self.mine, 0, self.per_core)
        return jnp.where(used, slot, -1)

    def ask(self, turn):
        slots = jnp.arange(self.per_core, dtype=jnp.int32)
        found = self.slot(turn)[None] == slots[:, None]
        asked = jnp.max(jnp.where(found, self.inside[None], 0), 1).reshape(-1, SLOT_ROWS)
        header = jnp.broadcast_to(self.need, (asked.shape[0], 1))
        return lax.all_to_all(jnp.concatenate([asked, header], 1), "dev", 0, 0)

    def answer(self, wanted):
        numbers = jnp.arange(self.table.shape[0], dtype=jnp.int32)
        pick = (wanted[:, :SLOT_ROWS].reshape(-1, 1) == numbers[None]).astype(B16)
        sent = jnp.dot(pick, self.table, preferred_element_type=F32).astype(B16)
        return sent.reshape(-1, SLOT_ROWS, self.table.shape[1])

    def fetch(self, sent):
        got = lax.all_to_all(sent, "dev", 0, 0)
        return got.reshape(self.per_core, self.table.shape[1])

    def place(self, turn, got):
        slots = jnp.arange(2 * self.per_core, dtype=jnp.int32)
        spread = (self.slot(turn)[:, None] == slots[None]).astype(B16)
        both = jnp.concatenate([got, partner(got)], 0)
        return jnp.dot(spread, both, preferred_element_type=F32)

    def finish(self, base, wanted, got):
        most = jnp.max(wanted[:, SLOT_ROWS])
        most = jnp.maximum(most, partner(most.reshape(1, 1))[0, 0])

        def again(state):
            return state[0] < most

        def turn(state):
            got = self.fetch(self.answer(self.ask(state[0])))
            return (state[0] + 1, state[1] + self.place(state[0], got))

        return lax.while_loop(again, turn, (jnp.int32(1), base + self.place(0, got)))[1]


def adamw_update(weight, moment, square, gradient, corr_one, corr_two):
    moment = BETA_ONE * moment + (1.0 - BETA_ONE) * gradient
    square = BETA_TWO * square + (1.0 - BETA_TWO) * gradient * gradient
    weight = weight - LEARN_RATE * (
        moment / corr_one / (jnp.sqrt(square / corr_two) + ADAM_EPS) + DECAY_RATE * weight
    )
    return (weight, moment, square)


def local(
    token_ids,
    bucket,
    seq_lengths,
    loss_pos,
    targets,
    wte,
    wpe,
    w_qkv,
    w_out,
    w_fc,
    w_proj,
    frozen_vec,
    fc_bias,
    final_norm,
    prefix_table,
    inner_weight,
    inner_bias,
    outer_weight,
    outer_bias,
    moment_prefix,
    square_prefix,
    moment_inner,
    square_inner,
    moment_inner_bias,
    square_inner_bias,
    moment_outer,
    square_outer,
    moment_outer_bias,
    square_outer_bias,
):
    row_count = token_ids.shape[0]
    scored = loss_pos.shape[0]
    width = wte.shape[1]
    half = w_qkv.shape[3]
    size = lax.axis_size("dev")
    own_index = lax.axis_index("ta")
    plen = prefix_table.shape[0]
    prefix_rows = 16
    me = lax.axis_index("dev").astype(jnp.int32).reshape(1)
    orders = (bit_orders(size, 3), bit_orders(size, 4))
    stages = len(orders[0][0])
    bucket_width = bucket[0]
    shift = jnp.where(bucket_width == 256, 8, 10).astype(jnp.int32)
    layout = jnp.concatenate([shift.reshape(1), bucket_width.reshape(1), seq_lengths[0]])

    rounds = Rounds()
    ff = w_fc.shape[2]
    totals = (4 * half, 2 * ff)
    cuts = [[cuts_of(total, LANES, len(order)) for total in totals] for order in orders]

    def add_layer(layer_id, qkv, out, fc, proj):
        sides = (
            jnp.concatenate([qkv[c] for c in range(3)] + [out.T], 1),
            jnp.concatenate([fc, proj.T], 1),
        )
        parts = [
            [
                rows[:, c[p] : c[p + 1]]
                for rows, c in zip(sides, cuts[layer_id])
            ]
            for p in range(len(orders[layer_id]))
        ]
        rounds.add(
            layer_id,
            orders[layer_id],
            [jnp.concatenate(part, 1) for part in parts],
            [part[0].shape[1] for part in parts],
        )

    def weight(layer_id, side, first, last):
        segments = [
            (rounds.held[layer_id, p, side], order, cuts[layer_id][side][p])
            for p, order in enumerate(orders[layer_id])
        ]
        return Gathered(segments, first, last)

    def attention_weight(layer_id, first=0):
        return weight(layer_id, 0, first * half, 4 * half)

    def mlp_weights(layer_id):
        return weight(layer_id, 1, 0, ff), weight(layer_id, 1, ff, 2 * ff)

    def head_bias(layer_id):
        part = lax.dynamic_slice_in_dim(frozen_vec[layer_id, 4:7], own_index * half, half, 1)
        return part.reshape(1, 3 * half)

    add_layer(0, w_qkv[0], w_out[0], w_fc[0], w_proj[0])
    ids, prefix_in = rounds.step(
        0,
        0,
        through=(
            (token_ids, targets),
            (prefix_table, inner_weight, inner_bias, outer_weight),
        ),
    )
    lookup = TableRows(jnp.concatenate(ids), wte)
    wanted = lookup.ask(0)
    hidden = jnp.tanh(jnp.dot(prefix_in[0], prefix_in[1], precision=HIGHEST) + prefix_in[2])
    sums = jnp.einsum("pr,rlcd->lcpd", hidden, prefix_in[3], precision=HIGHEST)
    for stage in range(stages - 2):
        sums = sums + flip(sums, 1 << stage)

    wanted, sums = rounds.step(0, 1, through=(wanted, sums))
    sent = lookup.answer(wanted)
    sums = sums + flip(sums, 1 << (stages - 2))
    for stage in range(2, stages - 2):
        rounds.step(0, stage)

    sent, wanted, sums, last_layer = rounds.step(
        0,
        stages - 2,
        through=(sent, wanted, sums, (w_qkv[1], w_out[1], w_fc[1], w_proj[1])),
    )
    got = lookup.fetch(sent)
    add_layer(1, *last_layer)
    sums = sums + flip(sums, 1 << (stages - 1))
    prefix_kv = (sums + outer_bias[:, :, None, :]).astype(B16)
    prefix_kv = jnp.pad(prefix_kv, ((0, 0), (0, 0), (0, prefix_rows - plen), (0, 0)))

    got, wanted, places, prefix_kv, next_rows = rounds.step(
        0,
        stages - 1,
        0,
        through=(got, wanted, wpe, prefix_kv, [rounds.held[1, p][0] for p in range(len(orders[1]))]),
    )
    for part, array in enumerate(next_rows):
        rounds.held[1, part] = [array]
    repeat = row_count // 256
    places = jnp.where(bucket_width == 256, jnp.tile(places[:256], (repeat, 1)), places[:row_count])
    places = jnp.concatenate([places, jnp.zeros((scored, width), places.dtype)], 0)
    stream = lookup.finish(places.astype(F32), wanted, got)

    stream = rounds.step(0, stages - 1, 1, through=stream)
    part, q0, mixed0, lse0 = first_attention(
        stream,
        row_count,
        frozen_vec[0, 0:2],
        head_bias(0),
        prefix_kv[0],
        layout,
        me,
        attention_weight(0),
        plen,
    )

    part = rounds.step(1, 0, through=part)
    other = partner(part)

    part, other = rounds.step(1, 1, through=(part, other))
    vec = frozen_vec[0]
    part_two, middle0, slope0 = mlp(
        stream,
        part,
        other,
        jnp.stack([vec[7], vec[2], vec[3]]),
        fc_bias[0:1],
        me,
        *mlp_weights(0),
    )

    part_two, table = rounds.step(1, 2, through=(part_two, wte))
    other = partner(part_two)
    entries = wte.shape[0]
    table_half = -(-entries // 64) * 64
    table = jnp.pad(table, ((0, table_half - entries), (0, 0)))
    for stage in range(3, stages - 1):
        rounds.step(1, stage)

    table, part_two, other = rounds.step(1, stages - 1, 0, through=(table, part_two, other))
    table = jnp.concatenate([table, partner(table)], 0)

    part_two, other, table = rounds.step(1, stages - 1, 1, through=(part_two, other, table))

    vec_last = frozen_vec[1]
    picks_column = loss_pos.reshape(scored, 1)
    stream1, part, k1, v1, q1, mixed1, lse1, chosen = last_attention(
        middle0,
        part_two,
        other,
        jnp.stack([vec[8], vec_last[0], vec_last[1]]),
        head_bias(1),
        prefix_kv[1],
        layout,
        loss_pos,
        picks_column,
        me,
        attention_weight(1),
        plen,
    )
    part_two, middle1, slope1 = mlp(
        chosen,
        part,
        partner(part),
        jnp.stack([vec_last[7], vec_last[2], vec_last[3]]),
        fc_bias[1:2],
        me,
        *mlp_weights(1),
    )
    core = own_index.astype(jnp.int32).reshape(1)
    cuts_head = (0, 48, 96, scored // 2)
    head_rows, head_in, mine = head_rows_of(
        middle1,
        part_two,
        partner(part_two),
        jnp.stack([vec_last[8], final_norm[0], final_norm[1]]),
        core,
        cuts_head,
    )

    head_order = bit_orders(size, 3)
    head = Rounds()
    head.add(0, head_order, mine)
    for stage in range(stages):
        head.step(0, stage)
    near, far = [
        [head.held[0, p][side].reshape(-1, width) for p in range(len(head_order))]
        for side in range(2)
    ]
    keep = vocabulary(near[:1], table, entries)
    far, keep, near = lax.optimization_barrier((far, keep, near))
    send = vocabulary(far, table, entries)
    keep = list(keep) + list(vocabulary(near[1:], table, entries))
    for stage in reversed(range(stages)):
        got = [flip(array, head_order[p][stage]) for p, array in enumerate(send)]
        keep, send = merge(keep, got, stage == 0)
    (own_means,) = keep
    other_means = partner(own_means)
    place = loss_pos % bucket_width
    slot = loss_pos // bucket_width
    lengths = jnp.sum(
        jnp.where(
            slot[:, None] == jnp.arange(seq_lengths.shape[1], dtype=jnp.int32)[None],
            seq_lengths[0][None],
            0,
        ),
        1,
    )
    counted = (place < lengths).astype(F32).reshape(scored, 1)
    count_total = float(scored * size)
    grad_rows, loss_terms = head_back(
        own_means,
        other_means,
        head_rows,
        head_in,
        stream,
        row_count,
        counted,
        final_norm,
        core,
        count_total,
    )
    loss_part = jnp.sum(loss_terms[:, 0])

    (part,) = mlp_back(grad_rows, slope1, me, *mlp_weights(1))
    part, spread_grad, d_prefix1 = last_attention_back(
        grad_rows,
        part,
        partner(part),
        middle1,
        vec_last[2:3],
        q1,
        k1,
        v1,
        lse1,
        prefix_kv[1],
        layout,
        loss_pos,
        me,
        attention_weight(1),
        plen,
    )
    part, grad_stream = mlp_back(
        spread_grad,
        slope0,
        me,
        *mlp_weights(0),
        (stream1, vec_last[0:1], part, partner(part)),
    )
    d_prefix0 = first_prefix_back(
        grad_stream,
        part,
        partner(part),
        middle0,
        vec[2:3],
        q0,
        mixed0,
        lse0,
        prefix_kv[0],
        me,
        attention_weight(0, 3),
        plen,
    )
    d_prefix = sum_over_dev(jnp.stack([d_prefix0, d_prefix1])[:, :, :plen])

    d_outer = jnp.einsum("pr,lcpd->rlcd", hidden, d_prefix, precision=HIGHEST)
    d_outer_bias = jnp.sum(d_prefix, 2)
    hidden_part = jnp.einsum("lcpd,rlcd->pr", d_prefix, outer_weight, precision=HIGHEST)
    outer_square = jnp.sum(d_outer * d_outer) + jnp.sum(d_outer_bias * d_outer_bias) / size
    over_ta = jnp.concatenate(
        [hidden_part, jnp.broadcast_to(outer_square, (1, hidden_part.shape[1]))], 0
    )
    over_ta = over_ta + partner(over_ta)
    d_hidden = over_ta[:plen]
    d_pre = d_hidden * (1.0 - hidden * hidden)
    d_inner = jnp.dot(prefix_table.T, d_pre, precision=HIGHEST)
    d_inner_bias = jnp.sum(d_pre, 0)
    table_part = jnp.dot(d_pre, inner_weight.T, precision=HIGHEST)
    squares = over_ta[plen, 0] + jnp.sum(d_inner * d_inner) + jnp.sum(d_inner_bias * d_inner_bias)
    lane = jnp.arange(table_part.shape[1], dtype=jnp.int32)
    last_row = jnp.where(lane == 0, squares, jnp.where(lane == 1, loss_part, 0.0))
    totals = sum_over_dev(jnp.concatenate([table_part, last_row[None]], 0))
    d_table = totals[:plen]
    square_sum = totals[plen, 0]
    loss_value = totals[plen, 1] / count_total
    grad_total = jnp.sqrt(square_sum + jnp.sum(d_table * d_table))
    factor = jnp.minimum(1.0, CLIP_NORM / (grad_total + 1e-06))
    corr_one = 1.0 - BETA_ONE**adam_steps
    corr_two = 1.0 - BETA_TWO**adam_steps
    prefix_out = adamw_update(
        prefix_table, moment_prefix, square_prefix, factor * d_table, corr_one, corr_two
    )
    inner_out = adamw_update(
        inner_weight, moment_inner, square_inner, factor * d_inner, corr_one, corr_two
    )
    ibias_out = adamw_update(
        inner_bias, moment_inner_bias, square_inner_bias, factor * d_inner_bias, corr_one, corr_two
    )
    d_outer = with_layout_constraint(d_outer, Layout(major_to_minor=(0, 1, 2, 3)))
    outer_out = adamw_update(
        outer_weight, moment_outer, square_outer, factor * d_outer, corr_one, corr_two
    )
    obias_out = adamw_update(
        outer_bias, moment_outer_bias, square_outer_bias, factor * d_outer_bias, corr_one, corr_two
    )
    return (
        loss_value.reshape(1),
        grad_total.reshape(1),
        prefix_out[0],
        prefix_out[1],
        prefix_out[2],
        inner_out[0],
        inner_out[1],
        inner_out[2],
        ibias_out[0],
        ibias_out[1],
        ibias_out[2],
        outer_out[0],
        outer_out[1],
        outer_out[2],
        obias_out[0],
        obias_out[1],
        obias_out[2],
        prefix_out[0].astype(B16),
        inner_out[0].astype(B16),
        ibias_out[0].astype(B16),
        outer_out[0].astype(B16),
        obias_out[0].astype(B16),
    )


def solution(mesh):
    in_specs = (
        P("dev"),
        P("dev"),
        P("dev", None),
        P("dev"),
        P("dev"),
        P(("dev", "ta"), None),
        P(),
        P(None, None, "dev", "ta"),
        P(None, "ta", "dev"),
        P(None, "dev", "ta"),
        P(None, "ta", "dev"),
        P(),
        P(None, "ta"),
        P(),
        P(),
        P(None, "dev"),
        P("dev"),
        P("dev", None, None, "ta"),
        P(None, None, "ta"),
        P(),
        P(),
        P(None, "dev"),
        P(None, "dev"),
        P("dev"),
        P("dev"),
        P("dev", None, None, "ta"),
        P("dev", None, None, "ta"),
        P(None, None, "ta"),
        P(None, None, "ta"),
    )
    out_specs = (
        P(),
        P(),
        P(),
        P(),
        P(),
        P(None, "dev"),
        P(None, "dev"),
        P(None, "dev"),
        P("dev"),
        P("dev"),
        P("dev"),
        P("dev", None, None, "ta"),
        P("dev", None, None, "ta"),
        P("dev", None, None, "ta"),
        P(None, None, "ta"),
        P(None, None, "ta"),
        P(None, None, "ta"),
        P(),
        P(None, "dev"),
        P("dev"),
        P("dev", None, None, "ta"),
        P(None, None, "ta"),
    )
    return jax.shard_map(local, mesh=mesh, in_specs=in_specs, out_specs=out_specs, check_vma=False)
```

```python
import functools

import jax
import jax.numpy as jnp
from jax import lax
from jax.experimental import pallas as pl
from jax.experimental.layout import Layout, with_layout_constraint
from jax.experimental.pallas import tpu as pltpu
from jax.sharding import PartitionSpec as P

HEAD_DIM = 64


EPS_NORM = 1e-05
CLIP_NORM = 0.001
LEARN_RATE = 0.02
BETA_ONE = 0.9
BETA_TWO = 0.999
ADAM_EPS = 1e-08
DECAY_RATE = 0.01
adam_steps = 10.0
NEG_BIG = -1e30
HIGHEST = lax.Precision.HIGHEST
F32 = jnp.float32
B16 = jnp.bfloat16
GELU_SCALE = 0.7978845608028654
GELU_CUBE = 0.044715
SLOT_ROWS = 48
BLOCK = 256
LANES = 128
PIECE = 2048
SWAP = [(0, 1), (1, 0)]


def shape(dims, dtype):
    return jax.ShapeDtypeStruct(dims, dtype)


def params(mebibytes, grid=True):
    return pltpu.CompilerParams(
        dimension_semantics=("arbitrary",) if grid else None, vmem_limit_bytes=mebibytes << 20
    )


def cost(microseconds):
    return pl.CostEstimate(
        flops=int(microseconds * 1.15e9), transcendentals=0, bytes_accessed=1024
    )


def flip(array, bit):
    size = lax.axis_size("dev")
    return lax.ppermute(array, "dev", [(i, i ^ bit) for i in range(size)])


def partner(array):
    return lax.ppermute(array, "ta", SWAP)


def bit_orders(size, parts):
    bits = [1 << k for k in range(size.bit_length() - 1)]
    if size == 16:
        x, y, near, far = bits
        if parts == 3:
            return ((far, y, near, x), (near, far, x, y), (far, x, y, near))
        return (
            (x, y, near, far),
            (x, y, far, near),
            (near, far, x, y),
            (far, near, y, x),
        )
    return tuple(tuple(bits[k:] + bits[:k]) for k in range(parts))


def cuts_of(total, unit, parts):
    sixths = (0, 2, 4) if parts == 3 else (0, 1, 2, 4)
    return [total * k // 6 // unit * unit for k in sixths] + [total]


def pack(groups):
    arrays = [array for group, unused, unused in groups for array in group]
    outs = []
    moves = []
    for number, (group, first, last) in enumerate(groups):
        total = 0
        for array in group:
            moves.append((number, total, array.shape[0], first, last - first))
            total += array.shape[0]
        outs.append(shape((total, group[0].shape[1], last - first), group[0].dtype))

    def body(*refs):
        sems = refs[-1]
        copies = [
            pltpu.make_async_copy(
                refs[index].at[:, :, pl.ds(first, wide)],
                refs[len(arrays) + number].at[pl.ds(begin, count)],
                sems.at[index],
            )
            for index, (number, begin, count, first, wide) in enumerate(moves)
        ]
        for copy in copies:
            copy.start()
        for copy in copies:
            copy.wait()

    return pl.pallas_call(
        body,
        in_specs=[pl.BlockSpec(memory_space=pl.ANY)] * len(arrays),
        out_specs=[pl.BlockSpec(memory_space=pltpu.VMEM)] * len(outs),
        out_shape=outs,
        scratch_shapes=[pltpu.SemaphoreType.DMA((len(arrays),))],
        compiler_params=params(20, False),
        cost_estimate=cost(2),
        name="pack",
    )(*arrays)


class Rounds:
    def __init__(self):
        self.orders = {}
        self.held = {}
        self.split = {}
        self.before = []

    def add(self, chunk, orders, arrays, splits=None):
        self.orders[chunk] = orders
        for part, array in enumerate(arrays):
            self.held[chunk, part] = [array[None]]
            self.split[chunk, part] = splits[part] if splits else None

    def step(self, chunk, stage, side=None, through=()):
        parts = range(len(self.orders[chunk]))
        held = [self.held[chunk, part] for part in parts]
        if stage == 0:
            sends = [arrays[0] for arrays in held]
        else:
            spans = []
            for part, arrays in zip(parts, held):
                cut, width = self.split[chunk, part], arrays[0].shape[2]
                spans.append((cut if side == 1 else 0, cut if side == 0 else width))
            sends = pack([(arrays, *span) for arrays, span in zip(held, spans)])
        through, sends, unused = lax.optimization_barrier((through, sends, self.before))
        self.before = []
        for part, send in enumerate(sends):
            got = flip(send, self.orders[chunk][part][stage])
            self.held[(chunk, part) if side is None else (chunk, part, side)] = [send, got]
            self.before.append(got)
        return through


def sum_over_dev(array):
    size = lax.axis_size("dev")
    bit = 1
    while bit < size:
        if bit * 2 < size:
            near, far, both = flip(array, bit), flip(array, bit * 2), flip(array, bit * 3)
            array = (array + near) + (far + both)
        else:
            array = array + flip(array, bit)
        bit = bit * 4
    return array


def norm_rows(x):
    center = x - jnp.mean(x, -1, keepdims=True)
    scale = lax.rsqrt(jnp.mean(center * center, -1, keepdims=True) + EPS_NORM)
    return center * scale, scale


def norm_rows_back(gradient, x, gain):
    xhat, scale = norm_rows(x)
    e2 = gradient * gain
    mean_one = jnp.mean(e2, -1, keepdims=True)
    mean_two = jnp.mean(e2 * xhat, -1, keepdims=True)
    return (e2 - mean_one - xhat * mean_two) * scale


def dot_nn(a, b):
    return lax.dot_general(a, b, (((1,), (0,)), ((), ())), preferred_element_type=F32)


def dot_nt(a, b):
    return lax.dot_general(a, b, (((1,), (1,)), ((), ())), preferred_element_type=F32)


def dot_tn(a, b):
    return lax.dot_general(a, b, (((0,), (0,)), ((), ())), preferred_element_type=F32)


class Gathered:
    def __init__(self, segments, first, last):
        self.pieces = []
        for stacks, order, begin in segments:
            low, high = max(first, begin), min(last, begin + stacks[0].shape[2])
            if low < high:
                self.pieces.append((stacks, order, low - begin, high - low, low - first))
        stacks, order, *unused = self.pieces[0]
        self.rows = stacks[0].shape[1]
        self.blocks = 1 << len(order)
        self.scratch = [
            pltpu.VMEM((self.blocks * self.rows, last - first), B16),
            pltpu.SemaphoreType.DMA((len(self.pieces) * self.blocks,)),
        ]
        self.operands = [array for piece in self.pieces for array in piece[0]]
        self.specs = [pl.BlockSpec(memory_space=pl.ANY)] * len(self.operands)

    def each(self, act, me, refs, full, sems):
        for number, (stacks, order, source, wide, target) in enumerate(self.pieces):
            blocks = self.blocks // len(stacks)
            for side, ref in enumerate(refs[number * len(stacks) : (number + 1) * len(stacks)]):

                def one(index, carry, side=side, ref=ref):
                    place = me ^ (order[-1] if side else 0)
                    for k, bit in enumerate(order[:-1]):
                        place = place ^ jnp.where((index >> k) % 2 == 1, bit, 0)
                    start = pl.multiple_of(place * self.rows, self.rows)
                    copy = pltpu.make_async_copy(
                        ref.at[index, :, pl.ds(source, wide)],
                        full.at[pl.ds(start, self.rows), pl.ds(target, wide)],
                        sems.at[number * self.blocks + side * blocks + index],
                    )
                    act(copy)
                    return carry

                lax.fori_loop(0, blocks, one, 0)

    def start(self, *refs):
        self.each(lambda copy: copy.start(), *refs)

    def wait(self, *refs):
        self.each(lambda copy: copy.wait(), *refs)


def rows_spec(width, block=BLOCK):
    return pl.BlockSpec((block, width), lambda i, *refs: (i, 0))


def whole_spec(dims):
    return pl.BlockSpec(dims, lambda i, *refs: (0,) * len(dims))


def key_bias(layout_ref, query_pos, key_count):
    shift = layout_ref[0]
    dims = (query_pos.shape[0], key_count)
    key_pos = lax.broadcasted_iota(jnp.int32, (1, key_count), 1)
    key_seg = lax.shift_right_logical(key_pos, jnp.full((1, key_count), shift, jnp.int32))
    query_seg = lax.shift_right_logical(query_pos, jnp.full(query_pos.shape, shift, jnp.int32))
    length = jnp.zeros((1, key_count), jnp.int32)
    for slot in range(layout_ref.shape[0] - 2):
        length = jnp.where(key_seg == slot, layout_ref[2 + slot], length)
    place = key_pos - key_seg * layout_ref[1]
    key_seg = jnp.where(place < length, key_seg, -1)
    seen = (jnp.broadcast_to(query_seg, dims) == jnp.broadcast_to(key_seg, dims)) & (
        jnp.broadcast_to(key_pos, dims) <= jnp.broadcast_to(query_pos, dims)
    )
    return jnp.where(seen, 0.0, NEG_BIG)


def prefix_bias(rows, prefix_rows, prefix_len):
    lane = lax.broadcasted_iota(jnp.int32, (rows, prefix_rows), 1)
    return jnp.where(lane < prefix_len, 0.0, NEG_BIG)


def attend(query, key, value, key_prefix, value_prefix, bias, bias_prefix):
    scores = dot_nt(query, key) + bias
    scores_prefix = dot_nt(query, key_prefix) + bias_prefix
    highest = jnp.maximum(
        jnp.max(scores, -1, keepdims=True), jnp.max(scores_prefix, -1, keepdims=True)
    )
    shares = jnp.exp(scores - highest)
    shares_prefix = jnp.exp(scores_prefix - highest)
    total = jnp.sum(shares, -1, keepdims=True) + jnp.sum(shares_prefix, -1, keepdims=True)
    mixed = dot_nn(shares.astype(B16), value) + dot_nn(shares_prefix.astype(B16), value_prefix)
    return mixed / total, highest + jnp.log(total)


def attend_pairs(q_ref, k_ref, v_ref, prefix_ref, mixed_ref, lse_ref, rows, key_count, bias, plen):
    prefix_rows = prefix_ref.shape[1]
    bias_prefix = prefix_bias(BLOCK, prefix_rows, plen)
    lse_ref[rows, :] = jnp.zeros((BLOCK, LANES), F32)
    lane = lax.broadcasted_iota(jnp.int32, (BLOCK, LANES), 1)

    def pair(index, carry):
        columns = pl.ds(pl.multiple_of(index * LANES, LANES), LANES)
        query = q_ref[rows, columns]
        key = k_ref[pl.ds(0, key_count), columns]
        value = v_ref[pl.ds(0, key_count), columns]
        key_prefix = prefix_ref[0, :, columns]
        value_prefix = prefix_ref[1, :, columns]
        parts = []
        for side in range(2):
            cut = slice(side * HEAD_DIM, (side + 1) * HEAD_DIM)
            mixed, lse = attend(
                query[:, cut],
                key[:, cut],
                value[:, cut],
                key_prefix[:, cut],
                value_prefix[:, cut],
                bias,
                bias_prefix,
            )
            parts.append(mixed)
            lse_ref[rows, :] = jnp.where(
                lane // prefix_rows == 2 * index + side, lse, lse_ref[rows, :]
            )
        mixed_ref[rows, columns] = jnp.concatenate(parts, 1).astype(B16)
        return carry

    lax.fori_loop(0, q_ref.shape[1] // LANES, pair, 0)


def first_attention(stream, row_count, vectors, bias_qkv, prefix, layout, me, weight, plen):
    width = stream.shape[1]
    half = prefix.shape[2]
    scale = HEAD_DIM ** (-0.5)

    stacks = len(weight.operands)

    def body(me_ref, layout_ref, stream_ref, vec_ref, bias_ref, prefix_ref, *refs):
        part_ref, q_out, mixed_out, lse_out, full, sems, q_s, k_s, v_s = refs[stacks:]
        step = pl.program_id(0)
        refs = (me_ref[0], refs[:stacks], full, sems)

        @pl.when(step == 0)
        def _():
            weight.start(*refs)
            weight.wait(*refs)

        xhat, unused = norm_rows(stream_ref[...])
        normed = (xhat * vec_ref[0:1, :] + vec_ref[1:2, :]).astype(B16)
        qkv = dot_nn(normed, full[:, : 3 * half]) + bias_ref[...]
        rows = pl.ds(pl.multiple_of(step * BLOCK, BLOCK), BLOCK)
        q_s[...] = (qkv[:, :half].astype(B16) * scale).astype(B16)
        k_s[rows, :] = qkv[:, half : 2 * half].astype(B16)
        v_s[rows, :] = qkv[:, 2 * half :].astype(B16)
        q_out[...] = q_s[...]
        local_pos = lax.broadcasted_iota(jnp.int32, (BLOCK, 1), 0)
        for case in range(row_count // BLOCK):

            @pl.when(step == case)
            def _(case=case):
                key_count = (case + 1) * BLOCK
                bias = key_bias(layout_ref, local_pos + case * BLOCK, key_count)
                attend_pairs(
                    q_s, k_s, v_s, prefix_ref, mixed_out, lse_out,
                    pl.ds(0, BLOCK), key_count, bias, plen,
                )

        part_ref[...] = dot_nt(mixed_out[...], full[:, 3 * half :]).astype(B16)

    return pl.pallas_call(
        body,
        grid_spec=pltpu.PrefetchScalarGridSpec(
            num_scalar_prefetch=2,
            grid=(row_count // BLOCK,),
            in_specs=[
                rows_spec(width),
                whole_spec(vectors.shape),
                whole_spec(bias_qkv.shape),
                whole_spec(prefix.shape),
                *weight.specs,
            ],
            out_specs=[rows_spec(width), rows_spec(half), rows_spec(half), rows_spec(LANES)],
            scratch_shapes=weight.scratch
            + [pltpu.VMEM((BLOCK, half), B16)]
            + [pltpu.VMEM((row_count, half), B16)] * 2,
        ),
        out_shape=[
            shape((row_count, width), B16),
            shape((row_count, half), B16),
            shape((row_count, half), B16),
            shape((row_count, LANES), F32),
        ],
        compiler_params=params(32),
        cost_estimate=cost(30 * row_count // 1024),
        name="first_attention",
    )(me, layout, stream, vectors, bias_qkv, prefix, *weight.operands)


def mlp(base, own, other, vectors, bias_up, me, w_up, w_down):
    row_count, width = own.shape
    hidden = bias_up.shape[1]

    ups, downs = len(w_up.operands), len(w_down.operands)

    def body(me_ref, base_ref, own_ref, other_ref, vec_ref, bias_ref, *refs):
        part_ref, middle_ref, slope_ref, up, up_sems, down, down_sems = refs[ups + downs :]
        step = pl.program_id(0)
        up_refs = (me_ref[0], refs[:ups], up, up_sems)
        down_refs = (me_ref[0], refs[ups : ups + downs], down, down_sems)

        @pl.when(step == 0)
        def _():
            w_up.start(*up_refs)
            w_down.start(*down_refs)

        middle = base_ref[...] + (
            (own_ref[...].astype(F32) + other_ref[...].astype(F32)) + vec_ref[0:1, :]
        )
        middle_ref[...] = middle
        xhat, unused = norm_rows(middle)
        normed = (xhat * vec_ref[1:2, :] + vec_ref[2:3, :]).astype(B16)

        @pl.when(step == 0)
        def _():
            w_up.wait(*up_refs)

        total = None
        for first in range(0, hidden, PIECE):
            piece = slice(first, first + PIECE)
            u = dot_nn(normed, up[:, piece]) + bias_ref[:, piece]
            square = u * u
            t = jnp.tanh(GELU_SCALE * u * (1.0 + GELU_CUBE * square))
            half_one = 0.5 + 0.5 * t
            active = (u * half_one).astype(B16)
            bend = (0.5 * GELU_SCALE) * u * (1.0 - t * t) * (1.0 + 3 * GELU_CUBE * square)
            slope_ref[:, piece] = (half_one + bend).astype(B16)
            if first == 0:

                @pl.when(step == 0)
                def _():
                    w_down.wait(*down_refs)

            product = dot_nt(active, down[:, piece])
            total = product if total is None else total + product
        part_ref[...] = total.astype(B16)

    return pl.pallas_call(
        body,
        grid_spec=pltpu.PrefetchScalarGridSpec(
            num_scalar_prefetch=1,
            grid=(row_count // BLOCK,),
            in_specs=[
                rows_spec(width),
                rows_spec(width),
                rows_spec(width),
                whole_spec(vectors.shape),
                whole_spec(bias_up.shape),
                *w_up.specs,
                *w_down.specs,
            ],
            out_specs=[rows_spec(width), rows_spec(width), rows_spec(hidden)],
            scratch_shapes=w_up.scratch + w_down.scratch,
        ),
        out_shape=[
            shape((row_count, width), B16),
            shape((row_count, width), F32),
            shape((row_count, hidden), B16),
        ],
        compiler_params=params(36),
        cost_estimate=cost(23 * row_count // 1024),
        name="mlp",
    )(me, base, own, other, vectors, bias_up, *w_up.operands, *w_down.operands)


def last_attention(base, own, other, vectors, bias_qkv, prefix, layout, picks, picks_column, me,
                   weight, plen):
    row_count, width = base.shape
    half = prefix.shape[2]
    scored = picks.shape[0]
    steps = row_count // BLOCK
    scale = HEAD_DIM ** (-0.5)

    stacks = len(weight.operands)

    def body(me_ref, layout_ref, picks_ref, base_ref, own_ref, other_ref, vec_ref, bias_ref,
             prefix_ref, column_ref, *refs):
        (stream_out, part_ref, k_out, v_out, q_out, mixed_out, lse_out, chosen_out,
         full, sems, stream_s, k_s, v_s) = refs[stacks:]
        step = pl.program_id(0)
        refs = (me_ref[0], refs[:stacks], full, sems)

        @pl.when(step == 0)
        def _():
            weight.start(*refs)
            weight.wait(*refs)

        stream = base_ref[...] + (
            (own_ref[...].astype(F32) + other_ref[...].astype(F32)) + vec_ref[0:1, :]
        )
        stream_out[...] = stream
        rows = pl.ds(pl.multiple_of(step * BLOCK, BLOCK), BLOCK)
        stream_s[rows, :] = stream
        xhat, unused = norm_rows(stream)
        normed = (xhat * vec_ref[1:2, :] + vec_ref[2:3, :]).astype(B16)
        keys_values = (
            dot_nn(normed, full[:, half : 3 * half]) + bias_ref[:, half : 3 * half]
        ).astype(B16)
        k_out[...] = keys_values[:, :half]
        v_out[...] = keys_values[:, half:]
        k_s[rows, :] = keys_values[:, :half]
        v_s[rows, :] = keys_values[:, half:]

        @pl.when(step == steps - 1)
        def _():
            def pick(index, carry):
                chosen_out[pl.ds(index, 1), :] = stream_s[pl.ds(picks_ref[index], 1), :]
                return carry

            lax.fori_loop(0, scored, pick, 0, unroll=8)
            for first in range(0, scored, BLOCK):
                block = pl.ds(first, BLOCK)
                chosen_hat, unused = norm_rows(chosen_out[block, :])
                chosen = (chosen_hat * vec_ref[1:2, :] + vec_ref[2:3, :]).astype(B16)
                query = (dot_nn(chosen, full[:, :half]) + bias_ref[:, :half]).astype(B16)
                q_out[block, :] = (query * scale).astype(B16)
                bias = key_bias(layout_ref, column_ref[block, :], row_count)
                attend_pairs(
                    q_out, k_s, v_s, prefix_ref, mixed_out, lse_out, block, row_count, bias, plen
                )
                part_ref[block, :] = dot_nt(mixed_out[block, :], full[:, 3 * half :]).astype(B16)

    return pl.pallas_call(
        body,
        grid_spec=pltpu.PrefetchScalarGridSpec(
            num_scalar_prefetch=3,
            grid=(steps,),
            in_specs=[
                rows_spec(width),
                rows_spec(width),
                rows_spec(width),
                whole_spec(vectors.shape),
                whole_spec(bias_qkv.shape),
                whole_spec(prefix.shape),
                whole_spec(picks_column.shape),
                *weight.specs,
            ],
            out_specs=[
                rows_spec(width),
                whole_spec((scored, width)),
                rows_spec(half),
                rows_spec(half),
                whole_spec((scored, half)),
                whole_spec((scored, half)),
                whole_spec((scored, LANES)),
                whole_spec((scored, width)),
            ],
            scratch_shapes=weight.scratch
            + [pltpu.VMEM((row_count, width), F32)]
            + [pltpu.VMEM((row_count, half), B16)] * 2,
        ),
        out_shape=[
            shape((row_count, width), F32),
            shape((scored, width), B16),
            shape((row_count, half), B16),
            shape((row_count, half), B16),
            shape((scored, half), B16),
            shape((scored, half), B16),
            shape((scored, LANES), F32),
            shape((scored, width), F32),
        ],
        compiler_params=params(36),
        cost_estimate=cost(22),
        name="last_attention",
    )(me, layout, picks, base, own, other, vectors, bias_qkv, prefix, picks_column, *weight.operands)


def split_lse(lse, rows):
    high = lse.astype(B16).astype(F32)
    middle = (lse - high).astype(B16).astype(F32)
    low = (lse - high) - middle
    lane = lax.broadcasted_iota(jnp.int32, (rows, LANES), 1)
    packed = jnp.where(lane == 0, high, jnp.where(lane == 1, middle, jnp.where(lane == 2, low, 0.0)))
    return packed.astype(B16)


VMEM = pl.BlockSpec(memory_space=pltpu.VMEM)


def vocabulary(stacks, table, entries):
    width = table.shape[1]
    padded = table.shape[0]
    half = padded // 2
    ends = [0]
    for stack in stacks:
        ends.append(ends[-1] + stack.shape[0])
    block = max(b for b in range(16, 400, 16) if ends[-1] % b == 0)

    def body(*refs):
        table_ref = refs[len(stacks)]
        outs = refs[len(stacks) + 1 : -2]
        rows_s, mean_s = refs[-2:]
        for ref, first, last in zip(refs, ends[:-1], ends[1:]):
            rows_s[first:last, :] = ref[...]

        def turn(index, carry):
            rows = pl.ds(pl.multiple_of(index * block, block), block)
            logits = dot_nt(rows_s[rows, :], table_ref[...])
            pieces = []
            for first in range(0, padded, LANES):
                piece = logits[:, first : first + LANES]
                if any(c % half >= entries for c in range(first, first + LANES)):
                    lane = lax.broadcasted_iota(jnp.int32, piece.shape, 1) + first
                    piece = jnp.where(lane % half < entries, piece, NEG_BIG)
                pieces.append(piece)
            logits = jnp.concatenate(pieces, 1)
            highest = jnp.max(logits, -1, keepdims=True)
            shares = jnp.exp(logits - highest)
            total = jnp.sum(shares, -1, keepdims=True)
            mean = dot_nn(shares.astype(B16), table_ref[...]) / total
            mean_s[rows, :width] = mean.astype(B16)
            mean_s[rows, width:] = split_lse(highest + jnp.log(total), block)
            return carry

        lax.fori_loop(0, ends[-1] // block, turn, 0)
        for out, first, last in zip(outs, ends[:-1], ends[1:]):
            out[...] = mean_s[first:last, :]

    return pl.pallas_call(
        body,
        in_specs=[VMEM] * (len(stacks) + 1),
        out_specs=[VMEM] * len(stacks),
        out_shape=[shape((stack.shape[0], width + LANES), B16) for stack in stacks],
        scratch_shapes=[
            pltpu.VMEM((ends[-1], width), B16),
            pltpu.VMEM((ends[-1], width + LANES), B16),
        ],
        compiler_params=params(32, False),
        cost_estimate=cost(10 * ends[-1] // 384),
        name="vocabulary",
    )(*stacks, table)


def joined_lse(block, width):
    return jnp.sum(block[:, width:].astype(F32)[:, 0:4], -1, keepdims=True)


def merge(firsts, seconds, last):
    wide = firsts[0].shape[1]
    width = wide - LANES
    count = len(firsts)
    pieces = 1 if last else 2
    begins = [0]
    for array in firsts:
        begins.append(begins[-1] + array.shape[0])

    def body(*refs):
        outs = refs[2 * count :]
        for part in range(count):
            first_ref, second_ref = refs[part], refs[count + part]
            rows = first_ref.shape[0] // pieces
            for piece in range(pieces):
                one = first_ref[piece * rows : (piece + 1) * rows, :]
                two = second_ref[piece * rows : (piece + 1) * rows, :]
                lse_one, lse_two = joined_lse(one, width), joined_lse(two, width)
                highest = jnp.maximum(lse_one, lse_two)
                scale_one, scale_two = jnp.exp(lse_one - highest), jnp.exp(lse_two - highest)
                total = scale_one + scale_two
                mean = one[:, :width].astype(F32) * (scale_one / total)
                mean = mean + two[:, :width].astype(F32) * (scale_two / total)
                if last:
                    out_ref = outs[0].at[begins[part] : begins[part + 1]]
                else:
                    out_ref = outs[piece * count + part]
                out_ref[:, :width] = mean.astype(B16)
                out_ref[:, width:] = split_lse(highest + jnp.log(total), rows)

    outs = pl.pallas_call(
        body,
        in_specs=[VMEM] * (2 * count),
        out_specs=[VMEM] * (1 if last else 2 * count),
        out_shape=[shape((begins[-1], wide), B16)]
        if last
        else [shape((a.shape[0] // 2, wide), B16) for a in firsts] * 2,
        compiler_params=params(20, False),
        cost_estimate=cost(3),
        name="merge",
    )(*firsts, *seconds)
    return (outs, None) if last else (outs[:count], outs[count:])


def head_rows_of(middle, own, other, vectors, core, cuts):
    scored, width = middle.shape
    core_rows = scored // 2
    sizes = [b - a for a, b in zip(cuts[:-1], cuts[1:])]

    def body(core_ref, middle_ref, own_ref, other_ref, vec_ref, rows_ref, in_ref, *parts):
        both = own_ref[...].astype(F32) + other_ref[...].astype(F32)
        rows = middle_ref[...] + (both + vec_ref[0:1, :])
        rows_ref[...] = rows
        xhat, unused = norm_rows(rows)
        normed = xhat * vec_ref[1:2, :] + vec_ref[2:3, :]
        in_ref[...] = normed.astype(B16)
        mine = jnp.where(core_ref[0] == 0, normed[:core_rows], normed[core_rows:]).astype(B16)
        for ref, first, last in zip(parts, cuts[:-1], cuts[1:]):
            ref[...] = mine[first:last]

    outs = pl.pallas_call(
        body,
        in_specs=[pl.BlockSpec(memory_space=pltpu.SMEM)] + [VMEM] * 4,
        out_specs=[VMEM] * (2 + len(sizes)),
        out_shape=[shape((scored, width), F32), shape((scored, width), B16)]
        + [shape((size, width), B16) for size in sizes],
        compiler_params=params(16, False),
        cost_estimate=cost(3),
        name="head_rows",
    )(core, middle, own, other, vectors)
    return outs[0], outs[1], outs[2:]


def head_back(own, other, head_rows, head_in, rows, skip, counted, final_norm, core, count_total):
    scored, width = head_rows.shape

    def body(core_ref, own_ref, other_ref, rows_ref, in_ref, target_ref, counted_ref, norm_ref,
             grad_ref, loss_ref):
        own_mean, other_mean = own_ref[...].astype(F32), other_ref[...].astype(F32)
        first = core_ref[0] == 0
        mean = jnp.concatenate(
            [jnp.where(first, own_mean, other_mean), jnp.where(first, other_mean, own_mean)], 0
        )
        lse = joined_lse(mean, width)
        target = target_ref[...]
        logit = jnp.sum(in_ref[...].astype(F32) * target, -1, keepdims=True)
        seen = counted_ref[...]
        loss_ref[...] = jnp.broadcast_to((lse - logit) * seen, (scored, LANES))
        d_head = (mean[:, :width] - target) * (seen / count_total)
        grad_ref[...] = norm_rows_back(d_head, rows_ref[...], norm_ref[0:1, :])

    return pl.pallas_call(
        body,
        grid_spec=pltpu.PrefetchScalarGridSpec(
            num_scalar_prefetch=1,
            grid=(1,),
            in_specs=[
                whole_spec(own.shape),
                whole_spec(other.shape),
                whole_spec(head_rows.shape),
                whole_spec(head_in.shape),
                pl.BlockSpec((scored, width), lambda i, *refs: (skip // scored, 0)),
                whole_spec(counted.shape),
                whole_spec(final_norm.shape),
            ],
            out_specs=[whole_spec((scored, width)), whole_spec((scored, LANES))],
        ),
        out_shape=[shape((scored, width), F32), shape((scored, LANES), F32)],
        compiler_params=params(24),
        cost_estimate=cost(4),
        name="head_back",
    )(core, own, other, head_rows, head_in, rows, counted, final_norm)


def mlp_back(gradient, slope, me, w_up, w_down, residual=None):
    row_count, width = gradient.shape
    hidden = slope.shape[1]
    extra = [] if residual is None else list(residual)
    ups, downs = len(w_up.operands), len(w_down.operands)

    def body(me_ref, *refs):
        grad_ref, slope_ref = refs[0], refs[1]
        extra_refs = refs[2 : 2 + len(extra)]
        refs = refs[2 + len(extra) :]
        part_ref, *rest = refs[ups + downs :]
        up, up_sems, down, down_sems = rest[-4:]
        step = pl.program_id(0)
        up_refs = (me_ref[0], refs[:ups], up, up_sems)
        down_refs = (me_ref[0], refs[ups : ups + downs], down, down_sems)

        @pl.when(step == 0)
        def _():
            w_down.start(*down_refs)
            w_up.start(*up_refs)

        grad = grad_ref[...]
        if extra:
            stream_ref, gain_ref, own_ref, other_ref = extra_refs
            incoming = own_ref[...].astype(F32) + other_ref[...].astype(F32)
            grad = grad + norm_rows_back(incoming, stream_ref[...], gain_ref[...])
            rest[0][...] = grad

        @pl.when(step == 0)
        def _():
            w_down.wait(*down_refs)

        low = grad.astype(B16)
        total = None
        for first in range(0, hidden, PIECE):
            piece = slice(first, first + PIECE)
            d_active = dot_nn(low, down[:, piece])
            d_upward = (d_active * slope_ref[:, piece].astype(F32)).astype(B16)
            if first == 0:

                @pl.when(step == 0)
                def _():
                    w_up.wait(*up_refs)

            product = dot_nt(d_upward, up[:, piece])
            total = product if total is None else total + product
        part_ref[...] = total.astype(B16)

    extra_specs = (
        [rows_spec(width), whole_spec(extra[1].shape), rows_spec(width), rows_spec(width)]
        if extra
        else []
    )
    return pl.pallas_call(
        body,
        grid_spec=pltpu.PrefetchScalarGridSpec(
            num_scalar_prefetch=1,
            grid=(row_count // BLOCK,),
            in_specs=[rows_spec(width), rows_spec(hidden)] + extra_specs + w_up.specs + w_down.specs,
            out_specs=[rows_spec(width)] * (2 if extra else 1),
            scratch_shapes=w_up.scratch + w_down.scratch,
        ),
        out_shape=[shape((row_count, width), B16)]
        + ([shape((row_count, width), F32)] if extra else []),
        compiler_params=params(36),
        cost_estimate=cost(20 * row_count // 1024),
        name="mlp_back",
    )(me, gradient, slope, *extra, *w_up.operands, *w_down.operands)


def last_attention_back(gradient, own, other, middle, gain, q, k, v, lse, prefix, layout, picks,
                        me, weight, plen):
    scored, width = gradient.shape
    row_count, half = k.shape
    prefix_rows = prefix.shape[1]
    scale = HEAD_DIM ** (-0.5)

    stacks = len(weight.operands)

    def body(me_ref, layout_ref, picks_ref, grad_ref, own_ref, other_ref, middle_ref, gain_ref,
             q_ref, k_ref, v_ref, lse_ref, prefix_ref, picks_row_ref, *refs):
        (part_ref, spread_ref, dprefix_ref, full, sems,
         dmix_s, lse_s, dq_s, dkv_s, sum_s, rows_s) = refs[stacks:]
        refs = (me_ref[0], refs[:stacks], full, sems)
        weight.start(*refs)
        incoming = own_ref[...].astype(F32) + other_ref[...].astype(F32)
        grad_mid = grad_ref[...] + norm_rows_back(incoming, middle_ref[...], gain_ref[...])
        rows_s[...] = grad_mid
        spread_ref[...] = jnp.zeros((row_count, width), F32)

        def put(index, carry):
            spread_ref[pl.ds(picks_ref[index], 1), :] = rows_s[pl.ds(index, 1), :]
            return carry

        lax.fori_loop(0, scored, put, 0, unroll=8)
        weight.wait(*refs)
        dmix_s[...] = dot_nn(grad_mid.astype(B16), full[:, 3 * half :]).astype(B16)
        bias = jnp.transpose(key_bias(layout_ref, jnp.transpose(picks_row_ref[...]), row_count))
        bias_prefix = jnp.where(
            lax.broadcasted_iota(jnp.int32, (prefix_rows, scored), 0) < plen, 0.0, NEG_BIG
        )
        lse_s[...] = jnp.transpose(lse_ref[...])

        def pair(index, carry):
            columns = pl.ds(pl.multiple_of(index * LANES, LANES), LANES)
            query, key, value = q_ref[:, columns], k_ref[:, columns], v_ref[:, columns]
            d_mixed = dmix_s[:, columns]
            key_p, value_p = prefix_ref[0, :, columns], prefix_ref[1, :, columns]
            found = [[], [], [], [], []]
            for side in range(2):
                cut = slice(side * HEAD_DIM, (side + 1) * HEAD_DIM)
                place = pl.multiple_of(prefix_rows * (2 * index + side), prefix_rows)
                log_total = lse_s[pl.ds(place, 1), :]
                qh, dh, kh, kp = query[:, cut], d_mixed[:, cut], key[:, cut], key_p[:, cut]
                shares = jnp.exp(dot_nt(kh, qh) + bias - log_total)
                shares_p = jnp.exp(dot_nt(kp, qh) + bias_prefix - log_total)
                d_shares = dot_nt(value[:, cut], dh).astype(B16).astype(F32)
                d_shares_p = dot_nt(value_p[:, cut], dh).astype(B16).astype(F32)
                inner = jnp.sum(shares * d_shares, 0, keepdims=True) + jnp.sum(
                    shares_p * d_shares_p, 0, keepdims=True
                )
                d_scores = (shares * (d_shares - inner)).astype(B16)
                d_scores_p = (shares_p * (d_shares_p - inner)).astype(B16)
                found[0].append((dot_tn(kh, d_scores) + dot_tn(kp, d_scores_p)) * scale)
                found[1].append(dot_nn(d_scores, qh))
                found[2].append(dot_nn(shares.astype(B16), dh))
                found[3].append(dot_nn(d_scores_p, qh))
                found[4].append(dot_nn(shares_p.astype(B16), dh))
            dq_s[columns, :] = jnp.concatenate(found[0], 0)
            joined = [jnp.concatenate(f, 1) for f in found[1:]]
            dkv_s[:, columns] = joined[0].astype(B16)
            dkv_s[:, pl.ds(pl.multiple_of(half + index * LANES, LANES), LANES)] = joined[1].astype(B16)
            dprefix_ref[0, :, columns] = joined[2]
            dprefix_ref[1, :, columns] = joined[3]
            return carry

        lax.fori_loop(0, half // LANES, pair, 0)
        sum_s[...] = dot_nt(dkv_s[...], full[:, half : 3 * half])
        rows_s[...] = dot_nt(jnp.transpose(dq_s[...]).astype(B16), full[:, :half])

        def add(index, carry):
            place = pl.ds(picks_ref[index], 1)
            sum_s[place, :] = sum_s[place, :] + rows_s[pl.ds(index, 1), :]
            return carry

        lax.fori_loop(0, scored, add, 0, unroll=8)
        part_ref[...] = sum_s[...].astype(B16)

    inputs = [gradient, own, other, middle, gain, q, k, v, lse, prefix, picks.reshape(1, scored)]
    return pl.pallas_call(
        body,
        grid_spec=pltpu.PrefetchScalarGridSpec(
            num_scalar_prefetch=3,
            grid=(1,),
            in_specs=[whole_spec(a.shape) for a in inputs] + weight.specs,
            out_specs=[
                whole_spec((row_count, width)),
                whole_spec((row_count, width)),
                whole_spec(prefix.shape),
            ],
            scratch_shapes=weight.scratch
            + [
                pltpu.VMEM((scored, half), B16),
                pltpu.VMEM((LANES, scored), F32),
                pltpu.VMEM((half, scored), F32),
                pltpu.VMEM((row_count, 2 * half), B16),
                pltpu.VMEM((row_count, width), F32),
                pltpu.VMEM((scored, width), F32),
            ],
        ),
        out_shape=[
            shape((row_count, width), B16),
            shape((row_count, width), F32),
            shape(prefix.shape, F32),
        ],
        compiler_params=params(48),
        cost_estimate=cost(24),
        name="last_attention_back",
    )(me, layout, picks, *inputs, *weight.operands)


def first_prefix_back(gradient, own, other, middle, gain, q, mixed, lse, prefix, me, weight, plen):
    row_count, width = gradient.shape
    half = q.shape[1]
    prefix_rows = prefix.shape[1]
    lanes = half // HEAD_DIM * prefix_rows
    stacks = len(weight.operands)

    def own_head(dims, lane_axis):
        lane = lax.broadcasted_iota(jnp.int32, dims, lane_axis)
        column = lax.broadcasted_iota(jnp.int32, dims, 1 - lane_axis)
        return lane // prefix_rows == column // HEAD_DIM

    def body(me_ref, grad_ref, own_ref, other_ref, middle_ref, gain_ref, q_ref, mixed_ref,
             lse_ref, prefix_ref, *refs):
        dprefix_ref, full, sems, spread_s, sum_s = refs[stacks:]
        step = pl.program_id(0)
        refs = (me_ref[0], refs[:stacks], full, sems)

        @pl.when(step == 0)
        def _():
            weight.start(*refs)
            sum_s[...] = jnp.zeros(sum_s.shape, F32)
            for c in range(2):
                tiled = jnp.concatenate([prefix_ref[c]] * (lanes // prefix_rows), 0)
                spread_s[c] = jnp.where(
                    own_head((lanes, half), 0), tiled.astype(F32), 0.0
                ).astype(B16)
            spread_s[2] = jnp.where(own_head((lanes, half), 0), 1.0, 0.0).astype(B16)

        incoming = own_ref[...].astype(F32) + other_ref[...].astype(F32)
        grad_mid = grad_ref[...] + norm_rows_back(incoming, middle_ref[...], gain_ref[...])

        @pl.when(step == 0)
        def _():
            weight.wait(*refs)

        d_mixed = dot_nn(grad_mid.astype(B16), full[...]).astype(B16)
        product = d_mixed.astype(F32) * mixed_ref[...].astype(F32)
        high = product.astype(B16)
        low = (product - high.astype(F32)).astype(B16)
        inner = dot_nt(high, spread_s[2]) + dot_nt(low, spread_s[2])
        lane = lax.broadcasted_iota(jnp.int32, (BLOCK, lanes), 1)
        shares = jnp.exp(dot_nt(q_ref[...], spread_s[0]) - lse_ref[:, :lanes])
        shares = jnp.where(lane % prefix_rows < plen, shares, 0.0)
        d_shares = dot_nt(d_mixed, spread_s[1]).astype(B16).astype(F32)
        d_scores = (shares * (d_shares - inner)).astype(B16)
        sum_s[0] += dot_tn(d_scores, q_ref[...])
        sum_s[1] += dot_tn(shares.astype(B16), d_mixed)

        @pl.when(step == row_count // BLOCK - 1)
        def _():
            for c in range(2):
                held = jnp.where(own_head((lanes, half), 0), sum_s[c], 0.0)
                total = held[:prefix_rows]
                for first in range(prefix_rows, lanes, prefix_rows):
                    total = total + held[first : first + prefix_rows]
                dprefix_ref[c] = total

    return pl.pallas_call(
        body,
        grid_spec=pltpu.PrefetchScalarGridSpec(
            num_scalar_prefetch=1,
            grid=(row_count // BLOCK,),
            in_specs=[
                rows_spec(width),
                rows_spec(width),
                rows_spec(width),
                rows_spec(width),
                whole_spec(gain.shape),
                rows_spec(half),
                rows_spec(half),
                rows_spec(LANES),
                whole_spec(prefix.shape),
                *weight.specs,
            ],
            out_specs=whole_spec(prefix.shape),
            scratch_shapes=weight.scratch
            + [pltpu.VMEM((3, lanes, half), B16), pltpu.VMEM((2, lanes, half), F32)],
        ),
        out_shape=shape(prefix.shape, F32),
        compiler_params=params(24),
        cost_estimate=cost(11),
        name="first_prefix_back",
    )(me, gradient, own, other, middle, gain, q, mixed, lse, prefix, *weight.operands)


class TableRows:
    def __init__(self, ids, table):
        count = ids.shape[0]
        shard_rows = table.shape[0]
        ta_size = lax.axis_size("ta")
        shard = ids // shard_rows
        self.table = table
        self.inside = ids % shard_rows
        self.owner = shard // ta_size
        order = jnp.arange(count, dtype=jnp.int32)
        same = ids[:, None] == ids[None, :]
        first = jnp.min(jnp.where(same, order[None], count), 1)
        is_first = first == order
        earlier = is_first[None] & (shard[None] == shard[:, None]) & (order[None] < first[:, None])
        self.rank = jnp.sum(earlier.astype(jnp.int32), 1)
        self.mine = shard % ta_size == lax.axis_index("ta")
        self.need = jnp.max(jnp.where(self.mine, self.rank, 0)) // SLOT_ROWS + 1
        self.per_core = lax.axis_size("dev") * SLOT_ROWS

    def slot(self, turn):
        rank = self.rank - turn * SLOT_ROWS
        used = (rank >= 0) & (rank < SLOT_ROWS)
        slot = self.owner * SLOT_ROWS + rank + jnp.where(self.mine, 0, self.per_core)
        return jnp.where(used, slot, -1)

    def ask(self, turn):
        slots = jnp.arange(self.per_core, dtype=jnp.int32)
        found = self.slot(turn)[None] == slots[:, None]
        asked = jnp.max(jnp.where(found, self.inside[None], 0), 1).reshape(-1, SLOT_ROWS)
        header = jnp.broadcast_to(self.need, (asked.shape[0], 1))
        return lax.all_to_all(jnp.concatenate([asked, header], 1), "dev", 0, 0)

    def answer(self, wanted):
        numbers = jnp.arange(self.table.shape[0], dtype=jnp.int32)
        pick = (wanted[:, :SLOT_ROWS].reshape(-1, 1) == numbers[None]).astype(B16)
        sent = jnp.dot(pick, self.table, preferred_element_type=F32).astype(B16)
        return sent.reshape(-1, SLOT_ROWS, self.table.shape[1])

    def fetch(self, sent):
        got = lax.all_to_all(sent, "dev", 0, 0)
        return got.reshape(self.per_core, self.table.shape[1])

    def place(self, turn, got):
        slots = jnp.arange(2 * self.per_core, dtype=jnp.int32)
        spread = (self.slot(turn)[:, None] == slots[None]).astype(B16)
        both = jnp.concatenate([got, partner(got)], 0)
        return jnp.dot(spread, both, preferred_element_type=F32)

    def finish(self, base, wanted, got):
        most = jnp.max(wanted[:, SLOT_ROWS])
        most = jnp.maximum(most, partner(most.reshape(1, 1))[0, 0])

        def again(state):
            return state[0] < most

        def turn(state):
            got = self.fetch(self.answer(self.ask(state[0])))
            return (state[0] + 1, state[1] + self.place(state[0], got))

        return lax.while_loop(again, turn, (jnp.int32(1), base + self.place(0, got)))[1]


def adamw_update(weight, moment, square, gradient, corr_one, corr_two):
    moment = BETA_ONE * moment + (1.0 - BETA_ONE) * gradient
    square = BETA_TWO * square + (1.0 - BETA_TWO) * gradient * gradient
    weight = weight - LEARN_RATE * (
        moment / corr_one / (jnp.sqrt(square / corr_two) + ADAM_EPS) + DECAY_RATE * weight
    )
    return (weight, moment, square)


def local(
    token_ids,
    bucket,
    seq_lengths,
    loss_pos,
    targets,
    wte,
    wpe,
    w_qkv,
    w_out,
    w_fc,
    w_proj,
    frozen_vec,
    fc_bias,
    final_norm,
    prefix_table,
    inner_weight,
    inner_bias,
    outer_weight,
    outer_bias,
    moment_prefix,
    square_prefix,
    moment_inner,
    square_inner,
    moment_inner_bias,
    square_inner_bias,
    moment_outer,
    square_outer,
    moment_outer_bias,
    square_outer_bias,
):
    row_count = token_ids.shape[0]
    scored = loss_pos.shape[0]
    width = wte.shape[1]
    half = w_qkv.shape[3]
    size = lax.axis_size("dev")
    own_index = lax.axis_index("ta")
    plen = prefix_table.shape[0]
    prefix_rows = 16
    me = lax.axis_index("dev").astype(jnp.int32).reshape(1)
    orders = (bit_orders(size, 3), bit_orders(size, 4))
    stages = len(orders[0][0])
    bucket_width = bucket[0]
    shift = jnp.where(bucket_width == 256, 8, 10).astype(jnp.int32)
    layout = jnp.concatenate([shift.reshape(1), bucket_width.reshape(1), seq_lengths[0]])

    rounds = Rounds()
    ff = w_fc.shape[2]
    totals = (4 * half, 2 * ff)
    cuts = [[cuts_of(total, LANES, len(order)) for total in totals] for order in orders]

    def add_layer(layer_id, qkv, out, fc, proj):
        sides = (
            jnp.concatenate([qkv[c] for c in range(3)] + [out.T], 1),
            jnp.concatenate([fc, proj.T], 1),
        )
        parts = [
            [
                rows[:, c[p] : c[p + 1]]
                for rows, c in zip(sides, cuts[layer_id])
            ]
            for p in range(len(orders[layer_id]))
        ]
        rounds.add(
            layer_id,
            orders[layer_id],
            [jnp.concatenate(part, 1) for part in parts],
            [part[0].shape[1] for part in parts],
        )

    def weight(layer_id, side, first, last):
        segments = [
            (rounds.held[layer_id, p, side], order, cuts[layer_id][side][p])
            for p, order in enumerate(orders[layer_id])
        ]
        return Gathered(segments, first, last)

    def attention_weight(layer_id, first=0):
        return weight(layer_id, 0, first * half, 4 * half)

    def mlp_weights(layer_id):
        return weight(layer_id, 1, 0, ff), weight(layer_id, 1, ff, 2 * ff)

    def head_bias(layer_id):
        part = lax.dynamic_slice_in_dim(frozen_vec[layer_id, 4:7], own_index * half, half, 1)
        return part.reshape(1, 3 * half)

    add_layer(0, w_qkv[0], w_out[0], w_fc[0], w_proj[0])
    ids, prefix_in = rounds.step(
        0,
        0,
        through=(
            (token_ids, targets),
            (prefix_table, inner_weight, inner_bias, outer_weight),
        ),
    )
    lookup = TableRows(jnp.concatenate(ids), wte)
    wanted = lookup.ask(0)
    hidden = jnp.tanh(jnp.dot(prefix_in[0], prefix_in[1], precision=HIGHEST) + prefix_in[2])
    sums = jnp.einsum("pr,rlcd->lcpd", hidden, prefix_in[3], precision=HIGHEST)
    for stage in range(stages - 2):
        sums = sums + flip(sums, 1 << stage)

    wanted, sums = rounds.step(0, 1, through=(wanted, sums))
    sent = lookup.answer(wanted)
    sums = sums + flip(sums, 1 << (stages - 2))
    for stage in range(2, stages - 2):
        rounds.step(0, stage)

    sent, wanted, sums, last_layer = rounds.step(
        0,
        stages - 2,
        through=(sent, wanted, sums, (w_qkv[1], w_out[1], w_fc[1], w_proj[1])),
    )
    got = lookup.fetch(sent)
    add_layer(1, *last_layer)
    sums = sums + flip(sums, 1 << (stages - 1))
    prefix_kv = (sums + outer_bias[:, :, None, :]).astype(B16)
    prefix_kv = jnp.pad(prefix_kv, ((0, 0), (0, 0), (0, prefix_rows - plen), (0, 0)))

    got, wanted, places, prefix_kv, next_rows = rounds.step(
        0,
        stages - 1,
        0,
        through=(got, wanted, wpe, prefix_kv, [rounds.held[1, p][0] for p in range(len(orders[1]))]),
    )
    for part, array in enumerate(next_rows):
        rounds.held[1, part] = [array]
    repeat = row_count // 256
    places = jnp.where(bucket_width == 256, jnp.tile(places[:256], (repeat, 1)), places[:row_count])
    places = jnp.concatenate([places, jnp.zeros((scored, width), places.dtype)], 0)
    stream = lookup.finish(places.astype(F32), wanted, got)

    stream = rounds.step(0, stages - 1, 1, through=stream)
    part, q0, mixed0, lse0 = first_attention(
        stream,
        row_count,
        frozen_vec[0, 0:2],
        head_bias(0),
        prefix_kv[0],
        layout,
        me,
        attention_weight(0),
        plen,
    )

    part = rounds.step(1, 0, through=part)
    other = partner(part)

    part, other = rounds.step(1, 1, through=(part, other))
    vec = frozen_vec[0]
    part_two, middle0, slope0 = mlp(
        stream,
        part,
        other,
        jnp.stack([vec[7], vec[2], vec[3]]),
        fc_bias[0:1],
        me,
        *mlp_weights(0),
    )

    part_two, table = rounds.step(1, 2, through=(part_two, wte))
    other = partner(part_two)
    entries = wte.shape[0]
    table_half = -(-entries // 64) * 64
    table = jnp.pad(table, ((0, table_half - entries), (0, 0)))
    for stage in range(3, stages - 1):
        rounds.step(1, stage)

    table, part_two, other = rounds.step(1, stages - 1, 0, through=(table, part_two, other))
    table = jnp.concatenate([table, partner(table)], 0)

    part_two, other, table = rounds.step(1, stages - 1, 1, through=(part_two, other, table))

    vec_last = frozen_vec[1]
    picks_column = loss_pos.reshape(scored, 1)
    stream1, part, k1, v1, q1, mixed1, lse1, chosen = last_attention(
        middle0,
        part_two,
        other,
        jnp.stack([vec[8], vec_last[0], vec_last[1]]),
        head_bias(1),
        prefix_kv[1],
        layout,
        loss_pos,
        picks_column,
        me,
        attention_weight(1),
        plen,
    )
    part_two, middle1, slope1 = mlp(
        chosen,
        part,
        partner(part),
        jnp.stack([vec_last[7], vec_last[2], vec_last[3]]),
        fc_bias[1:2],
        me,
        *mlp_weights(1),
    )
    core = own_index.astype(jnp.int32).reshape(1)
    cuts_head = (0, 48, 96, scored // 2)
    head_rows, head_in, mine = head_rows_of(
        middle1,
        part_two,
        partner(part_two),
        jnp.stack([vec_last[8], final_norm[0], final_norm[1]]),
        core,
        cuts_head,
    )

    head_order = bit_orders(size, 3)
    head = Rounds()
    head.add(0, head_order, mine)
    for stage in range(stages):
        head.step(0, stage)
    near, far = [
        [head.held[0, p][side].reshape(-1, width) for p in range(len(head_order))]
        for side in range(2)
    ]
    keep = vocabulary(near[:1], table, entries)
    far, keep, near = lax.optimization_barrier((far, keep, near))
    send = vocabulary(far, table, entries)
    keep = list(keep) + list(vocabulary(near[1:], table, entries))
    for stage in reversed(range(stages)):
        got = [flip(array, head_order[p][stage]) for p, array in enumerate(send)]
        keep, send = merge(keep, got, stage == 0)
    (own_means,) = keep
    other_means = partner(own_means)
    place = loss_pos % bucket_width
    slot = loss_pos // bucket_width
    lengths = jnp.sum(
        jnp.where(
            slot[:, None] == jnp.arange(seq_lengths.shape[1], dtype=jnp.int32)[None],
            seq_lengths[0][None],
            0,
        ),
        1,
    )
    counted = (place < lengths).astype(F32).reshape(scored, 1)
    count_total = float(scored * size)
    grad_rows, loss_terms = head_back(
        own_means,
        other_means,
        head_rows,
        head_in,
        stream,
        row_count,
        counted,
        final_norm,
        core,
        count_total,
    )
    loss_part = jnp.sum(loss_terms[:, 0])

    (part,) = mlp_back(grad_rows, slope1, me, *mlp_weights(1))
    part, spread_grad, d_prefix1 = last_attention_back(
        grad_rows,
        part,
        partner(part),
        middle1,
        vec_last[2:3],
        q1,
        k1,
        v1,
        lse1,
        prefix_kv[1],
        layout,
        loss_pos,
        me,
        attention_weight(1),
        plen,
    )
    part, grad_stream = mlp_back(
        spread_grad,
        slope0,
        me,
        *mlp_weights(0),
        (stream1, vec_last[0:1], part, partner(part)),
    )
    d_prefix0 = first_prefix_back(
        grad_stream,
        part,
        partner(part),
        middle0,
        vec[2:3],
        q0,
        mixed0,
        lse0,
        prefix_kv[0],
        me,
        attention_weight(0, 3),
        plen,
    )
    d_prefix = sum_over_dev(jnp.stack([d_prefix0, d_prefix1])[:, :, :plen])

    d_outer = jnp.einsum("pr,lcpd->rlcd", hidden, d_prefix, precision=HIGHEST)
    d_outer_bias = jnp.sum(d_prefix, 2)
    hidden_part = jnp.einsum("lcpd,rlcd->pr", d_prefix, outer_weight, precision=HIGHEST)
    outer_square = jnp.sum(d_outer * d_outer) + jnp.sum(d_outer_bias * d_outer_bias) / size
    over_ta = jnp.concatenate(
        [hidden_part, jnp.broadcast_to(outer_square, (1, hidden_part.shape[1]))], 0
    )
    over_ta = over_ta + partner(over_ta)
    d_hidden = over_ta[:plen]
    d_pre = d_hidden * (1.0 - hidden * hidden)
    d_inner = jnp.dot(prefix_table.T, d_pre, precision=HIGHEST)
    d_inner_bias = jnp.sum(d_pre, 0)
    table_part = jnp.dot(d_pre, inner_weight.T, precision=HIGHEST)
    squares = over_ta[plen, 0] + jnp.sum(d_inner * d_inner) + jnp.sum(d_inner_bias * d_inner_bias)
    lane = jnp.arange(table_part.shape[1], dtype=jnp.int32)
    last_row = jnp.where(lane == 0, squares, jnp.where(lane == 1, loss_part, 0.0))
    totals = sum_over_dev(jnp.concatenate([table_part, last_row[None]], 0))
    d_table = totals[:plen]
    square_sum = totals[plen, 0]
    loss_value = totals[plen, 1] / count_total
    grad_total = jnp.sqrt(square_sum + jnp.sum(d_table * d_table))
    factor = jnp.minimum(1.0, CLIP_NORM / (grad_total + 1e-06))
    corr_one = 1.0 - BETA_ONE**adam_steps
    corr_two = 1.0 - BETA_TWO**adam_steps
    prefix_out = adamw_update(
        prefix_table, moment_prefix, square_prefix, factor * d_table, corr_one, corr_two
    )
    inner_out = adamw_update(
        inner_weight, moment_inner, square_inner, factor * d_inner, corr_one, corr_two
    )
    ibias_out = adamw_update(
        inner_bias, moment_inner_bias, square_inner_bias, factor * d_inner_bias, corr_one, corr_two
    )
    d_outer = with_layout_constraint(d_outer, Layout(major_to_minor=(0, 1, 2, 3)))
    outer_out = adamw_update(
        outer_weight, moment_outer, square_outer, factor * d_outer, corr_one, corr_two
    )
    obias_out = adamw_update(
        outer_bias, moment_outer_bias, square_outer_bias, factor * d_outer_bias, corr_one, corr_two
    )
    return (
        loss_value.reshape(1),
        grad_total.reshape(1),
        prefix_out[0],
        prefix_out[1],
        prefix_out[2],
        inner_out[0],
        inner_out[1],
        inner_out[2],
        ibias_out[0],
        ibias_out[1],
        ibias_out[2],
        outer_out[0],
        outer_out[1],
        outer_out[2],
        obias_out[0],
        obias_out[1],
        obias_out[2],
        prefix_out[0].astype(B16),
        inner_out[0].astype(B16),
        ibias_out[0].astype(B16),
        outer_out[0].astype(B16),
        obias_out[0].astype(B16),
    )


def solution(mesh):
    in_specs = (
        P("dev"),
        P("dev"),
        P("dev", None),
        P("dev"),
        P("dev"),
        P(("dev", "ta"), None),
        P(),
        P(None, None, "dev", "ta"),
        P(None, "ta", "dev"),
        P(None, "dev", "ta"),
        P(None, "ta", "dev"),
        P(),
        P(None, "ta"),
        P(),
        P(),
        P(None, "dev"),
        P("dev"),
        P("dev", None, None, "ta"),
        P(None, None, "ta"),
        P(),
        P(),
        P(None, "dev"),
        P(None, "dev"),
        P("dev"),
        P("dev"),
        P("dev", None, None, "ta"),
        P("dev", None, None, "ta"),
        P(None, None, "ta"),
        P(None, None, "ta"),
    )
    out_specs = (
        P(),
        P(),
        P(),
        P(),
        P(),
        P(None, "dev"),
        P(None, "dev"),
        P(None, "dev"),
        P("dev"),
        P("dev"),
        P("dev"),
        P("dev", None, None, "ta"),
        P("dev", None, None, "ta"),
        P("dev", None, None, "ta"),
        P(None, None, "ta"),
        P(None, None, "ta"),
        P(None, None, "ta"),
        P(),
        P(None, "dev"),
        P("dev"),
        P("dev", None, None, "ta"),
        P(None, None, "ta"),
    )
    return jax.shard_map(local, mesh=mesh, in_specs=in_specs, out_specs=out_specs, check_vma=False)
```
